256 devices in a mesh: dp: 16 (over x, y), tensor: 16 (over z, core).
Axes of the slice: x: 4, y: 4, z: 8, core: 2. Of those that a mesh axis runs over, the one named last changes fastest.
Arguments:
- tokens: bfloat16 [4096, 2048], P(('dp', 'tensor')), may hold values from -6 to 6
- attn_gain: bfloat16 [2048], replicated, may hold values from 0.099609375 to 1.8984375
- mlp_gain: bfloat16 [2048], replicated, may hold values from 0.099609375 to 1.8984375
- project_in: bfloat16 [3, 2048, 2048], P(None, None, 'tensor'), may hold values from -6 to 6
- project_out: bfloat16 [2048, 2048], P('tensor'), may hold values from -0.125 to 0.125
- gate_up: bfloat16 [2, 2048, 8192], P(None, None, 'tensor'), may hold values from -0.125 to 0.125
- project_down: bfloat16 [8192, 2048], P('tensor'), may hold values from -0.0625 to 0.0625
- kv_cache: bfloat16 [2, 65536, 2048], P(None, 'dp', 'tensor'), may hold values from -10 to 10
- lengths: int32 [4096], replicated, may hold values from 1 to 1024, as said below
- owners: int32 [4096], replicated, may hold values from 0 to 15, as said below
- cache_start: int32 [4096], replicated, may hold values from 0 to 4094, as said below
Outputs:
- hidden_states: bfloat16 [4096, 2048], P(('dp', 'tensor'))
- log_sum_exp: float32 [4096, 32], P('dp', 'tensor')
- kv_updated: bfloat16 [2, 65536, 2048], P(None, 'dp', 'tensor')
The draws below stay inside these ranges and needn't reach their ends.
Inputs may be any that keep to these rules, and one draw needn't show every extreme that they name: `lengths`: the largest length is exactly 1024 in every draw. `owners`: in each aligned block of 256 requests (those of one dp index) exactly 128 requests name another owner than the block's index and the rest name the block's index; no other owner is named by more than 9 requests of one block, and in every block one owner is named by exactly 9. The requests of one owner occupy disjoint ranges of positions from cache_start to cache_start + length, the last of these (the position for the new token) included, all within that owner's 4096 positions.
All inputs are finite; a program needn't handle non-finite values.
Results may differ from the reference program's by a relative error of at most 0.008.
Values may be sent and summed in bfloat16 or wider, within the bound.
A program may use at most 64 MiB of HBM per device.

```python
import jax
import jax.numpy as jnp
from jax import lax

D = 2048
FF = 8192
HEADS = 32
REQ_DEV = 256
MAXLEN = 1024
HD = 64
REQUESTS = 4096
CAP = 9
ROWS = 4096
CACHE_ROWS = 65536


def layout_ints(key):
    group_count = REQUESTS // REQ_DEV
    remote_count = REQ_DEV // 2
    key_list = jax.random.split(jax.random.fold_in(key, 17), 6)
    shuffled = jax.vmap(lambda sub_key: jax.random.permutation(sub_key, REQ_DEV))(jax.random.split(key_list[0], group_count))
    ranking = jnp.argsort(shuffled, axis=1).astype(jnp.int32)
    hot_offset = jax.random.randint(key_list[1], (group_count, 1), 0, group_count - 1)
    shift_by = jax.random.randint(key_list[2], (group_count, 1), 0, group_count - 2)
    rest_offset = (hot_offset + 1 + (ranking - CAP + shift_by) % (group_count - 2)) % (group_count - 1)
    offsets = jnp.where(ranking < CAP, hot_offset, rest_offset)
    source = jnp.arange(group_count, dtype=jnp.int32)[:, None]
    owners = jnp.where(ranking < remote_count, (source + 1 + offsets) % group_count, source)
    owners = owners.reshape(REQUESTS).astype(jnp.int32)
    onehot = (owners[:, None] == jnp.arange(group_count, dtype=jnp.int32)[None, :]).astype(jnp.int32)
    hosted = jnp.sum(onehot, axis=0)
    before = jnp.cumsum(onehot, axis=0) - onehot
    host_rank = jnp.sum(before * onehot, axis=1)
    weights = jax.random.randint(key_list[3], (REQUESTS,), 1, 9)
    zone_pick = jax.random.randint(key_list[4], (), 0, group_count)
    shares = jax.random.randint(key_list[5], (group_count,), 1, 5)
    shares = jnp.where(jnp.arange(group_count) == zone_pick, 4, shares)
    weights = jnp.where((owners == zone_pick) & (host_rank == 0), 100000, weights)
    total_weight = jnp.sum(onehot * weights[:, None], axis=0)
    budget = (ROWS - 2 * hosted) * shares // 4
    lengths = jnp.minimum(MAXLEN, 1 + weights * jnp.take(budget, owners) // jnp.take(total_weight, owners))
    in_zone = owners == zone_pick
    last_in_zone = in_zone & (host_rank == jnp.take(hosted, owners) - 1)
    lengths = jnp.where(last_in_zone, 1, lengths)
    needed = onehot * (lengths + 1)[:, None]
    cache_start = jnp.sum((jnp.cumsum(needed, axis=0) - needed) * onehot, axis=1)
    used = jnp.sum(needed, axis=0)
    cache_start = jnp.where(in_zone, cache_start + ROWS - jnp.take(used, owners), cache_start)
    return (owners.astype(jnp.int32), lengths.astype(jnp.int32), cache_start.astype(jnp.int32))


def draw_lengths(key, part):
    return layout_ints(key)[1]


def draw_owners(key, part):
    return layout_ints(key)[0]


def draw_cache_start(key, part):
    return layout_ints(key)[2]


def draw_project_in(key, part):
    base = jax.random.normal(jax.random.fold_in(key, 3), (3, D, D), jnp.float32)
    base = jnp.clip(base, -6.0, 6.0) * D ** (-0.5)
    return base.astype(jnp.bfloat16)


def draw_kv_cache(key, part):
    base = jax.random.normal(jax.random.fold_in(key, 5), (2, CACHE_ROWS, D), jnp.float32)
    base = jnp.clip(base, -6.0, 6.0)
    return base.astype(jnp.bfloat16)


def steps_of(key, shape, cuts, low, largest):
    loudness, own = 1.0, jax.random.fold_in(key, 6)
    for dim, shards_of in cuts:
        heights = jnp.exp(jax.random.uniform(jax.random.fold_in(own, dim), (shards_of,), jnp.float32, low / len(cuts), largest / len(cuts)))
        loudness = loudness * jnp.repeat(heights, shape[dim] // shards_of).reshape([-1 if axis == dim else 1 for axis in range(len(shape))])
    return loudness


def normal_values(key, dims, scale, reach, cuts=(), held_as=jnp.bfloat16):
    entries = jax.random.normal(key, dims, jnp.float32) * scale
    if len(cuts) > 0:
        entries = steps_of(key, dims, cuts, -0.22, 0.18) * entries
    return jnp.clip(entries, min=-reach, max=reach).astype(held_as)


def setup_inputs(seed: int = 0) -> dict:
    key_of = jax.random.split(jax.random.key(seed), 12)
    return {
        "tokens": normal_values(key_of[0], (REQUESTS, D), 1.0, 6.0, ((0, 256),)),
        "attn_gain": jnp.clip(1.0 + 0.18 * jax.random.normal(key_of[1], (D,), jnp.float32), 0.099609375, 1.8984375).astype(jnp.bfloat16),
        "mlp_gain": jnp.clip(1.0 + 0.18 * jax.random.normal(key_of[2], (D,), jnp.float32), 0.099609375, 1.8984375).astype(jnp.bfloat16),
        "project_in": draw_project_in(jax.random.fold_in(key_of[11], 71), 0),
        "project_out": normal_values(key_of[4], (D, D), D ** -0.5, 0.125, ((0, 16),)),
        "gate_up": normal_values(key_of[5], (2, D, FF), D ** -0.5, 0.125, ((2, 16),)),
        "project_down": normal_values(key_of[6], (FF, D), FF ** -0.5, 0.0625, ((0, 16),)),
        "kv_cache": draw_kv_cache(jax.random.fold_in(key_of[11], 71), 0),
        "lengths": draw_lengths(jax.random.fold_in(key_of[11], 71), 0),
        "owners": draw_owners(jax.random.fold_in(key_of[11], 71), 0),
        "cache_start": draw_cache_start(jax.random.fold_in(key_of[11], 71), 0),
    }


NORM_EPS = 1e-05
ROPE_BASE = 130000.0

def scaled_norm(values, scales):
    wide = values.astype(jnp.float32)
    factor = lax.rsqrt(lax.optimization_barrier(jnp.mean(wide * wide, axis=-1, keepdims=True)) + NORM_EPS)
    return (wide * factor * scales.astype(jnp.float32)).astype(jnp.bfloat16)

def rotate(values, positions, head_size):
    half_size = head_size // 2
    freqs = ROPE_BASE ** (-(jnp.arange(half_size, dtype=jnp.float32) * 2.0 / head_size))
    angles = positions.astype(jnp.float32)[:, None] * freqs[None, :]
    cosine = jnp.cos(angles)[:, None, :]
    sine = jnp.sin(angles)[:, None, :]
    first = values[..., :half_size]
    second = values[..., half_size:]
    return jnp.concatenate([first * cosine - second * sine, second * cosine + first * sine], axis=-1)

def reference(tokens, attn_gain, mlp_gain, project_in, project_out, gate_up, project_down, kv_cache, lengths, owners, cache_start):
    normed = scaled_norm(tokens, attn_gain)
    projected = jnp.einsum('rd,cde->rce', normed.astype(jnp.float32), project_in.astype(jnp.float32))
    request_count = tokens.shape[0]
    queries = rotate(projected[:, 0].reshape(request_count, HEADS, HD), lengths, HD).astype(jnp.bfloat16)
    keys_new = rotate(projected[:, 1].reshape(request_count, HEADS, HD), lengths, HD).astype(jnp.bfloat16)
    values_new = projected[:, 2].reshape(request_count, HEADS, HD).astype(jnp.bfloat16)
    padded = jnp.pad(kv_cache, ((0, 0), (0, MAXLEN), (0, 0)))
    starts = (owners * ROWS + cache_start).astype(jnp.int32)
    scale = 1.0 / HD ** 0.5

    def attend(item):
        query_row, key_row, value_row, start_row, length_row = item
        window = lax.dynamic_slice(padded, (jnp.int32(0), start_row.astype(jnp.int32), jnp.int32(0)), (2, MAXLEN, D))
        past_keys = window[0].astype(jnp.float32).reshape(MAXLEN, HEADS, HD)
        past_values = window[1].astype(jnp.float32).reshape(MAXLEN, HEADS, HD)
        query_wide = query_row.astype(jnp.float32)
        scores = jnp.einsum('he,phe->hp', query_wide, past_keys, precision=lax.Precision.HIGHEST) * scale
        live = (jnp.arange(MAXLEN) < length_row)[None, :]
        scores = jnp.where(live, scores, -jnp.inf)
        own = lax.optimization_barrier(jnp.sum(query_wide * key_row.astype(jnp.float32), axis=-1)) * scale
        top = jnp.maximum(lax.optimization_barrier(jnp.max(scores, axis=-1)), own)
        weights = jnp.where(live, jnp.exp(scores - top[:, None]), 0.0)
        own_weight = jnp.exp(own - top)
        total = lax.optimization_barrier(jnp.sum(weights, axis=-1)) + own_weight
        summed = jnp.einsum('hp,phe->he', weights, past_values, precision=lax.Precision.HIGHEST)
        summed = summed + own_weight[:, None] * value_row.astype(jnp.float32)
        attended = (summed / total[:, None]).astype(jnp.bfloat16).reshape(D)
        return (attended, top + jnp.log(total))
    attention, log_sum_exp = lax.map(attend, (queries, keys_new, values_new, starts, lengths))
    target_rows = (starts + lengths).astype(jnp.int32)
    kv_updated = kv_cache.at[0, target_rows].set(keys_new.reshape(request_count, D))
    kv_updated = kv_updated.at[1, target_rows].set(values_new.reshape(request_count, D))
    resid = (tokens.astype(jnp.float32) + jnp.dot(attention, project_out, preferred_element_type=jnp.float32)).astype(jnp.bfloat16)
    normed_mlp = scaled_norm(resid, mlp_gain)
    gate = jnp.dot(normed_mlp, gate_up[0], preferred_element_type=jnp.float32)
    upward = jnp.dot(normed_mlp, gate_up[1], preferred_element_type=jnp.float32)
    inner = (jax.nn.silu(gate) * upward).astype(jnp.bfloat16)
    hidden_states = (resid.astype(jnp.float32) + jnp.dot(inner, project_down, preferred_element_type=jnp.float32)).astype(jnp.bfloat16)
    return (hidden_states, log_sum_exp, kv_updated)
```

```python
import functools

import jax
import jax.numpy as jnp
import numpy as np
from jax import lax
from jax.experimental import pallas as pl
from jax.experimental.pallas import tpu as pltpu
from jax.sharding import PartitionSpec as P

MESH = pl.DeviceIdType.MESH
BF = jnp.bfloat16
F32 = jnp.float32
I32 = jnp.int32

EPS = 1e-05
ROPE_BASE = 130000.0
LOW = -1e30
HD = 64
NDP = 16
NTP = 16
NZ = 8
D = 2048
HALF = 1024
BLK = 16
REQ = 256
HOME = 128
SLOTS = HOME + NDP * BLK
ROWS = 4096
FFL = 512
PBLK = 512

AG_RIGHT = ((1, 0), (1, 1), (2, 0), (2, 1), (3, 0), (3, 1), (4, 0))
AG_LEFT = ((1, 1), (1, 0), (2, 1), (2, 0), (3, 1), (3, 0), (4, 1))
RS_RIGHT = ((4, 0), (3, 1), (3, 0), (2, 1), (2, 0), (1, 1), (1, 0))
RS_LEFT = ((4, 1), (3, 0), (3, 1), (2, 0), (2, 1), (1, 0), (1, 1))


class Place:
    def __init__(self):
        self.d = lax.axis_index("dp")
        self.t = lax.axis_index("tensor")
        self.z = self.t // 2
        self.c = self.t % 2
        self.sib = (self.d, self.t + 1 - 2 * self.c)
        self.zdev = (
            (self.d, ((self.z + 1) % NZ) * 2 + self.c),
            (self.d, ((self.z + NZ - 1) % NZ) * 2 + self.c),
        )

    def dp_peer(self, offset):
        return (self.d + offset) % NDP


def greet(me):
    barrier = pltpu.get_barrier_semaphore()
    targets = [me.zdev[0], me.zdev[1], me.sib]
    targets += [(me.dp_peer(i), me.t) for i in range(1, NDP)]
    for target in targets:
        pl.semaphore_signal(barrier, inc=1, device_id=target, device_id_type=MESH)
    return lambda: pl.semaphore_wait(barrier, len(targets))


def iota(shape, axis):
    return lax.broadcasted_iota(I32, shape, axis)


def scaled_norm(wide, gain):
    factor = lax.rsqrt(jnp.mean(wide * wide, axis=-1, keepdims=True) + EPS)
    return (wide * factor * gain).astype(BF)


def all_gather_z(me, buf, row_of, ring_send, ring_recv, sib_send, sib_recv):
    lists = (AG_RIGHT, AG_LEFT)
    signs = (1, -1)
    sib_copies = []
    started = []

    def block(origin, half):
        return buf.at[half, pl.ds(pl.multiple_of(row_of(origin, me.c), BLK), BLK), :]

    def message(way, index):
        k, half = lists[way][index]
        origin = (me.z + NZ - signs[way] * (k - 1)) % NZ
        ref = block(origin, half)
        return pltpu.make_async_remote_copy(
            src_ref=ref, dst_ref=ref, send_sem=ring_send.at[way, index], recv_sem=ring_recv.at[way, index],
            device_id=me.zdev[way], device_id_type=MESH,
        )

    def sibling(origin, half):
        index = len(sib_copies)
        ref = block(origin, half)
        copy = pltpu.make_async_remote_copy(
            src_ref=ref, dst_ref=ref, send_sem=sib_send.at[index], recv_sem=sib_recv.at[index],
            device_id=me.sib, device_id_type=MESH,
        )
        copy.start()
        sib_copies.append(copy)

    def start(way, index):
        copy = message(way, index)
        copy.start()
        started.append(copy)

    def begin():
        for index in range(2):
            for way in range(2):
                start(way, index)
        for half in range(2):
            sibling(me.z, half)

    def finish():
        for index in range(7):
            for way in range(2):
                k, half = lists[way][index]
                message(way, index).wait_recv()
                if (k + 1, half) in lists[way]:
                    start(way, lists[way].index((k + 1, half)))
                sibling((me.z + NZ - signs[way] * k) % NZ, half)
        for copy in sib_copies:
            copy.wait_recv()

    def drain():
        for copy in started:
            copy.wait_send()
        for copy in sib_copies:
            copy.wait_send()

    return begin, finish, drain


def reduce_scatter_z(me, product, sib_out, sib_in, own, ring_out, ring_in, ring_send, ring_recv, sib_send, sib_recv):
    lists = (RS_RIGHT, RS_LEFT)
    signs = (1, -1)
    started = []

    def message(way, index):
        return pltpu.make_async_remote_copy(
            src_ref=ring_out.at[way, index], dst_ref=ring_in.at[way, index],
            send_sem=ring_send.at[way, index], recv_sem=ring_recv.at[way, index],
            device_id=me.zdev[way], device_id_type=MESH,
        )

    def mine(way, distance, half):
        target = (me.z + NZ + signs[way] * distance) % NZ
        return own[half, pl.ds(pl.multiple_of(target * BLK, BLK), BLK), :]

    def send(way, index, value):
        ring_out[way, index] = value.astype(BF)
        copy = message(way, index)
        copy.start()
        started.append(copy)

    for half in range(2):
        product(half, 1 - me.c, sib_out)
        copy = pltpu.make_async_remote_copy(
            src_ref=sib_out.at[half], dst_ref=sib_in.at[half], send_sem=sib_send.at[half], recv_sem=sib_recv.at[half],
            device_id=me.sib, device_id_type=MESH,
        )
        copy.start()
        started.append(copy)
        product(half, me.c, own)
    for half in range(2):
        started[half].wait_recv()
        own[half] = own[half] + sib_in[half].astype(F32)
        first = half
        send(first, 0, mine(first, 4, half))
        send(1 - first, 1, mine(1 - first, 3, half))
        if half == 1:
            pass
    total = [own[half, pl.ds(pl.multiple_of(me.z * BLK, BLK), BLK), :] for half in range(2)]
    for index in range(7):
        for way in range(2):
            distance, half = lists[way][index]
            message(way, index).wait_recv()
            arrived = ring_in[way, index].astype(F32)
            if distance > 1:
                send(way, lists[way].index((distance - 1, half)), arrived + mine(way, distance - 1, half))
            else:
                total[half] = total[half] + arrived
    return total, lambda: [copy.wait_send() for copy in started]


def exchange_dp(me, source, landing, send, recv):
    copies = []
    for i in range(1, NDP):
        peer = me.dp_peer(i)
        copy = pltpu.make_async_remote_copy(
            src_ref=source.at[pl.ds(pl.multiple_of(peer * BLK, BLK), BLK), :],
            dst_ref=landing.at[pl.ds(pl.multiple_of(me.d * BLK, BLK), BLK), :],
            send_sem=send.at[i - 1], recv_sem=recv.at[i - 1],
            device_id=(peer, me.t), device_id_type=MESH,
        )
        copy.start()
        copies.append(copy)
    here = pl.ds(pl.multiple_of(me.d * BLK, BLK), BLK)
    landing[here, :] = source[here, :]
    return copies


def column_of(row, hits):
    return jnp.sum(jnp.where(hits, row, 0.0), axis=1, keepdims=True)


def first_kernel(
    tokens, gain, lengths, owners, starts, freqs, w_hbm,
    compact_out, start_out, end_out, end_row_out, sel_out, scat_out,
    gathered, w, packed, outgoing, arrived,
    ring_send, ring_recv, sib_send, sib_recv, dp_send, dp_recv, w_sem,
):
    me = Place()
    w_copies = [
        pltpu.make_async_copy(w_hbm.at[m], w.at[:, pl.ds(m * 128, 128)], w_sem.at[m]) for m in range(3)
    ]
    for copy in w_copies:
        copy.start()
    wait_all = greet(me)
    normed = scaled_norm(tokens[...].astype(F32), gain[...].astype(F32))
    row_of = lambda zz, cc: (zz * 2 + cc) * BLK
    my_rows = pl.ds(pl.multiple_of(row_of(me.z, me.c), BLK), BLK)
    for half in range(2):
        gathered[half, my_rows, :] = normed[:, half * HALF : (half + 1) * HALF]
    wait_all()
    begin, finish, drain = all_gather_z(me, gathered, row_of, ring_send, ring_recv, sib_send, sib_recv)
    begin()

    def wide(ref):
        return jnp.concatenate([ref[pl.ds(0, NDP, stride=2), :], ref[pl.ds(1, NDP, stride=2), :]], axis=1)

    def mine(ref):
        return jnp.concatenate([ref[pl.ds(2 * me.d, 1), :], ref[pl.ds(2 * me.d + 1, 1), :]], axis=1)

    own_all, len_all, start_all = wide(owners), wide(lengths), wide(starts)
    own_row, len_row, start_row = mine(owners), mine(lengths).astype(F32), mine(starts).astype(F32)
    before = jnp.where(iota((REQ, REQ), 0) < iota((REQ, REQ), 1), 1.0, 0.0).astype(BF)
    here = own_all == me.d
    here_rank = jnp.dot(jnp.where(here, 1.0, 0.0).astype(BF), before, preferred_element_type=F32)
    away = here & (iota((NDP, REQ), 0) != me.d)
    place_in = jnp.where(away, here_rank, -1.0)
    onehot = jnp.where(iota((NDP, REQ), 0) == own_row, 1.0, 0.0)
    counts = jnp.dot(onehot.astype(BF), before, preferred_element_type=F32)
    rank = jnp.sum(onehot * counts, axis=0, keepdims=True)
    own_wide = own_row.astype(F32)
    place = jnp.where(own_row == me.d, rank, HOME + own_wide * BLK + rank)
    sel = iota((SLOTS, REQ), 0).astype(F32) == place
    sel_out[...] = jnp.where(sel, 1.0, 0.0).astype(BF)
    request = iota((REQ, REQ), 0)
    natural = ((request >> 4) & 7) * 32 + (request >> 7) * 16 + (request & 15)
    place_col = column_of(place, natural == iota((REQ, REQ), 1))
    scat_out[...] = jnp.where(iota((REQ, SLOTS), 1).astype(F32) == place_col, 1.0, 0.0).astype(BF)

    def spread(rows16):
        return jnp.concatenate(
            [jnp.broadcast_to(rows16[b : b + 1, :], (BLK, REQ)) for b in range(NDP)], axis=0
        )

    slot = (iota((NDP * BLK, REQ), 0) & (BLK - 1)).astype(F32)
    hits_in = spread(place_in) == slot
    begin_all = start_all.astype(F32)
    finish_all = begin_all + len_all.astype(F32)
    hits_home = sel[:HOME]
    begin_col = jnp.concatenate(
        [column_of(start_row + 1.0, hits_home), column_of(spread(begin_all) + 1.0, hits_in)], axis=0
    ) - 1.0
    finish_col = jnp.concatenate(
        [column_of(start_row + len_row + 1.0, hits_home), column_of(spread(finish_all) + 1.0, hits_in)], axis=0
    ) - 1.0
    start_out[...] = jnp.broadcast_to(begin_col, (SLOTS, 128))
    end_out[...] = jnp.broadcast_to(finish_col, (SLOTS, 128))
    eye = iota((SLOTS, SLOTS), 0) == iota((SLOTS, SLOTS), 1)
    end_row = jnp.sum(jnp.where(eye, finish_col, 0.0), axis=0, keepdims=True)
    end_row_out[...] = jnp.broadcast_to(end_row, (8, SLOTS))

    len_col = column_of(len_row, iota((REQ, REQ), 0) == iota((REQ, REQ), 1))
    angle = len_col * freqs[...]
    turns = jnp.floor(angle * (1.0 / (2.0 * np.pi)) + 0.5)
    left = (angle - turns * 6.28125) - turns * np.float32(2.0 * np.pi - 6.28125)
    x = 0.5 * left
    x2 = x * x
    sin_half = x * (1.0 + x2 * (-1 / 6 + x2 * (1 / 120 + x2 * (-1 / 5040 + x2 * (1 / 362880 - x2 / 39916800)))))
    cos_half = 1.0 + x2 * (
        -1 / 2 + x2 * (1 / 24 + x2 * (-1 / 720 + x2 * (1 / 40320 + x2 * (-1 / 3628800 + x2 / 479001600))))
    )
    sine = 2.0 * sin_half * cos_half
    cosine = 1.0 - 2.0 * sin_half * sin_half
    low_half = (iota((REQ, 128), 1) & (HD - 1)) < HD // 2
    signed = jnp.where(low_half, -sine, sine)

    finish()
    for copy in w_copies:
        copy.wait()
    projected = jnp.dot(gathered[0], w[:HALF], preferred_element_type=F32)
    projected = projected + jnp.dot(gathered[1], w[HALF:], preferred_element_type=F32)

    def turned(values):
        partner = jnp.where(low_half, pltpu.roll(values, 96, 1), pltpu.roll(values, 32, 1))
        return (values * cosine + partner * signed).astype(BF)

    packed[:, 0:128] = turned(projected[:, 0:128])
    packed[:, 128:256] = turned(projected[:, 128:256])
    packed[:, 256:384] = projected[:, 256:384].astype(BF)
    compact = jnp.dot(sel_out[...], packed[...], preferred_element_type=F32).astype(BF)
    outgoing[...] = compact[HOME:]
    copies = exchange_dp(me, outgoing, arrived, dp_send, dp_recv)
    compact_out[:HOME, :] = compact[:HOME]
    drain()
    for copy in copies:
        copy.wait_recv()
    compact_out[HOME:, :] = arrived[...]
    for copy in copies:
        copy.wait_send()


def middle_kernel(compact, start_ref, end_ref, end_row, cache, cache_out, ret, q2, live_top, live_sum, live_out):
    step = pl.program_id(0)
    low_lanes = iota((SLOTS, 128), 1) < HD

    @pl.when(step == 0)
    def _():
        q = compact[:, 0:128].astype(F32) * (1.0 / 8.0)
        k = compact[:, 128:256].astype(F32)
        v = compact[:, 256:384].astype(F32)
        for head in range(2):
            keep = low_lanes if head == 0 else jnp.logical_not(low_lanes)
            qh = jnp.where(keep, q, 0.0)
            rows = pl.ds(head * SLOTS, SLOTS)
            q2[rows, :] = qh.astype(BF)
            live_top[rows, :] = jnp.broadcast_to(jnp.sum(qh * k, axis=1, keepdims=True), (SLOTS, 128))
            live_sum[rows, :] = jnp.ones((SLOTS, 128), F32)
            live_out[rows, :] = v

    keys = cache[0]
    values = cache[1]
    base = step * PBLK
    position = (iota((PBLK, SLOTS), 0) + base).astype(F32)
    place = jnp.where(position == end_row[0:1, :], 1.0, 0.0)
    hit = jnp.max(place, axis=1, keepdims=True) > 0.5
    fresh = jnp.dot(place.astype(BF), compact[:, 128:384], preferred_element_type=F32)
    cache_out[0] = jnp.where(hit, fresh[:, 0:128], keys.astype(F32)).astype(BF)
    cache_out[1] = jnp.where(hit, fresh[:, 128:256], values.astype(F32)).astype(BF)

    across = (iota((SLOTS, PBLK), 1) + base).astype(F32)
    live = (across >= start_ref[:, 0:1]) & (across < end_ref[:, 0:1])
    for head in range(2):
        rows = pl.ds(head * SLOTS, SLOTS)
        scores = lax.dot_general(q2[rows, :], keys, (((1,), (1,)), ((), ())), preferred_element_type=F32)
        scores = jnp.where(live, scores, LOW)
        old_top = live_top[rows, 0:1]
        top = jnp.maximum(old_top, jnp.max(scores, axis=1, keepdims=True))
        weights = jnp.where(live, jnp.exp(scores - top), 0.0)
        factor = jnp.exp(old_top - top)
        live_sum[rows, :] = live_sum[rows, :] * factor + jnp.sum(weights, axis=1, keepdims=True)
        live_out[rows, :] = live_out[rows, :] * factor + jnp.dot(weights.astype(BF), values, preferred_element_type=F32)
        live_top[rows, :] = jnp.broadcast_to(top, (SLOTS, 128))

    @pl.when(step == pl.num_programs(0) - 1)
    def _():
        out = live_out[...] / live_sum[...]
        ret[:, 0:128] = jnp.where(low_lanes, out[:SLOTS], out[SLOTS:]).astype(BF)
        lse = live_top[...] + jnp.log(live_sum[...])
        high = lse.astype(BF).astype(F32)
        low = lse - high
        lane = iota((SLOTS, 128), 1)
        tail = jnp.where(lane == 0, high[:SLOTS], jnp.where(lane == 1, low[:SLOTS], jnp.where(lane == 2, high[SLOTS:], low[SLOTS:])))
        ret[:, 128:256] = tail.astype(BF)


def last_kernel(
    tokens, gain, ret, sel, scat, wo_hbm, gu_hbm, wd_hbm,
    hidden_out, lse_out,
    slots, landing, outgoing, attended, wo, gu, wd, gathered, inner, resid_keep,
    sib_out, sib_in, own, ring_out, ring_in,
    dp_send, dp_recv, ag_ring_send, ag_ring_recv, ag_sib_send, ag_sib_recv,
    rs_ring_send, rs_ring_recv, rs_sib_send, rs_sib_recv, w_sem,
):
    me = Place()
    wait_all = greet(me)
    w_copies = [
        pltpu.make_async_copy(wo_hbm, wo, w_sem.at[0]),
        pltpu.make_async_copy(gu_hbm, gu, w_sem.at[1]),
        pltpu.make_async_copy(wd_hbm, wd, w_sem.at[2]),
    ]
    for copy in w_copies:
        copy.start()
    outgoing[...] = ret[HOME:, :]
    slots[:HOME, :] = ret[:HOME, :]
    wait_all()
    copies = exchange_dp(me, outgoing, landing, dp_send, dp_recv)
    for copy in copies:
        copy.wait_recv()
    slots[HOME:, :] = landing[...]
    attended[...] = jnp.dot(scat[...], slots[:, 0:128], preferred_element_type=F32).astype(BF)
    w_copies[0].wait()

    def out_product(half, core, target):
        rows = pl.ds(pl.multiple_of(core * 128, 128), 128)
        value = jnp.dot(attended[rows, :], wo[:, half * HALF : (half + 1) * HALF], preferred_element_type=F32)
        target[half] = value.astype(target.dtype)

    total, drain_first = reduce_scatter_z(
        me, out_product, sib_out.at[0], sib_in.at[0], own, ring_out.at[0], ring_in.at[0],
        rs_ring_send.at[0], rs_ring_recv.at[0], rs_sib_send.at[0], rs_sib_recv.at[0],
    )
    resid = tokens[...].astype(F32) + jnp.concatenate(total, axis=1)
    resid = resid.astype(BF)
    resid_keep[...] = resid
    normed = scaled_norm(resid.astype(F32), gain[...].astype(F32))
    row_of = lambda zz, cc: cc * 128 + zz * BLK
    my_rows = pl.ds(pl.multiple_of(row_of(me.z, me.c), BLK), BLK)
    for half in range(2):
        gathered[half, my_rows, :] = normed[:, half * HALF : (half + 1) * HALF]
    begin, finish, drain = all_gather_z(me, gathered, row_of, ag_ring_send, ag_ring_recv, ag_sib_send, ag_sib_recv)
    begin()
    wide = sel[...].astype(F32)
    tail = slots[:, 128:256].astype(F32)
    for head in range(2):
        lse = tail[:, 2 * head : 2 * head + 1] + tail[:, 2 * head + 1 : 2 * head + 2]
        lse_out[head : head + 1, :] = jnp.sum(wide * lse, axis=0, keepdims=True)
    drain_first()
    for copy in copies:
        copy.wait_send()
    finish()
    w_copies[1].wait()
    w_copies[2].wait()
    for tile in range(FFL // 256):
        columns = pl.ds(tile * 256, 256)
        both = []
        for m in range(2):
            value = jnp.dot(gathered[0], gu[m, :HALF, columns], preferred_element_type=F32)
            both.append(value + jnp.dot(gathered[1], gu[m, HALF:, columns], preferred_element_type=F32))
        inner[:, columns] = (both[0] / (1.0 + jnp.exp(-both[0])) * both[1]).astype(BF)

    def down_product(half, core, target):
        rows = pl.ds(pl.multiple_of(core * 128, 128), 128)
        value = jnp.dot(inner[rows, :], wd[:, half * HALF : (half + 1) * HALF], preferred_element_type=F32)
        target[half] = value.astype(target.dtype)

    total, drain_last = reduce_scatter_z(
        me, down_product, sib_out.at[1], sib_in.at[1], own, ring_out.at[1], ring_in.at[1],
        rs_ring_send.at[1], rs_ring_recv.at[1], rs_sib_send.at[1], rs_sib_recv.at[1],
    )
    hidden_out[...] = (resid_keep[...].astype(F32) + jnp.concatenate(total, axis=1)).astype(BF)
    drain()
    drain_last()


VMEM_SPEC = pl.BlockSpec(memory_space=pltpu.VMEM)
ANY_SPEC = pl.BlockSpec(memory_space=pl.ANY)
DMA = pltpu.SemaphoreType.DMA


def on_device(tokens, attn_gain, mlp_gain, project_in, project_out, gate_up, project_down, kv_cache, lengths, owners, cache_start):
    half_index = np.arange(HD // 2, dtype=np.float32) * np.float32(2.0) / np.float32(HD)
    freqs = jnp.asarray(np.tile(np.float32(ROPE_BASE) ** -half_index, 4).astype(np.float32)[None, :])
    ints = [values.reshape(32, 128) for values in (lengths, owners, cache_start)]
    shape = jax.ShapeDtypeStruct
    compact, begin_col, end_col, end_row, sel, scat = pl.pallas_call(
        first_kernel,
        out_shape=(
            shape((SLOTS, 384), BF), shape((SLOTS, 128), F32), shape((SLOTS, 128), F32), shape((8, SLOTS), F32),
            shape((SLOTS, REQ), BF), shape((REQ, SLOTS), BF),
        ),
        in_specs=[VMEM_SPEC] * 6 + [ANY_SPEC],
        out_specs=(VMEM_SPEC,) * 6,
        scratch_shapes=[
            pltpu.VMEM((2, REQ, HALF), BF), pltpu.VMEM((D, 384), BF), pltpu.VMEM((REQ, 384), BF),
            pltpu.VMEM((NDP * BLK, 384), BF), pltpu.VMEM((NDP * BLK, 384), BF),
            DMA((2, 7)), DMA((2, 7)), DMA((16,)), DMA((16,)), DMA((15,)), DMA((15,)), DMA((3,)),
        ],
        compiler_params=pltpu.CompilerParams(collective_id=0, has_side_effects=True, vmem_limit_bytes=40 << 20),
        name="gather_project_route",
    )(tokens, attn_gain.reshape(1, D), *ints, freqs, project_in)

    whole = lambda *dims: pl.BlockSpec(dims, lambda s: (0,) * len(dims))
    kv_updated, ret = pl.pallas_call(
        middle_kernel,
        grid=(ROWS // PBLK,),
        out_shape=(shape((2, ROWS, 128), BF), shape((SLOTS, 256), BF)),
        in_specs=[
            whole(SLOTS, 384), whole(SLOTS, 128), whole(SLOTS, 128), whole(8, SLOTS),
            pl.BlockSpec((2, PBLK, 128), lambda s: (0, s, 0)),
        ],
        out_specs=(pl.BlockSpec((2, PBLK, 128), lambda s: (0, s, 0)), whole(SLOTS, 256)),
        scratch_shapes=[
            pltpu.VMEM((2 * SLOTS, 128), BF), pltpu.VMEM((2 * SLOTS, 128), F32), pltpu.VMEM((2 * SLOTS, 128), F32),
            pltpu.VMEM((2 * SLOTS, 128), F32),
        ],
        compiler_params=pltpu.CompilerParams(vmem_limit_bytes=40 << 20),
        name="attend_update",
    )(compact, begin_col, end_col, end_row, kv_cache)

    hidden_states, lse = pl.pallas_call(
        last_kernel,
        out_shape=(shape((BLK, D), BF), shape((2, REQ), F32)),
        in_specs=[VMEM_SPEC] * 5 + [ANY_SPEC] * 3,
        out_specs=(VMEM_SPEC,) * 2,
        scratch_shapes=[
            pltpu.VMEM((SLOTS, 256), BF), pltpu.VMEM((NDP * BLK, 256), BF), pltpu.VMEM((NDP * BLK, 256), BF),
            pltpu.VMEM((REQ, 128), BF), pltpu.VMEM((128, D), BF), pltpu.VMEM((2, D, FFL), BF), pltpu.VMEM((FFL, D), BF),
            pltpu.VMEM((2, REQ, HALF), BF), pltpu.VMEM((REQ, FFL), BF), pltpu.VMEM((BLK, D), BF),
            pltpu.VMEM((2, 2, 128, HALF), BF), pltpu.VMEM((2, 2, 128, HALF), BF), pltpu.VMEM((2, 128, HALF), F32),
            pltpu.VMEM((2, 2, 7, BLK, HALF), BF), pltpu.VMEM((2, 2, 7, BLK, HALF), BF),
            DMA((15,)), DMA((15,)), DMA((2, 7)), DMA((2, 7)), DMA((16,)), DMA((16,)),
            DMA((2, 2, 7)), DMA((2, 2, 7)), DMA((2, 2)), DMA((2, 2)), DMA((3,)),
        ],
        compiler_params=pltpu.CompilerParams(collective_id=1, has_side_effects=True, vmem_limit_bytes=48 << 20),
        name="return_project_mlp",
    )(tokens, mlp_gain.reshape(1, D), ret, sel, scat, project_out, gate_up, project_down)
    return hidden_states, lse.T, kv_updated


def solution(mesh):
    placed = (
        P(("dp", "tensor"), None),
        P(),
        P(),
        P(None, None, "tensor"),
        P("tensor", None),
        P(None, None, "tensor"),
        P("tensor", None),
        P(None, "dp", "tensor"),
        P(),
        P(),
        P(),
    )
    return jax.shard_map(
        on_device,
        mesh=mesh,
        in_specs=placed,
        out_specs=(P(("dp", "tensor"), None), P("dp", "tensor"), P(None, "dp", "tensor")),
        check_vma=False,
    )
```

```python
import functools

import jax
import jax.numpy as jnp
import numpy as np
from jax import lax
from jax.experimental import pallas as pl
from jax.experimental.pallas import tpu as pltpu
from jax.sharding import PartitionSpec as P

MESH = pl.DeviceIdType.MESH
BF = jnp.bfloat16
F32 = jnp.float32
I32 = jnp.int32

EPS = 1e-05
ROPE_BASE = 130000.0
LOW = -1e30
HD = 64
NDP = 16
NTP = 16
NZ = 8
D = 2048
HALF = 1024
BLK = 16
REQ = 256
HOME = 128
SLOTS = HOME + NDP * BLK
ROWS = 4096
FFL = 512
PBLK = 1024

AG_RIGHT = ((1, 0), (1, 1), (2, 0), (2, 1), (3, 0), (3, 1), (4, 0))
AG_LEFT = ((1, 1), (1, 0), (2, 1), (2, 0), (3, 1), (3, 0), (4, 1))
RS_RIGHT = ((4, 0), (3, 1), (3, 0), (2, 1), (2, 0), (1, 1), (1, 0))
RS_LEFT = ((4, 1), (3, 0), (3, 1), (2, 0), (2, 1), (1, 0), (1, 1))


class Place:
    def __init__(self):
        self.d = lax.axis_index("dp")
        self.t = lax.axis_index("tensor")
        self.z = self.t // 2
        self.c = self.t % 2
        self.sib = (self.d, self.t + 1 - 2 * self.c)
        self.zdev = (
            (self.d, ((self.z + 1) % NZ) * 2 + self.c),
            (self.d, ((self.z + NZ - 1) % NZ) * 2 + self.c),
        )

    def dp_peer(self, offset):
        return (self.d + offset) % NDP


def greet(me):
    barrier = pltpu.get_barrier_semaphore()
    targets = [me.zdev[0], me.zdev[1], me.sib]
    targets += [(me.dp_peer(i), me.t) for i in range(1, NDP)]
    for target in targets:
        pl.semaphore_signal(barrier, inc=1, device_id=target, device_id_type=MESH)
    return lambda: pl.semaphore_wait(barrier, len(targets))


def iota(shape, axis):
    return lax.broadcasted_iota(I32, shape, axis)


def scaled_norm(wide, gain):
    factor = lax.rsqrt(jnp.mean(wide * wide, axis=-1, keepdims=True) + EPS)
    return (wide * factor * gain).astype(BF)


def all_gather_z(me, buf, row_of, ring_send, ring_recv, sib_send, sib_recv):
    lists = (AG_RIGHT, AG_LEFT)
    signs = (1, -1)
    sib_copies = []
    started = []

    def block(origin, half):
        return buf.at[half, pl.ds(pl.multiple_of(row_of(origin, me.c), BLK), BLK), :]

    def message(way, index):
        k, half = lists[way][index]
        origin = (me.z + NZ - signs[way] * (k - 1)) % NZ
        ref = block(origin, half)
        return pltpu.make_async_remote_copy(
            src_ref=ref, dst_ref=ref, send_sem=ring_send.at[way, index], recv_sem=ring_recv.at[way, index],
            device_id=me.zdev[way], device_id_type=MESH,
        )

    def sibling(origin, half):
        index = len(sib_copies)
        ref = block(origin, half)
        copy = pltpu.make_async_remote_copy(
            src_ref=ref, dst_ref=ref, send_sem=sib_send.at[index], recv_sem=sib_recv.at[index],
            device_id=me.sib, device_id_type=MESH,
        )
        copy.start()
        sib_copies.append(copy)

    def start(way, index):
        copy = message(way, index)
        copy.start()
        started.append(copy)

    def begin():
        for index in range(2):
            for way in range(2):
                start(way, index)
        for half in range(2):
            sibling(me.z, half)

    def finish():
        for index in range(7):
            for way in range(2):
                k, half = lists[way][index]
                message(way, index).wait_recv()
                if (k + 1, half) in lists[way]:
                    start(way, lists[way].index((k + 1, half)))
                sibling((me.z + NZ - signs[way] * k) % NZ, half)
        for copy in sib_copies:
            copy.wait_recv()

    def drain():
        for copy in started:
            copy.wait_send()
        for copy in sib_copies:
            copy.wait_send()

    return begin, finish, drain


def reduce_scatter_z(me, product, sib_out, sib_in, own, ring_out, ring_in, ring_send, ring_recv, sib_send, sib_recv):
    lists = (RS_RIGHT, RS_LEFT)
    signs = (1, -1)
    started = []

    def message(way, index):
        return pltpu.make_async_remote_copy(
            src_ref=ring_out.at[way, index], dst_ref=ring_in.at[way, index],
            send_sem=ring_send.at[way, index], recv_sem=ring_recv.at[way, index],
            device_id=me.zdev[way], device_id_type=MESH,
        )

    def mine(way, distance, half):
        target = (me.z + NZ + signs[way] * distance) % NZ
        return own[half, pl.ds(pl.multiple_of(target * BLK, BLK), BLK), :]

    def send(way, index, value):
        ring_out[way, index] = value.astype(BF)
        copy = message(way, index)
        copy.start()
        started.append(copy)

    for half in range(2):
        product(half, 1 - me.c, sib_out)
        copy = pltpu.make_async_remote_copy(
            src_ref=sib_out.at[half], dst_ref=sib_in.at[half], send_sem=sib_send.at[half], recv_sem=sib_recv.at[half],
            device_id=me.sib, device_id_type=MESH,
        )
        copy.start()
        started.append(copy)
        product(half, me.c, own)
    for half in range(2):
        started[half].wait_recv()
        own[half] = own[half] + sib_in[half].astype(F32)
        first = half
        send(first, 0, mine(first, 4, half))
        send(1 - first, 1, mine(1 - first, 3, half))
    total = [own[half, pl.ds(pl.multiple_of(me.z * BLK, BLK), BLK), :] for half in range(2)]
    for index in range(7):
        for way in range(2):
            distance, half = lists[way][index]
            message(way, index).wait_recv()
            arrived = ring_in[way, index].astype(F32)
            if distance > 1:
                send(way, lists[way].index((distance - 1, half)), arrived + mine(way, distance - 1, half))
            else:
                total[half] = total[half] + arrived
    return total, lambda: [copy.wait_send() for copy in started]


def exchange_dp(me, source, landing, send, recv):
    copies = []
    for i in range(1, NDP):
        peer = me.dp_peer(i)
        copy = pltpu.make_async_remote_copy(
            src_ref=source.at[pl.ds(pl.multiple_of(peer * BLK, BLK), BLK), :],
            dst_ref=landing.at[pl.ds(pl.multiple_of(me.d * BLK, BLK), BLK), :],
            send_sem=send.at[i - 1], recv_sem=recv.at[i - 1],
            device_id=(peer, me.t), device_id_type=MESH,
        )
        copy.start()
        copies.append(copy)
    here = pl.ds(pl.multiple_of(me.d * BLK, BLK), BLK)
    landing[here, :] = source[here, :]
    return copies


def column_of(row, hits):
    return jnp.sum(jnp.where(hits, row, 0.0), axis=1, keepdims=True)


def layer_kernel(
    tokens_hbm, attn_gain_hbm, mlp_gain_hbm, lengths_hbm, owners_hbm, starts_hbm, w_hbm, wo_hbm, gu_hbm, wd_hbm, cache_hbm,
    hidden_out, lse_out, cache_out,
    tokens, attn_gain, mlp_gain, ints, w, wo, gu, wd, cache,
    gathered, packed, compact, outgoing, sel, scat, begin_ref, end_ref, end_row,
    q2, top_ref, out_ref, ret_home, ret_away, landing, slots, attended, inner, resid_keep,
    sib_out, sib_in, own, ring_out, ring_in,
    dp_send, dp_recv, ag_ring_send, ag_ring_recv, ag_sib_send, ag_sib_recv,
    rs_ring_send, rs_ring_recv, rs_sib_send, rs_sib_recv, load_sem, store_sem,
):
    me = Place()
    pairs = [
        (tokens_hbm, tokens), (attn_gain_hbm, attn_gain), (owners_hbm, ints.at[0]), (lengths_hbm, ints.at[1]),
        (starts_hbm, ints.at[2]), (w_hbm.at[0], w.at[:, pl.ds(0, 128)]), (w_hbm.at[1], w.at[:, pl.ds(128, 128)]),
        (w_hbm.at[2], w.at[:, pl.ds(256, 128)]), (cache_hbm, cache), (wo_hbm, wo), (mlp_gain_hbm, mlp_gain), (gu_hbm, gu), (wd_hbm, wd),
    ]
    loads = [pltpu.make_async_copy(src, dst, load_sem.at[i]) for i, (src, dst) in enumerate(pairs)]
    for copy in loads:
        copy.start()
    wait_all = greet(me)
    loads[0].wait()
    loads[1].wait()

    def gain_row(ref):
        return jnp.concatenate([ref[i : i + 1, :].astype(F32) for i in range(16)], axis=1)

    normed = scaled_norm(tokens[...].astype(F32), gain_row(attn_gain))
    row_of = lambda zz, cc: (zz * 2 + cc) * BLK
    my_rows = pl.ds(pl.multiple_of(row_of(me.z, me.c), BLK), BLK)
    for half in range(2):
        gathered[0, half, my_rows, :] = normed[:, half * HALF : (half + 1) * HALF]
    wait_all()
    begin, finish, drain_gather = all_gather_z(
        me, gathered.at[0], row_of, ag_ring_send.at[0], ag_ring_recv.at[0], ag_sib_send.at[0], ag_sib_recv.at[0]
    )
    begin()

    for copy in loads[2:5]:
        copy.wait()

    def wide(m):
        return jnp.concatenate([ints[m, pl.ds(0, NDP, stride=2), :], ints[m, pl.ds(1, NDP, stride=2), :]], axis=1)

    def mine(m):
        return jnp.concatenate([ints[m, pl.ds(2 * me.d, 1), :], ints[m, pl.ds(2 * me.d + 1, 1), :]], axis=1)

    own_all, len_all, start_all = wide(0), wide(1), wide(2)
    own_row, len_row, start_row = mine(0), mine(1).astype(F32), mine(2).astype(F32)
    before = jnp.where(iota((REQ, REQ), 0) < iota((REQ, REQ), 1), 1.0, 0.0).astype(BF)
    here = own_all == me.d
    here_rank = jnp.dot(jnp.where(here, 1.0, 0.0).astype(BF), before, preferred_element_type=F32)
    away = here & (iota((NDP, REQ), 0) != me.d)
    place_in = jnp.where(away, here_rank, -1.0)
    onehot = jnp.where(iota((NDP, REQ), 0) == own_row, 1.0, 0.0)
    counts = jnp.dot(onehot.astype(BF), before, preferred_element_type=F32)
    rank = jnp.sum(onehot * counts, axis=0, keepdims=True)
    own_wide = own_row.astype(F32)
    place = jnp.where(own_row == me.d, rank, HOME + own_wide * BLK + rank)
    chosen = iota((SLOTS, REQ), 0).astype(F32) == place
    sel[...] = jnp.where(chosen, 1.0, 0.0).astype(BF)
    request = iota((REQ, REQ), 0)
    natural = ((request >> 4) & 7) * 32 + (request >> 7) * 16 + (request & 15)
    place_col = column_of(place, natural == iota((REQ, REQ), 1))
    scat[...] = jnp.where(iota((REQ, SLOTS), 1).astype(F32) == place_col, 1.0, 0.0).astype(BF)

    def spread(rows16):
        return jnp.concatenate(
            [jnp.broadcast_to(rows16[b : b + 1, :], (BLK, REQ)) for b in range(NDP)], axis=0
        )

    slot = (iota((NDP * BLK, REQ), 0) & (BLK - 1)).astype(F32)
    hits_in = spread(place_in) == slot
    begin_all = start_all.astype(F32)
    finish_all = begin_all + len_all.astype(F32)
    hits_home = chosen[:HOME]
    begin_col = jnp.concatenate(
        [column_of(start_row + 1.0, hits_home), column_of(spread(begin_all) + 1.0, hits_in)], axis=0
    ) - 1.0
    finish_col = jnp.concatenate(
        [column_of(start_row + len_row + 1.0, hits_home), column_of(spread(finish_all) + 1.0, hits_in)], axis=0
    ) - 1.0
    begin_ref[...] = jnp.broadcast_to(begin_col, (SLOTS, 128))
    end_ref[...] = jnp.broadcast_to(finish_col, (SLOTS, 128))
    eye = iota((SLOTS, SLOTS), 0) == iota((SLOTS, SLOTS), 1)
    end_row[...] = jnp.broadcast_to(jnp.sum(jnp.where(eye, finish_col, 0.0), axis=0, keepdims=True), (8, SLOTS))

    len_col = column_of(len_row, iota((REQ, REQ), 0) == iota((REQ, REQ), 1))
    lane = iota((1, 128), 1) & (HD // 2 - 1)
    freqs = jnp.exp(lane.astype(F32) * np.float32(-np.log(ROPE_BASE) / (HD // 2)))
    angle = len_col * freqs
    turns = jnp.floor(angle * (1.0 / (2.0 * np.pi)) + 0.5)
    left = (angle - turns * 6.28125) - turns * np.float32(2.0 * np.pi - 6.28125)
    x = 0.5 * left
    x2 = x * x
    sin_half = x * (1.0 + x2 * (-1 / 6 + x2 * (1 / 120 + x2 * (-1 / 5040 + x2 * (1 / 362880 - x2 / 39916800)))))
    cos_half = 1.0 + x2 * (
        -1 / 2 + x2 * (1 / 24 + x2 * (-1 / 720 + x2 * (1 / 40320 + x2 * (-1 / 3628800 + x2 / 479001600))))
    )
    sine = 2.0 * sin_half * cos_half
    cosine = 1.0 - 2.0 * sin_half * sin_half
    low_half = (iota((REQ, 128), 1) & (HD - 1)) < HD // 2
    signed = jnp.where(low_half, -sine, sine)

    finish()
    for copy in loads[5:8]:
        copy.wait()
    projected = jnp.dot(gathered[0, 0], w[:HALF], preferred_element_type=F32)
    projected = projected + jnp.dot(gathered[0, 1], w[HALF:], preferred_element_type=F32)

    def turned(values):
        partner = jnp.where(low_half, pltpu.roll(values, 96, 1), pltpu.roll(values, 32, 1))
        return (values * cosine + partner * signed).astype(BF)

    packed[:, 0:128] = turned(projected[:, 0:128])
    packed[:, 128:256] = turned(projected[:, 128:256])
    packed[:, 256:384] = projected[:, 256:384].astype(BF)
    outgoing[...] = jnp.dot(sel[HOME:, :], packed[...], preferred_element_type=F32).astype(BF)
    sent = exchange_dp(me, outgoing, compact.at[pl.ds(HOME, NDP * BLK), :], dp_send.at[0], dp_recv.at[0])
    compact[:HOME, :] = jnp.dot(sel[:HOME, :], packed[...], preferred_element_type=F32).astype(BF)
    loads[8].wait()

    def attend(first, count, ret):
        low_lanes = iota((count, 128), 1) < HD
        rows = pl.ds(first, count)
        q = compact[rows, 0:128].astype(F32) * (1.0 / 8.0)
        k = compact[rows, 128:256].astype(F32)
        v = compact[rows, 256:384].astype(F32)
        for head in range(2):
            keep = low_lanes if head == 0 else jnp.logical_not(low_lanes)
            qh = jnp.where(keep, q, 0.0)
            own_rows = pl.ds(head * count, count)
            q2[own_rows, :] = qh.astype(BF)
            top_ref[own_rows, :] = jnp.broadcast_to(jnp.sum(qh * k, axis=1, keepdims=True), (count, 128))
            out_ref[own_rows, 0:128] = v
            out_ref[own_rows, 128:256] = jnp.ones((count, 128), F32)

        @pl.loop(0, ROWS // PBLK)
        def _(block):
            base = pl.multiple_of(block * PBLK, PBLK)
            keys = cache[0, pl.ds(base, PBLK), :]
            values = jnp.concatenate([cache[1, pl.ds(base, PBLK), :], jnp.ones((PBLK, 128), BF)], axis=1)
            across = (iota((1, PBLK), 1) + base).astype(F32)
            live = (across >= begin_ref[rows, 0:1]) & (across < end_ref[rows, 0:1])
            for head in range(2):
                own_rows = pl.ds(head * count, count)
                scores = lax.dot_general(q2[own_rows, :], keys, (((1,), (1,)), ((), ())), preferred_element_type=F32)
                scores = jnp.where(live, scores, LOW)
                old_top = top_ref[own_rows, 0:1]
                top = jnp.maximum(old_top, jnp.max(scores, axis=1, keepdims=True))
                weights = jnp.exp(scores - top).astype(BF)
                added = jnp.dot(weights, values, preferred_element_type=F32)
                out_ref[own_rows, :] = out_ref[own_rows, :] * jnp.exp(old_top - top) + added
                top_ref[own_rows, :] = jnp.broadcast_to(top, (count, 128))

        first_rows, second_rows = pl.ds(0, count), pl.ds(count, count)
        upper = jnp.where(low_lanes, out_ref[first_rows, 0:128], out_ref[second_rows, 0:128])
        lower = jnp.where(low_lanes, out_ref[first_rows, 128:256], out_ref[second_rows, 128:256])
        ret[:, 0:128] = (upper / lower).astype(BF)
        lse = [top_ref[r, :] + jnp.log(out_ref[r, 128:256]) for r in (first_rows, second_rows)]
        high = [value.astype(BF).astype(F32) for value in lse]
        low = [a - b for a, b in zip(lse, high)]
        lane = iota((count, 128), 1)
        tail = jnp.where(lane == 0, high[0], jnp.where(lane == 1, low[0], jnp.where(lane == 2, high[1], low[1])))
        ret[:, 128:256] = tail.astype(BF)

    attend(0, HOME, ret_home)
    drain_gather()
    for copy in sent:
        copy.wait_recv()
    attend(HOME, NDP * BLK, ret_away)
    back = exchange_dp(me, ret_away, landing, dp_send.at[1], dp_recv.at[1])

    @pl.loop(0, ROWS // PBLK)
    def _(block):
        base = pl.multiple_of(block * PBLK, PBLK)
        span = pl.ds(base, PBLK)
        position = (iota((PBLK, SLOTS), 0) + base).astype(F32)
        written = jnp.where(position == end_row[0:1, :], 1.0, 0.0)
        hit = jnp.max(written, axis=1, keepdims=True) > 0.5
        fresh = jnp.dot(written.astype(BF), compact[:, 128:384], preferred_element_type=F32)
        cache[0, span, :] = jnp.where(hit, fresh[:, 0:128], cache[0, span, :].astype(F32)).astype(BF)
        cache[1, span, :] = jnp.where(hit, fresh[:, 128:256], cache[1, span, :].astype(F32)).astype(BF)

    store = pltpu.make_async_copy(cache, cache_out, store_sem.at[0])
    store.start()
    slots[:HOME, :] = ret_home[...]
    loads[9].wait()
    for copy in back:
        copy.wait_recv()
    slots[HOME:, :] = landing[...]
    attended[...] = jnp.dot(scat[...], slots[:, 0:128], preferred_element_type=F32).astype(BF)

    def out_product(half, core, target):
        rows = pl.ds(pl.multiple_of(core * 128, 128), 128)
        value = jnp.dot(attended[rows, :], wo[:, half * HALF : (half + 1) * HALF], preferred_element_type=F32)
        target[half] = value.astype(target.dtype)

    total, drain_first = reduce_scatter_z(
        me, out_product, sib_out.at[0], sib_in.at[0], own, ring_out.at[0], ring_in.at[0],
        rs_ring_send.at[0], rs_ring_recv.at[0], rs_sib_send.at[0], rs_sib_recv.at[0],
    )
    resid = (tokens[...].astype(F32) + jnp.concatenate(total, axis=1)).astype(BF)
    resid_keep[...] = resid
    loads[10].wait()
    normed = scaled_norm(resid.astype(F32), gain_row(mlp_gain))
    row_of_core = lambda zz, cc: cc * 128 + zz * BLK
    my_rows = pl.ds(pl.multiple_of(row_of_core(me.z, me.c), BLK), BLK)
    for half in range(2):
        gathered[1, half, my_rows, :] = normed[:, half * HALF : (half + 1) * HALF]
    begin, finish_mlp, drain_mlp = all_gather_z(
        me, gathered.at[1], row_of_core, ag_ring_send.at[1], ag_ring_recv.at[1], ag_sib_send.at[1], ag_sib_recv.at[1]
    )
    begin()
    spread_sel = sel[...].astype(F32)
    tail = slots[:, 128:256].astype(F32)
    for head in range(2):
        lse = tail[:, 2 * head : 2 * head + 1] + tail[:, 2 * head + 1 : 2 * head + 2]
        lse_out[head : head + 1, :] = jnp.sum(spread_sel * lse, axis=0, keepdims=True)
    drain_first()
    for copy in sent + back:
        copy.wait_send()
    loads[11].wait()
    loads[12].wait()
    finish_mlp()
    for tile in range(FFL // 256):
        columns = pl.ds(tile * 256, 256)
        both = []
        for m in range(2):
            value = jnp.dot(gathered[1, 0], gu[m, :HALF, columns], preferred_element_type=F32)
            both.append(value + jnp.dot(gathered[1, 1], gu[m, HALF:, columns], preferred_element_type=F32))
        inner[:, columns] = (both[0] / (1.0 + jnp.exp(-both[0])) * both[1]).astype(BF)

    def down_product(half, core, target):
        rows = pl.ds(pl.multiple_of(core * 128, 128), 128)
        value = jnp.dot(inner[rows, :], wd[:, half * HALF : (half + 1) * HALF], preferred_element_type=F32)
        target[half] = value.astype(target.dtype)

    total, drain_last = reduce_scatter_z(
        me, down_product, sib_out.at[1], sib_in.at[1], own, ring_out.at[1], ring_in.at[1],
        rs_ring_send.at[1], rs_ring_recv.at[1], rs_sib_send.at[1], rs_sib_recv.at[1],
    )
    hidden_out[...] = (resid_keep[...].astype(F32) + jnp.concatenate(total, axis=1)).astype(BF)
    drain_mlp()
    drain_last()
    store.wait()


VMEM_SPEC = pl.BlockSpec(memory_space=pltpu.VMEM)
ANY_SPEC = pl.BlockSpec(memory_space=pl.ANY)
DMA = pltpu.SemaphoreType.DMA


def on_device(tokens, attn_gain, mlp_gain, project_in, project_out, gate_up, project_down, kv_cache, lengths, owners, cache_start):
    shape = jax.ShapeDtypeStruct
    hidden_states, lse, kv_updated = pl.pallas_call(
        layer_kernel,
        out_shape=(shape((BLK, D), BF), shape((2, REQ), F32), shape((2, ROWS, 128), BF)),
        in_specs=[ANY_SPEC] * 11,
        out_specs=(VMEM_SPEC, VMEM_SPEC, ANY_SPEC),
        scratch_shapes=[
            pltpu.VMEM((BLK, D), BF), pltpu.VMEM((16, 128), BF), pltpu.VMEM((16, 128), BF), pltpu.VMEM((3, 32, 128), I32),
            pltpu.VMEM((D, 384), BF), pltpu.VMEM((128, D), BF), pltpu.VMEM((2, D, FFL), BF), pltpu.VMEM((FFL, D), BF),
            pltpu.VMEM((2, ROWS, 128), BF),
            pltpu.VMEM((2, 2, REQ, HALF), BF), pltpu.VMEM((REQ, 384), BF), pltpu.VMEM((SLOTS, 384), BF),
            pltpu.VMEM((NDP * BLK, 384), BF), pltpu.VMEM((SLOTS, REQ), BF), pltpu.VMEM((REQ, SLOTS), BF),
            pltpu.VMEM((SLOTS, 128), F32), pltpu.VMEM((SLOTS, 128), F32), pltpu.VMEM((8, SLOTS), F32),
            pltpu.VMEM((512, 128), BF), pltpu.VMEM((512, 128), F32), pltpu.VMEM((512, 256), F32),
            pltpu.VMEM((HOME, 256), BF), pltpu.VMEM((NDP * BLK, 256), BF), pltpu.VMEM((NDP * BLK, 256), BF),
            pltpu.VMEM((SLOTS, 256), BF), pltpu.VMEM((REQ, 128), BF), pltpu.VMEM((REQ, FFL), BF), pltpu.VMEM((BLK, D), BF),
            pltpu.VMEM((2, 2, 128, HALF), BF), pltpu.VMEM((2, 2, 128, HALF), BF), pltpu.VMEM((2, 128, HALF), F32),
            pltpu.VMEM((2, 2, 7, BLK, HALF), BF), pltpu.VMEM((2, 2, 7, BLK, HALF), BF),
            DMA((2, 15)), DMA((2, 15)), DMA((2, 2, 7)), DMA((2, 2, 7)), DMA((2, 16)), DMA((2, 16)),
            DMA((2, 2, 7)), DMA((2, 2, 7)), DMA((2, 2)), DMA((2, 2)), DMA((13,)), DMA((1,)),
        ],
        compiler_params=pltpu.CompilerParams(collective_id=0, has_side_effects=True, vmem_limit_bytes=56 << 20),
        name="decode_layer",
    )(
        tokens, attn_gain.reshape(16, 128), mlp_gain.reshape(16, 128), lengths.reshape(32, 128), owners.reshape(32, 128),
        cache_start.reshape(32, 128), project_in, project_out, gate_up, project_down, kv_cache,
    )
    return hidden_states, lse.T, kv_updated


def solution(mesh):
    placed = (
        P(("dp", "tensor"), None),
        P(),
        P(),
        P(None, None, "tensor"),
        P("tensor", None),
        P(None, None, "tensor"),
        P("tensor", None),
        P(None, "dp", "tensor"),
        P(),
        P(),
        P(),
    )
    return jax.shard_map(
        on_device,
        mesh=mesh,
        in_specs=placed,
        out_specs=(P(("dp", "tensor"), None), P("dp", "tensor"), P(None, "dp", "tensor")),
        check_vma=False,
    )
```

```python
import functools

import jax
import jax.numpy as jnp
import numpy as np
from jax import lax
from jax.experimental import pallas as pl
from jax.experimental.pallas import tpu as pltpu
from jax.sharding import PartitionSpec as P

MESH = pl.DeviceIdType.MESH
BF = jnp.bfloat16
F32 = jnp.float32
I32 = jnp.int32

EPS = 1e-05
ROPE_BASE = 130000.0
LOW = -1e30
HD = 64
NDP = 16
NTP = 16
NZ = 8
D = 2048
HALF = 1024
BLK = 16
REQ = 256
HOME = 128
SLOTS = HOME + NDP * BLK
ROWS = 4096
FFL = 512
PBLK = 1024


class Place:
    def __init__(self):
        self.d = lax.axis_index("dp")
        self.t = lax.axis_index("tensor")
        self.z = self.t // 2
        self.c = self.t % 2
        self.sib = (self.d, self.t + 1 - 2 * self.c)

    def along_z(self, offset):
        return (self.d, ((self.z + NZ + offset) % NZ) * 2 + self.c)

    def dp_peer(self, offset):
        return (self.d + offset) % NDP


def greet(me):
    barrier = pltpu.get_barrier_semaphore()
    targets = [me.along_z(k) for k in (1, -1, 2, -2)] + [me.sib]
    targets += [(me.dp_peer(i), me.t) for i in range(1, NDP)]
    for target in targets:
        pl.semaphore_signal(barrier, inc=1, device_id=target, device_id_type=MESH)
    return lambda: pl.semaphore_wait(barrier, len(targets))


def iota(shape, axis):
    return lax.broadcasted_iota(I32, shape, axis)


def scaled_norm(wide, gain):
    factor = lax.rsqrt(jnp.mean(wide * wide, axis=-1, keepdims=True) + EPS)
    return (wide * factor * gain).astype(BF)


def gather_z(me, buf, row_of, send, recv, sib_send=None, sib_recv=None):
    signs = (1, -1)
    started = []
    sib_copies = []
    kinds = lambda way: ((2, 0, 2), (2, 1, 2), (1, 0, 1), (1, 1, 1), (3, 0, 1), (3, 1, 1), (4, way, 2))

    def block(origin, half):
        return buf.at[half, pl.ds(pl.multiple_of(row_of(origin, me.c), BLK), BLK), :]

    def message(way, index):
        distance, half, hops = kinds(way)[index]
        ref = block((me.z + NZ - signs[way] * (distance - hops)) % NZ, half)
        return pltpu.make_async_remote_copy(
            src_ref=ref, dst_ref=ref, send_sem=send.at[way, index], recv_sem=recv.at[way, index],
            device_id=me.along_z(signs[way] * hops), device_id_type=MESH,
        )

    def start(way, index):
        copy = message(way, index)
        copy.start()
        started.append(copy)

    def sibling(origin, half):
        if sib_send is None:
            return
        index = len(sib_copies)
        ref = block(origin, half)
        copy = pltpu.make_async_remote_copy(
            src_ref=ref, dst_ref=ref, send_sem=sib_send.at[index], recv_sem=sib_recv.at[index],
            device_id=me.sib, device_id_type=MESH,
        )
        copy.start()
        sib_copies.append(copy)

    def begin():
        for index in range(4):
            for way in range(2):
                start(way, index ^ way if index < 2 else index)
        for half in range(2):
            sibling(me.z, half)

    def arrive(way, index):
        message(way, index).wait_recv()
        distance, half, _ = kinds(way)[index]
        if distance == 2:
            if half == way:
                start(way, 6)
            start(way, 4 + half)
        sibling((me.z + NZ - signs[way] * distance) % NZ, half)

    def finish():
        for index in (0, 1, 2, 3, 4, 5, 6):
            for way in range(2):
                arrive(way, index if index in (2, 3, 6) else index ^ way)
        for copy in sib_copies:
            copy.wait_recv()

    def drain():
        for copy in started + sib_copies:
            copy.wait_send()

    return begin, finish, drain


def reduce_z(me, product, own, out, landed, send, recv):
    signs = (1, -1)
    hops = (1, 1, 2, 2, 2, 1, 1)
    started = []

    def message(way, index):
        return pltpu.make_async_remote_copy(
            src_ref=out.at[way, index], dst_ref=landed.at[way, index],
            send_sem=send.at[way, index], recv_sem=recv.at[way, index],
            device_id=me.along_z(signs[way] * hops[index]), device_id_type=MESH,
        )

    def mine(offset, half):
        target = (me.z + NZ + offset) % NZ
        return own[half, pl.ds(pl.multiple_of(target * BLK, BLK), BLK), :]

    def go(way, index, value):
        out[way, index] = value.astype(BF)
        copy = message(way, index)
        copy.start()
        started.append(copy)

    def landed_sum(way, index):
        message(way, index).wait_recv()
        return landed[way, index].astype(F32)

    for half in range(2):
        own[half] = product(half)
        go(half, 2, mine(4 * signs[half], half))
        for way in range(2):
            go(way, half, mine(3 * signs[way], half))
    for half in range(2):
        for way in range(2):
            go(way, 5 + half, mine(signs[way], half))
    total = [mine(0, half) for half in range(2)]
    for half in range(2):
        for way in (1 - half, half):
            value = landed_sum(way, half) + mine(2 * signs[way], half)
            if half == way:
                value = value + landed_sum(way, 2)
            go(way, 3 + half, value)
    for base in (5, 3):
        for half in range(2):
            for way in range(2):
                total[half] = total[half] + landed_sum(way, base + half)
    return total, lambda: [copy.wait_send() for copy in started]


def exchange_dp(me, source, landing, send, recv):
    copies = []
    for i in range(1, NDP):
        peer = me.dp_peer(i)
        copy = pltpu.make_async_remote_copy(
            src_ref=source.at[pl.ds(pl.multiple_of(peer * BLK, BLK), BLK), :],
            dst_ref=landing.at[pl.ds(pl.multiple_of(me.d * BLK, BLK), BLK), :],
            send_sem=send.at[i - 1], recv_sem=recv.at[i - 1],
            device_id=(peer, me.t), device_id_type=MESH,
        )
        copy.start()
        copies.append(copy)
    here = pl.ds(pl.multiple_of(me.d * BLK, BLK), BLK)
    landing[here, :] = source[here, :]
    return copies


def column_of(row, hits):
    return jnp.sum(jnp.where(hits, row, 0.0), axis=1, keepdims=True)


def layer_kernel(
    tokens_hbm, attn_gain_hbm, mlp_gain_hbm, lengths_hbm, owners_hbm, starts_hbm, w_hbm, wo_hbm, gu_hbm, wd_hbm, cache_hbm,
    hidden_out, lse_out, cache_out,
    tokens, attn_gain, mlp_gain, ints, w, wo, gu, wd, cache,
    gathered, gathered_mlp, packed, compact, outgoing, sel, scat, begin_ref, end_ref, end_row,
    q2, top_ref, out_ref, ret_home, ret_away, landing, slots, attended, inner, resid_keep,
    own, ring_out, ring_in,
    dp_send, dp_recv, ag_send, ag_recv, ag_sib_send, ag_sib_recv, rs_send, rs_recv, core_send, core_recv, load_sem, store_sem,
):
    me = Place()
    pairs = [
        (tokens_hbm, tokens), (attn_gain_hbm, attn_gain), (owners_hbm, ints.at[0]), (lengths_hbm, ints.at[1]),
        (starts_hbm, ints.at[2]), (w_hbm.at[0], w.at[:, pl.ds(0, 128)]), (w_hbm.at[1], w.at[:, pl.ds(128, 128)]),
        (w_hbm.at[2], w.at[:, pl.ds(256, 128)]), (cache_hbm, cache), (wo_hbm, wo.at[0]), (mlp_gain_hbm, mlp_gain), (gu_hbm, gu.at[0]), (wd_hbm, wd.at[0]),
    ]
    loads = [pltpu.make_async_copy(src, dst, load_sem.at[i]) for i, (src, dst) in enumerate(pairs)]
    for copy in loads:
        copy.start()
    wait_all = greet(me)
    loads[0].wait()
    loads[1].wait()

    def gain_row(ref):
        return jnp.concatenate([ref[i : i + 1, :].astype(F32) for i in range(16)], axis=1)

    normed = scaled_norm(tokens[...].astype(F32), gain_row(attn_gain))
    row_of = lambda zz, cc: (zz * 2 + cc) * BLK
    my_rows = pl.ds(pl.multiple_of(row_of(me.z, me.c), BLK), BLK)
    for half in range(2):
        gathered[half, my_rows, :] = normed[:, half * HALF : (half + 1) * HALF]
    wait_all()
    begin, finish, drain_gather = gather_z(
        me, gathered, row_of, ag_send.at[0], ag_recv.at[0], ag_sib_send, ag_sib_recv
    )
    begin()

    for copy in loads[2:5]:
        copy.wait()

    def wide(m):
        return jnp.concatenate([ints[m, pl.ds(0, NDP, stride=2), :], ints[m, pl.ds(1, NDP, stride=2), :]], axis=1)

    def mine(m):
        return jnp.concatenate([ints[m, pl.ds(2 * me.d, 1), :], ints[m, pl.ds(2 * me.d + 1, 1), :]], axis=1)

    own_all, len_all, start_all = wide(0), wide(1), wide(2)
    own_row, len_row, start_row = mine(0), mine(1).astype(F32), mine(2).astype(F32)
    before = jnp.where(iota((REQ, REQ), 0) < iota((REQ, REQ), 1), 1.0, 0.0).astype(BF)
    here = own_all == me.d
    here_rank = jnp.dot(jnp.where(here, 1.0, 0.0).astype(BF), before, preferred_element_type=F32)
    away = here & (iota((NDP, REQ), 0) != me.d)
    place_in = jnp.where(away, here_rank, -1.0)
    onehot = jnp.where(iota((NDP, REQ), 0) == own_row, 1.0, 0.0)
    counts = jnp.dot(onehot.astype(BF), before, preferred_element_type=F32)
    rank = jnp.sum(onehot * counts, axis=0, keepdims=True)
    own_wide = own_row.astype(F32)
    place = jnp.where(own_row == me.d, rank, HOME + own_wide * BLK + rank)
    chosen = iota((SLOTS, REQ), 0).astype(F32) == place
    sel[...] = jnp.where(chosen, 1.0, 0.0).astype(BF)
    request = iota((REQ, REQ), 0)
    natural = ((request >> 4) & 7) * 32 + (request >> 7) * 16 + (request & 15)
    place_col = column_of(place, natural == iota((REQ, REQ), 1))
    scat[...] = jnp.where(iota((REQ, SLOTS), 1).astype(F32) == place_col, 1.0, 0.0).astype(BF)

    def spread(rows16):
        return jnp.concatenate(
            [jnp.broadcast_to(rows16[b : b + 1, :], (BLK, REQ)) for b in range(NDP)], axis=0
        )

    slot = (iota((NDP * BLK, REQ), 0) & (BLK - 1)).astype(F32)
    hits_in = spread(place_in) == slot
    begin_all = start_all.astype(F32)
    finish_all = begin_all + len_all.astype(F32)
    hits_home = chosen[:HOME]
    begin_col = jnp.concatenate(
        [column_of(start_row + 1.0, hits_home), column_of(spread(begin_all) + 1.0, hits_in)], axis=0
    ) - 1.0
    finish_col = jnp.concatenate(
        [column_of(start_row + len_row + 1.0, hits_home), column_of(spread(finish_all) + 1.0, hits_in)], axis=0
    ) - 1.0
    begin_ref[...] = jnp.broadcast_to(begin_col, (SLOTS, 128))
    end_ref[...] = jnp.broadcast_to(finish_col, (SLOTS, 128))
    eye = iota((SLOTS, SLOTS), 0) == iota((SLOTS, SLOTS), 1)
    end_row[...] = jnp.broadcast_to(jnp.sum(jnp.where(eye, finish_col, 0.0), axis=0, keepdims=True), (8, SLOTS))

    len_col = column_of(len_row, iota((REQ, REQ), 0) == iota((REQ, REQ), 1))
    lane = iota((1, 128), 1) & (HD // 2 - 1)
    freqs = jnp.exp(lane.astype(F32) * np.float32(-np.log(ROPE_BASE) / (HD // 2)))
    angle = len_col * freqs
    turns = jnp.floor(angle * (1.0 / (2.0 * np.pi)) + 0.5)
    left = (angle - turns * 6.28125) - turns * np.float32(2.0 * np.pi - 6.28125)
    x = 0.5 * left
    x2 = x * x
    sin_half = x * (1.0 + x2 * (-1 / 6 + x2 * (1 / 120 + x2 * (-1 / 5040 + x2 * (1 / 362880 - x2 / 39916800)))))
    cos_half = 1.0 + x2 * (
        -1 / 2 + x2 * (1 / 24 + x2 * (-1 / 720 + x2 * (1 / 40320 + x2 * (-1 / 3628800 + x2 / 479001600))))
    )
    sine = 2.0 * sin_half * cos_half
    cosine = 1.0 - 2.0 * sin_half * sin_half
    low_half = (iota((REQ, 128), 1) & (HD - 1)) < HD // 2
    signed = jnp.where(low_half, -sine, sine)

    finish()

    def to_core(src, dst, index):
        copy = pltpu.make_async_remote_copy(
            src_ref=src, dst_ref=dst, send_sem=core_send.at[index], recv_sem=core_recv.at[index],
            device_id=me.sib, device_id_type=MESH,
        )
        copy.start()
        return copy

    for copy in loads[5:8]:
        copy.wait()
    projected = jnp.dot(gathered[0], w[:HALF], preferred_element_type=F32)
    projected = projected + jnp.dot(gathered[1], w[HALF:], preferred_element_type=F32)

    def turned(values):
        partner = jnp.where(low_half, pltpu.roll(values, 96, 1), pltpu.roll(values, 32, 1))
        return (values * cosine + partner * signed).astype(BF)

    packed[:, 0:128] = turned(projected[:, 0:128])
    packed[:, 128:256] = turned(projected[:, 128:256])
    packed[:, 256:384] = projected[:, 256:384].astype(BF)
    outgoing[...] = jnp.dot(sel[HOME:, :], packed[...], preferred_element_type=F32).astype(BF)
    sent = exchange_dp(me, outgoing, compact.at[pl.ds(HOME, NDP * BLK), :], dp_send.at[0], dp_recv.at[0])
    compact[:HOME, :] = jnp.dot(sel[:HOME, :], packed[...], preferred_element_type=F32).astype(BF)
    shared = [to_core(wo_hbm, wo.at[1], 0), to_core(gu_hbm, gu.at[1], 1), to_core(wd_hbm, wd.at[1], 2)]
    loads[8].wait()

    def attend(first, count, ret):
        low_lanes = iota((count, 128), 1) < HD
        rows = pl.ds(first, count)
        q = compact[rows, 0:128].astype(F32) * (1.0 / 8.0)
        k = compact[rows, 128:256].astype(F32)
        v = compact[rows, 256:384].astype(F32)
        for head in range(2):
            keep = low_lanes if head == 0 else jnp.logical_not(low_lanes)
            qh = jnp.where(keep, q, 0.0)
            own_rows = pl.ds(head * count, count)
            q2[own_rows, :] = qh.astype(BF)
            top_ref[own_rows, :] = jnp.broadcast_to(jnp.sum(qh * k, axis=1, keepdims=True), (count, 128))
            out_ref[own_rows, 0:128] = v
            out_ref[own_rows, 128:256] = jnp.ones((count, 128), F32)

        @pl.loop(0, ROWS // PBLK)
        def _(block):
            base = pl.multiple_of(block * PBLK, PBLK)
            keys = cache[0, pl.ds(base, PBLK), :]
            values = jnp.concatenate([cache[1, pl.ds(base, PBLK), :], jnp.ones((PBLK, 128), BF)], axis=1)
            across = (iota((1, PBLK), 1) + base).astype(F32)
            live = (across >= begin_ref[rows, 0:1]) & (across < end_ref[rows, 0:1])
            for head in range(2):
                own_rows = pl.ds(head * count, count)
                scores = lax.dot_general(q2[own_rows, :], keys, (((1,), (1,)), ((), ())), preferred_element_type=F32)
                scores = jnp.where(live, scores, LOW)
                old_top = top_ref[own_rows, 0:1]
                top = jnp.maximum(old_top, jnp.max(scores, axis=1, keepdims=True))
                weights = jnp.exp(scores - top).astype(BF)
                added = jnp.dot(weights, values, preferred_element_type=F32)
                out_ref[own_rows, :] = out_ref[own_rows, :] * jnp.exp(old_top - top) + added
                top_ref[own_rows, :] = jnp.broadcast_to(top, (count, 128))

        first_rows, second_rows = pl.ds(0, count), pl.ds(count, count)
        upper = jnp.where(low_lanes, out_ref[first_rows, 0:128], out_ref[second_rows, 0:128])
        lower = jnp.where(low_lanes, out_ref[first_rows, 128:256], out_ref[second_rows, 128:256])
        ret[:, 0:128] = (upper / lower).astype(BF)
        lse = [top_ref[r, :] + jnp.log(out_ref[r, 128:256]) for r in (first_rows, second_rows)]
        high = [value.astype(BF).astype(F32) for value in lse]
        low = [a - b for a, b in zip(lse, high)]
        lane = iota((count, 128), 1)
        tail = jnp.where(lane == 0, high[0], jnp.where(lane == 1, low[0], jnp.where(lane == 2, high[1], low[1])))
        ret[:, 128:256] = tail.astype(BF)

    attend(0, HOME, ret_home)
    drain_gather()
    for copy in sent:
        copy.wait_recv()
    attend(HOME, NDP * BLK, ret_away)
    back = exchange_dp(me, ret_away, landing, dp_send.at[1], dp_recv.at[1])

    @pl.loop(0, ROWS // PBLK)
    def _(block):
        base = pl.multiple_of(block * PBLK, PBLK)
        span = pl.ds(base, PBLK)
        position = (iota((PBLK, SLOTS), 0) + base).astype(F32)
        written = jnp.where(position == end_row[0:1, :], 1.0, 0.0)
        hit = jnp.max(written, axis=1, keepdims=True) > 0.5
        fresh = jnp.dot(written.astype(BF), compact[:, 128:384], preferred_element_type=F32)
        cache[0, span, :] = jnp.where(hit, fresh[:, 0:128], cache[0, span, :].astype(F32)).astype(BF)
        cache[1, span, :] = jnp.where(hit, fresh[:, 128:256], cache[1, span, :].astype(F32)).astype(BF)

    store = pltpu.make_async_copy(cache, cache_out, store_sem.at[0])
    store.start()
    slots[:HOME, :] = ret_home[...]
    loads[9].wait()
    for copy in back:
        copy.wait_recv()
    slots[HOME:, :] = landing[...]

    def assemble(core):
        rows = pl.ds(pl.multiple_of(core * 128, 128), 128)
        return jnp.dot(scat[rows, :], slots[:, 0:128], preferred_element_type=F32).astype(BF)

    attended[2] = assemble(1 - me.c)
    swapped = to_core(attended.at[2], attended.at[1], 3)
    attended[0] = assemble(me.c)
    shared[0].wait_recv()
    swapped.wait_recv()

    def out_product(half):
        columns = pl.ds(half * HALF, HALF)
        value = jnp.dot(attended[0], wo[0, :, columns], preferred_element_type=F32)
        return value + jnp.dot(attended[1], wo[1, :, columns], preferred_element_type=F32)

    total, drain_first = reduce_z(
        me, out_product, own.at[0], ring_out.at[0], ring_in.at[0], rs_send.at[0], rs_recv.at[0]
    )
    resid = (tokens[...].astype(F32) + jnp.concatenate(total, axis=1)).astype(BF)
    resid_keep[...] = resid
    loads[10].wait()
    normed = scaled_norm(resid.astype(F32), gain_row(mlp_gain))
    row_of_chip = lambda zz, cc: zz * BLK
    my_rows = pl.ds(pl.multiple_of(me.z * BLK, BLK), BLK)
    for half in range(2):
        gathered_mlp[half, my_rows, :] = normed[:, half * HALF : (half + 1) * HALF]
    begin, finish_mlp, drain_mlp = gather_z(me, gathered_mlp, row_of_chip, ag_send.at[1], ag_recv.at[1])
    begin()
    spread_sel = sel[...].astype(F32)
    tail = slots[:, 128:256].astype(F32)
    for head in range(2):
        lse = tail[:, 2 * head : 2 * head + 1] + tail[:, 2 * head + 1 : 2 * head + 2]
        lse_out[head : head + 1, :] = jnp.sum(spread_sel * lse, axis=0, keepdims=True)
    drain_first()
    for copy in sent + back:
        copy.wait_send()
    loads[11].wait()
    loads[12].wait()
    shared[1].wait_recv()
    shared[2].wait_recv()
    finish_mlp()
    for core in range(2):
        for tile in range(FFL // 256):
            columns = pl.ds(tile * 256, 256)
            both = []
            for m in range(2):
                value = jnp.dot(gathered_mlp[0], gu[core, m, :HALF, columns], preferred_element_type=F32)
                both.append(value + jnp.dot(gathered_mlp[1], gu[core, m, HALF:, columns], preferred_element_type=F32))
            inner[core, :, columns] = (both[0] / (1.0 + jnp.exp(-both[0])) * both[1]).astype(BF)

    def down_product(half):
        columns = pl.ds(half * HALF, HALF)
        value = jnp.dot(inner[0], wd[0, :, columns], preferred_element_type=F32)
        return value + jnp.dot(inner[1], wd[1, :, columns], preferred_element_type=F32)

    total, drain_last = reduce_z(
        me, down_product, own.at[1], ring_out.at[1], ring_in.at[1], rs_send.at[1], rs_recv.at[1]
    )
    hidden_out[...] = (resid_keep[...].astype(F32) + jnp.concatenate(total, axis=1)).astype(BF)
    drain_mlp()
    drain_last()
    for copy in shared:
        copy.wait_send()
    swapped.wait_send()
    store.wait()


def store_kernel(hidden, lse, cache, hidden_out, lse_out, cache_out, sems):
    pairs = [(hidden, hidden_out), (lse, lse_out)]
    for part in range(8):
        span = pl.ds(part % 4 * (ROWS // 4), ROWS // 4)
        pairs.append((cache.at[part // 4, span], cache_out.at[part // 4, span]))
    copies = [pltpu.make_async_copy(src, dst, sems.at[i]) for i, (src, dst) in enumerate(pairs)]
    for copy in copies:
        copy.start()
    for copy in copies:
        copy.wait()


VMEM_SPEC = pl.BlockSpec(memory_space=pltpu.VMEM)
ANY_SPEC = pl.BlockSpec(memory_space=pl.ANY)
DMA = pltpu.SemaphoreType.DMA


def on_device(tokens, attn_gain, mlp_gain, project_in, project_out, gate_up, project_down, kv_cache, lengths, owners, cache_start):
    shape = jax.ShapeDtypeStruct
    results = (shape((BLK, D), BF), shape((2, REQ), F32), shape((2, ROWS, 128), BF))
    held = pl.pallas_call(
        layer_kernel,
        out_shape=results,
        in_specs=[ANY_SPEC] * 11,
        out_specs=(VMEM_SPEC, VMEM_SPEC, ANY_SPEC),
        scratch_shapes=[
            pltpu.VMEM((BLK, D), BF), pltpu.VMEM((16, 128), BF), pltpu.VMEM((16, 128), BF), pltpu.VMEM((3, 32, 128), I32),
            pltpu.VMEM((D, 384), BF), pltpu.VMEM((2, 128, D), BF), pltpu.VMEM((2, 2, D, FFL), BF), pltpu.VMEM((2, FFL, D), BF),
            pltpu.VMEM((2, ROWS, 128), BF),
            pltpu.VMEM((2, REQ, HALF), BF), pltpu.VMEM((2, 128, HALF), BF), pltpu.VMEM((REQ, 384), BF), pltpu.VMEM((SLOTS, 384), BF),
            pltpu.VMEM((NDP * BLK, 384), BF), pltpu.VMEM((SLOTS, REQ), BF), pltpu.VMEM((REQ, SLOTS), BF),
            pltpu.VMEM((SLOTS, 128), F32), pltpu.VMEM((SLOTS, 128), F32), pltpu.VMEM((8, SLOTS), F32),
            pltpu.VMEM((512, 128), BF), pltpu.VMEM((512, 128), F32), pltpu.VMEM((512, 256), F32),
            pltpu.VMEM((HOME, 256), BF), pltpu.VMEM((NDP * BLK, 256), BF), pltpu.VMEM((NDP * BLK, 256), BF),
            pltpu.VMEM((SLOTS, 256), BF), pltpu.VMEM((3, 128, 128), BF), pltpu.VMEM((2, 128, FFL), BF), pltpu.VMEM((BLK, D), BF),
            pltpu.VMEM((2, 2, 128, HALF), F32), pltpu.VMEM((2, 2, 7, BLK, HALF), BF), pltpu.VMEM((2, 2, 7, BLK, HALF), BF),
            DMA((2, 15)), DMA((2, 15)), DMA((2, 2, 7)), DMA((2, 2, 7)), DMA((16,)), DMA((16,)),
            DMA((2, 2, 7)), DMA((2, 2, 7)), DMA((4,)), DMA((4,)), DMA((13,)), DMA((1,)),
        ],
        compiler_params=pltpu.CompilerParams(collective_id=0, has_side_effects=True, vmem_limit_bytes=54 << 20),
        name="decode_layer",
    )(
        tokens, attn_gain.reshape(16, 128), mlp_gain.reshape(16, 128), lengths.reshape(32, 128), owners.reshape(32, 128),
        cache_start.reshape(32, 128), project_in, project_out, gate_up, project_down, kv_cache,
    )
    hidden_states, lse, kv_updated = pl.pallas_call(
        store_kernel,
        out_shape=results,
        in_specs=[ANY_SPEC] * 3,
        out_specs=(ANY_SPEC,) * 3,
        scratch_shapes=[DMA((10,))],
        name="store_results",
    )(*held)
    return hidden_states, lse.T, kv_updated


def solution(mesh):
    placed = (
        P(("dp", "tensor"), None),
        P(),
        P(),
        P(None, None, "tensor"),
        P("tensor", None),
        P(None, None, "tensor"),
        P("tensor", None),
        P(None, "dp", "tensor"),
        P(),
        P(),
        P(),
    )
    return jax.shard_map(
        on_device,
        mesh=mesh,
        in_specs=placed,
        out_specs=(P(("dp", "tensor"), None), P("dp", "tensor"), P(None, "dp", "tensor")),
        check_vma=False,
    )
```

```python
import functools

import jax
import jax.numpy as jnp
import numpy as np
from jax import lax
from jax.experimental import pallas as pl
from jax.experimental.pallas import tpu as pltpu
from jax.sharding import PartitionSpec as P

MESH = pl.DeviceIdType.MESH
BF = jnp.bfloat16
F32 = jnp.float32
I32 = jnp.int32

EPS = 1e-05
ROPE_BASE = 130000.0
LOW = -1e30
HD = 64
NDP = 16
NTP = 16
NZ = 8
D = 2048
HALF = 1024
BLK = 16
REQ = 256
HOME = 128
SLOTS = HOME + NDP * BLK
ROWS = 4096
FFL = 512
PBLK = 1024


FAR_FIRST = sorted(
    [(dx, dy) for dx in range(4) for dy in range(4) if (dx, dy) != (0, 0)],
    key=lambda at: -(min(at[0], 4 - at[0]) + min(at[1], 4 - at[1])),
)


class Place:
    def __init__(self):
        self.d = lax.axis_index("dp")
        self.t = lax.axis_index("tensor")
        self.z = self.t // 2
        self.c = self.t % 2
        self.sib = (self.d, self.t + 1 - 2 * self.c)

    def along_z(self, offset):
        return (self.d, ((self.z + NZ + offset) % NZ) * 2 + self.c)

    def dp_peer(self, dx, dy):
        return ((self.d // 4 + dx) % 4) * 4 + (self.d % 4 + dy) % 4


def greet(me):
    barrier = pltpu.get_barrier_semaphore()
    targets = [me.along_z(k) for k in (1, -1, 2, -2)] + [me.sib]
    targets += [(me.dp_peer(dx, dy), me.t) for dx, dy in FAR_FIRST]
    for target in targets:
        pl.semaphore_signal(barrier, inc=1, device_id=target, device_id_type=MESH)
    return lambda: pl.semaphore_wait(barrier, len(targets))


def iota(shape, axis):
    return lax.broadcasted_iota(I32, shape, axis)


def scaled_norm(wide, gain):
    factor = lax.rsqrt(jnp.mean(wide * wide, axis=-1, keepdims=True) + EPS)
    return (wide * factor * gain).astype(BF)


def gather_z(me, buf, row_of, send, recv, sib_send=None, sib_recv=None):
    signs = (1, -1)
    started = []
    sib_copies = []
    kinds = lambda way: ((2, 0, 2), (2, 1, 2), (1, 0, 1), (1, 1, 1), (3, 0, 1), (3, 1, 1), (4, way, 2))

    def block(origin, half):
        return buf.at[half, pl.ds(pl.multiple_of(row_of(origin, me.c), BLK), BLK), :]

    def message(way, index):
        distance, half, hops = kinds(way)[index]
        ref = block((me.z + NZ - signs[way] * (distance - hops)) % NZ, half)
        return pltpu.make_async_remote_copy(
            src_ref=ref, dst_ref=ref, send_sem=send.at[way, index], recv_sem=recv.at[way, index],
            device_id=me.along_z(signs[way] * hops), device_id_type=MESH,
        )

    def start(way, index):
        copy = message(way, index)
        copy.start()
        started.append(copy)

    def sibling(origin, half):
        if sib_send is None:
            return
        index = len(sib_copies)
        ref = block(origin, half)
        copy = pltpu.make_async_remote_copy(
            src_ref=ref, dst_ref=ref, send_sem=sib_send.at[index], recv_sem=sib_recv.at[index],
            device_id=me.sib, device_id_type=MESH,
        )
        copy.start()
        sib_copies.append(copy)

    def begin():
        for index in range(4):
            for way in range(2):
                start(way, index ^ way if index < 2 else index)
        for half in range(2):
            sibling(me.z, half)

    def arrive(way, index):
        message(way, index).wait_recv()
        distance, half, _ = kinds(way)[index]
        if distance == 2:
            if half == way:
                start(way, 6)
            start(way, 4 + half)
        sibling((me.z + NZ - signs[way] * distance) % NZ, half)

    def finish():
        for index in (0, 1, 2, 3, 4, 5, 6):
            for way in range(2):
                arrive(way, index if index in (2, 3, 6) else index ^ way)
        for copy in sib_copies:
            copy.wait_recv()

    def drain():
        for copy in started + sib_copies:
            copy.wait_send()

    return begin, finish, drain


def reduce_z(me, product, own, out, landed, send, recv):
    signs = (1, -1)
    hops = (1, 1, 2, 2, 2, 1, 1)
    started = []

    def message(way, index):
        return pltpu.make_async_remote_copy(
            src_ref=out.at[way, index], dst_ref=landed.at[way, index],
            send_sem=send.at[way, index], recv_sem=recv.at[way, index],
            device_id=me.along_z(signs[way] * hops[index]), device_id_type=MESH,
        )

    def mine(offset, half):
        target = (me.z + NZ + offset) % NZ
        return own[half, pl.ds(pl.multiple_of(target * BLK, BLK), BLK), :]

    def go(way, index, value):
        out[way, index] = value.astype(BF)
        copy = message(way, index)
        copy.start()
        started.append(copy)

    def landed_sum(way, index):
        message(way, index).wait_recv()
        return landed[way, index].astype(F32)

    for half in range(2):
        own[half] = product(half)
        go(half, 2, mine(4 * signs[half], half))
        for way in range(2):
            go(way, half, mine(3 * signs[way], half))
    for half in range(2):
        for way in range(2):
            go(way, 5 + half, mine(signs[way], half))
    total = [mine(0, half) for half in range(2)]
    for half in range(2):
        for way in (1 - half, half):
            value = landed_sum(way, half) + mine(2 * signs[way], half)
            if half == way:
                value = value + landed_sum(way, 2)
            go(way, 3 + half, value)
    for base in (5, 3):
        for half in range(2):
            for way in range(2):
                total[half] = total[half] + landed_sum(way, base + half)
    return total, lambda: [copy.wait_send() for copy in started]


def exchange_dp(me, source, landing, send, recv):
    copies = []
    for i, (dx, dy) in enumerate(FAR_FIRST):
        peer = me.dp_peer(dx, dy)
        copy = pltpu.make_async_remote_copy(
            src_ref=source.at[pl.ds(pl.multiple_of(peer * BLK, BLK), BLK), :],
            dst_ref=landing.at[pl.ds(pl.multiple_of(me.d * BLK, BLK), BLK), :],
            send_sem=send.at[i], recv_sem=recv.at[i],
            device_id=(peer, me.t), device_id_type=MESH,
        )
        copy.start()
        copies.append(copy)
    here = pl.ds(pl.multiple_of(me.d * BLK, BLK), BLK)
    landing[here, :] = source[here, :]
    return copies


def column_of(row, hits):
    return jnp.sum(jnp.where(hits, row, 0.0), axis=1, keepdims=True)


def layer_kernel(
    tokens_hbm, attn_gain_hbm, mlp_gain_hbm, lengths_hbm, owners_hbm, starts_hbm, w_hbm, wo_hbm, gu_hbm, wd_hbm, cache_hbm,
    hidden_out, lse_out, cache,
    tokens, attn_gain, mlp_gain, ints, w, wo, gu, wd,
    gathered, gathered_mlp, packed, compact, outgoing, sel, scat, begin_ref, end_ref, end_row,
    q2, top_ref, out_ref, ret_home, ret_away, landing, slots, attended, inner, resid_keep,
    own, ring_out, ring_in,
    dp_send, dp_recv, ag_send, ag_recv, ag_sib_send, ag_sib_recv, rs_send, rs_recv, core_send, core_recv, load_sem,
):
    me = Place()
    pairs = [
        (tokens_hbm, tokens), (attn_gain_hbm, attn_gain), (owners_hbm, ints.at[0]), (lengths_hbm, ints.at[1]),
        (starts_hbm, ints.at[2]), (w_hbm.at[0], w.at[:, pl.ds(0, 128)]), (w_hbm.at[1], w.at[:, pl.ds(128, 128)]),
        (w_hbm.at[2], w.at[:, pl.ds(256, 128)]), (cache_hbm, cache), (wo_hbm, wo.at[0]), (mlp_gain_hbm, mlp_gain), (gu_hbm, gu.at[0]), (wd_hbm, wd.at[0]),
    ]
    loads = [pltpu.make_async_copy(src, dst, load_sem.at[i]) for i, (src, dst) in enumerate(pairs)]
    for copy in loads:
        copy.start()
    wait_all = greet(me)
    loads[0].wait()
    loads[1].wait()

    def gain_row(ref):
        return jnp.concatenate([ref[i : i + 1, :].astype(F32) for i in range(16)], axis=1)

    normed = scaled_norm(tokens[...].astype(F32), gain_row(attn_gain))
    row_of = lambda zz, cc: (zz * 2 + cc) * BLK
    my_rows = pl.ds(pl.multiple_of(row_of(me.z, me.c), BLK), BLK)
    for half in range(2):
        gathered[half, my_rows, :] = normed[:, half * HALF : (half + 1) * HALF]
    wait_all()
    begin, finish, drain_gather = gather_z(
        me, gathered, row_of, ag_send.at[0], ag_recv.at[0], ag_sib_send, ag_sib_recv
    )
    begin()

    for copy in loads[2:5]:
        copy.wait()

    def wide(m):
        return jnp.concatenate([ints[m, pl.ds(0, NDP, stride=2), :], ints[m, pl.ds(1, NDP, stride=2), :]], axis=1)

    def mine(m):
        return jnp.concatenate([ints[m, pl.ds(2 * me.d, 1), :], ints[m, pl.ds(2 * me.d + 1, 1), :]], axis=1)

    own_all, len_all, start_all = wide(0), wide(1), wide(2)
    own_row, len_row, start_row = mine(0), mine(1).astype(F32), mine(2).astype(F32)
    before = jnp.where(iota((REQ, REQ), 0) < iota((REQ, REQ), 1), 1.0, 0.0).astype(BF)
    here = own_all == me.d
    here_rank = jnp.dot(jnp.where(here, 1.0, 0.0).astype(BF), before, preferred_element_type=F32)
    away = here & (iota((NDP, REQ), 0) != me.d)
    place_in = jnp.where(away, here_rank, -1.0)
    onehot = jnp.where(iota((NDP, REQ), 0) == own_row, 1.0, 0.0)
    counts = jnp.dot(onehot.astype(BF), before, preferred_element_type=F32)
    rank = jnp.sum(onehot * counts, axis=0, keepdims=True)
    own_wide = own_row.astype(F32)
    place = jnp.where(own_row == me.d, rank, HOME + own_wide * BLK + rank)
    chosen = iota((SLOTS, REQ), 0).astype(F32) == place
    sel[...] = jnp.where(chosen, 1.0, 0.0).astype(BF)
    request = iota((REQ, REQ), 0)
    natural = ((request >> 4) & 7) * 32 + (request >> 7) * 16 + (request & 15)
    place_col = column_of(place, natural == iota((REQ, REQ), 1))
    scat[...] = jnp.where(iota((REQ, SLOTS), 1).astype(F32) == place_col, 1.0, 0.0).astype(BF)

    def spread(rows16):
        return jnp.concatenate(
            [jnp.broadcast_to(rows16[b : b + 1, :], (BLK, REQ)) for b in range(NDP)], axis=0
        )

    slot = (iota((NDP * BLK, REQ), 0) & (BLK - 1)).astype(F32)
    hits_in = spread(place_in) == slot
    begin_all = start_all.astype(F32)
    finish_all = begin_all + len_all.astype(F32)
    hits_home = chosen[:HOME]
    begin_col = jnp.concatenate(
        [column_of(start_row + 1.0, hits_home), column_of(spread(begin_all) + 1.0, hits_in)], axis=0
    ) - 1.0
    finish_col = jnp.concatenate(
        [column_of(start_row + len_row + 1.0, hits_home), column_of(spread(finish_all) + 1.0, hits_in)], axis=0
    ) - 1.0
    begin_ref[...] = jnp.broadcast_to(begin_col, (SLOTS, 128))
    end_ref[...] = jnp.broadcast_to(finish_col, (SLOTS, 128))
    eye = iota((SLOTS, SLOTS), 0) == iota((SLOTS, SLOTS), 1)
    end_row[...] = jnp.broadcast_to(jnp.sum(jnp.where(eye, finish_col, 0.0), axis=0, keepdims=True), (8, SLOTS))

    len_col = column_of(len_row, iota((REQ, REQ), 0) == iota((REQ, REQ), 1))
    lane = iota((1, 128), 1) & (HD // 2 - 1)
    freqs = jnp.exp(lane.astype(F32) * np.float32(-np.log(ROPE_BASE) / (HD // 2)))
    angle = len_col * freqs
    turns = jnp.floor(angle * (1.0 / (2.0 * np.pi)) + 0.5)
    left = (angle - turns * 6.28125) - turns * np.float32(2.0 * np.pi - 6.28125)
    x = 0.5 * left
    x2 = x * x
    sin_half = x * (1.0 + x2 * (-1 / 6 + x2 * (1 / 120 + x2 * (-1 / 5040 + x2 * (1 / 362880 - x2 / 39916800)))))
    cos_half = 1.0 + x2 * (
        -1 / 2 + x2 * (1 / 24 + x2 * (-1 / 720 + x2 * (1 / 40320 + x2 * (-1 / 3628800 + x2 / 479001600))))
    )
    sine = 2.0 * sin_half * cos_half
    cosine = 1.0 - 2.0 * sin_half * sin_half
    low_half = (iota((REQ, 128), 1) & (HD - 1)) < HD // 2
    signed = jnp.where(low_half, -sine, sine)

    finish()

    def to_core(src, dst, index):
        copy = pltpu.make_async_remote_copy(
            src_ref=src, dst_ref=dst, send_sem=core_send.at[index], recv_sem=core_recv.at[index],
            device_id=me.sib, device_id_type=MESH,
        )
        copy.start()
        return copy

    for copy in loads[5:8]:
        copy.wait()
    projected = jnp.dot(gathered[0], w[:HALF], preferred_element_type=F32)
    projected = projected + jnp.dot(gathered[1], w[HALF:], preferred_element_type=F32)

    def turned(values):
        partner = jnp.where(low_half, pltpu.roll(values, 96, 1), pltpu.roll(values, 32, 1))
        return (values * cosine + partner * signed).astype(BF)

    packed[:, 0:128] = turned(projected[:, 0:128])
    packed[:, 128:256] = turned(projected[:, 128:256])
    packed[:, 256:384] = projected[:, 256:384].astype(BF)
    outgoing[...] = jnp.dot(sel[HOME:, :], packed[...], preferred_element_type=F32).astype(BF)
    sent = exchange_dp(me, outgoing, compact.at[pl.ds(HOME, NDP * BLK), :], dp_send.at[0], dp_recv.at[0])
    compact[:HOME, :] = jnp.dot(sel[:HOME, :], packed[...], preferred_element_type=F32).astype(BF)
    loads[8].wait()

    def attend(first, count, ret):
        low_lanes = iota((count, 128), 1) < HD
        rows = pl.ds(first, count)
        q = compact[rows, 0:128].astype(F32) * (1.0 / 8.0)
        k = compact[rows, 128:256].astype(F32)
        v = compact[rows, 256:384].astype(F32)
        for head in range(2):
            keep = low_lanes if head == 0 else jnp.logical_not(low_lanes)
            qh = jnp.where(keep, q, 0.0)
            own_rows = pl.ds(head * count, count)
            q2[own_rows, :] = qh.astype(BF)
            top_ref[own_rows, :] = jnp.broadcast_to(jnp.sum(qh * k, axis=1, keepdims=True), (count, 128))
            out_ref[own_rows, 0:128] = v
            out_ref[own_rows, 128:256] = jnp.ones((count, 128), F32)

        @pl.loop(0, ROWS // PBLK)
        def _(block):
            base = pl.multiple_of(block * PBLK, PBLK)
            keys = cache[0, pl.ds(base, PBLK), :]
            values = jnp.concatenate([cache[1, pl.ds(base, PBLK), :], jnp.ones((PBLK, 128), BF)], axis=1)
            across = (iota((1, PBLK), 1) + base).astype(F32)
            live = (across >= begin_ref[rows, 0:1]) & (across < end_ref[rows, 0:1])
            for head in range(2):
                own_rows = pl.ds(head * count, count)
                scores = lax.dot_general(q2[own_rows, :], keys, (((1,), (1,)), ((), ())), preferred_element_type=F32)
                scores = jnp.where(live, scores, LOW)
                old_top = top_ref[own_rows, 0:1]
                top = jnp.maximum(old_top, jnp.max(scores, axis=1, keepdims=True))
                weights = jnp.exp(scores - top).astype(BF)
                added = jnp.dot(weights, values, preferred_element_type=F32)
                out_ref[own_rows, :] = out_ref[own_rows, :] * jnp.exp(old_top - top) + added
                top_ref[own_rows, :] = jnp.broadcast_to(top, (count, 128))

        first_rows, second_rows = pl.ds(0, count), pl.ds(count, count)
        upper = jnp.where(low_lanes, out_ref[first_rows, 0:128], out_ref[second_rows, 0:128])
        lower = jnp.where(low_lanes, out_ref[first_rows, 128:256], out_ref[second_rows, 128:256])
        ret[:, 0:128] = (upper / lower).astype(BF)
        lse = [top_ref[r, :] + jnp.log(out_ref[r, 128:256]) for r in (first_rows, second_rows)]
        high = [value.astype(BF).astype(F32) for value in lse]
        low = [a - b for a, b in zip(lse, high)]
        lane = iota((count, 128), 1)
        tail = jnp.where(lane == 0, high[0], jnp.where(lane == 1, low[0], jnp.where(lane == 2, high[1], low[1])))
        ret[:, 128:256] = tail.astype(BF)

    attend(0, HOME, ret_home)
    drain_gather()
    for copy in sent:
        copy.wait_recv()
    shared = [to_core(wo_hbm, wo.at[1], 0), to_core(gu_hbm, gu.at[1], 1), to_core(wd_hbm, wd.at[1], 2)]
    attend(HOME, NDP * BLK, ret_away)
    back = exchange_dp(me, ret_away, landing, dp_send.at[1], dp_recv.at[1])

    @pl.loop(0, ROWS // PBLK)
    def _(block):
        base = pl.multiple_of(block * PBLK, PBLK)
        span = pl.ds(base, PBLK)
        position = (iota((PBLK, SLOTS), 0) + base).astype(F32)
        written = jnp.where(position == end_row[0:1, :], 1.0, 0.0)
        hit = jnp.max(written, axis=1, keepdims=True) > 0.5
        fresh = jnp.dot(written.astype(BF), compact[:, 128:384], preferred_element_type=F32)
        cache[0, span, :] = jnp.where(hit, fresh[:, 0:128], cache[0, span, :].astype(F32)).astype(BF)
        cache[1, span, :] = jnp.where(hit, fresh[:, 128:256], cache[1, span, :].astype(F32)).astype(BF)

    slots[:HOME, :] = ret_home[...]
    loads[9].wait()
    for copy in back:
        copy.wait_recv()
    slots[HOME:, :] = landing[...]

    def assemble(core):
        rows = pl.ds(pl.multiple_of(core * 128, 128), 128)
        return jnp.dot(scat[rows, :], slots[:, 0:128], preferred_element_type=F32).astype(BF)

    attended[2] = assemble(1 - me.c)
    swapped = to_core(attended.at[2], attended.at[1], 3)
    attended[0] = assemble(me.c)
    shared[0].wait_recv()
    swapped.wait_recv()

    def out_product(half):
        columns = pl.ds(half * HALF, HALF)
        value = jnp.dot(attended[0], wo[0, :, columns], preferred_element_type=F32)
        return value + jnp.dot(attended[1], wo[1, :, columns], preferred_element_type=F32)

    total, drain_first = reduce_z(
        me, out_product, own.at[0], ring_out.at[0], ring_in.at[0], rs_send.at[0], rs_recv.at[0]
    )
    resid = (tokens[...].astype(F32) + jnp.concatenate(total, axis=1)).astype(BF)
    resid_keep[...] = resid
    loads[10].wait()
    normed = scaled_norm(resid.astype(F32), gain_row(mlp_gain))
    row_of_chip = lambda zz, cc: zz * BLK
    my_rows = pl.ds(pl.multiple_of(me.z * BLK, BLK), BLK)
    for half in range(2):
        gathered_mlp[half, my_rows, :] = normed[:, half * HALF : (half + 1) * HALF]
    begin, finish_mlp, drain_mlp = gather_z(me, gathered_mlp, row_of_chip, ag_send.at[1], ag_recv.at[1])
    begin()
    spread_sel = sel[...].astype(F32)
    tail = slots[:, 128:256].astype(F32)
    for head in range(2):
        lse = tail[:, 2 * head : 2 * head + 1] + tail[:, 2 * head + 1 : 2 * head + 2]
        lse_out[head : head + 1, :] = jnp.sum(spread_sel * lse, axis=0, keepdims=True)
    drain_first()
    for copy in sent + back:
        copy.wait_send()
    loads[11].wait()
    loads[12].wait()
    shared[1].wait_recv()
    shared[2].wait_recv()
    finish_mlp()
    for core in range(2):
        for tile in range(FFL // 256):
            columns = pl.ds(tile * 256, 256)
            both = []
            for m in range(2):
                value = jnp.dot(gathered_mlp[0], gu[core, m, :HALF, columns], preferred_element_type=F32)
                both.append(value + jnp.dot(gathered_mlp[1], gu[core, m, HALF:, columns], preferred_element_type=F32))
            inner[core, :, columns] = (both[0] / (1.0 + jnp.exp(-both[0])) * both[1]).astype(BF)

    def down_product(half):
        columns = pl.ds(half * HALF, HALF)
        value = jnp.dot(inner[0], wd[0, :, columns], preferred_element_type=F32)
        return value + jnp.dot(inner[1], wd[1, :, columns], preferred_element_type=F32)

    total, drain_last = reduce_z(
        me, down_product, own.at[1], ring_out.at[1], ring_in.at[1], rs_send.at[1], rs_recv.at[1]
    )
    hidden_out[...] = (resid_keep[...].astype(F32) + jnp.concatenate(total, axis=1)).astype(BF)
    drain_mlp()
    drain_last()
    for copy in shared:
        copy.wait_send()
    swapped.wait_send()


def store_kernel(hidden, lse, cache, hidden_out, lse_out, cache_out, sems):
    pairs = [(cache.at[0], cache_out.at[0]), (cache.at[1], cache_out.at[1]), (hidden, hidden_out), (lse, lse_out)]
    copies = [pltpu.make_async_copy(src, dst, sems.at[i]) for i, (src, dst) in enumerate(pairs)]
    for copy in copies:
        copy.start()
    for copy in copies:
        copy.wait()


VMEM_SPEC = pl.BlockSpec(memory_space=pltpu.VMEM)
ANY_SPEC = pl.BlockSpec(memory_space=pl.ANY)
DMA = pltpu.SemaphoreType.DMA


def on_device(tokens, attn_gain, mlp_gain, project_in, project_out, gate_up, project_down, kv_cache, lengths, owners, cache_start):
    shape = jax.ShapeDtypeStruct
    results = (shape((BLK, D), BF), shape((2, REQ), F32), shape((2, ROWS, 128), BF))
    held = pl.pallas_call(
        layer_kernel,
        out_shape=(pltpu.VMEM((BLK, D), BF), pltpu.VMEM((2, REQ), F32), pltpu.VMEM((2, ROWS, 128), BF)),
        in_specs=[ANY_SPEC] * 11,
        out_specs=(VMEM_SPEC,) * 3,
        scratch_shapes=[
            pltpu.VMEM((BLK, D), BF), pltpu.VMEM((16, 128), BF), pltpu.VMEM((16, 128), BF), pltpu.VMEM((3, 32, 128), I32),
            pltpu.VMEM((D, 384), BF), pltpu.VMEM((2, 128, D), BF), pltpu.VMEM((2, 2, D, FFL), BF), pltpu.VMEM((2, FFL, D), BF),
            pltpu.VMEM((2, REQ, HALF), BF), pltpu.VMEM((2, 128, HALF), BF), pltpu.VMEM((REQ, 384), BF), pltpu.VMEM((SLOTS, 384), BF),
            pltpu.VMEM((NDP * BLK, 384), BF), pltpu.VMEM((SLOTS, REQ), BF), pltpu.VMEM((REQ, SLOTS), BF),
            pltpu.VMEM((SLOTS, 128), F32), pltpu.VMEM((SLOTS, 128), F32), pltpu.VMEM((8, SLOTS), F32),
            pltpu.VMEM((512, 128), BF), pltpu.VMEM((512, 128), F32), pltpu.VMEM((512, 256), F32),
            pltpu.VMEM((HOME, 256), BF), pltpu.VMEM((NDP * BLK, 256), BF), pltpu.VMEM((NDP * BLK, 256), BF),
            pltpu.VMEM((SLOTS, 256), BF), pltpu.VMEM((3, 128, 128), BF), pltpu.VMEM((2, 128, FFL), BF), pltpu.VMEM((BLK, D), BF),
            pltpu.VMEM((2, 2, 128, HALF), F32), pltpu.VMEM((2, 2, 7, BLK, HALF), BF), pltpu.VMEM((2, 2, 7, BLK, HALF), BF),
            DMA((2, 15)), DMA((2, 15)), DMA((2, 2, 7)), DMA((2, 2, 7)), DMA((16,)), DMA((16,)),
            DMA((2, 2, 7)), DMA((2, 2, 7)), DMA((4,)), DMA((4,)), DMA((13,)),
        ],
        compiler_params=pltpu.CompilerParams(collective_id=0, has_side_effects=True, vmem_limit_bytes=54 << 20),
        name="decode_layer",
    )(
        tokens, attn_gain.reshape(16, 128), mlp_gain.reshape(16, 128), lengths.reshape(32, 128), owners.reshape(32, 128),
        cache_start.reshape(32, 128), project_in, project_out, gate_up, project_down, kv_cache,
    )
    hidden_states, lse, kv_updated = pl.pallas_call(
        store_kernel,
        out_shape=results,
        in_specs=[VMEM_SPEC] * 3,
        out_specs=(ANY_SPEC,) * 3,
        scratch_shapes=[DMA((4,))],
        name="store_results",
    )(*(pltpu.with_memory_space_constraint(value, pltpu.VMEM) for value in held))
    return hidden_states, lse.T, kv_updated


def solution(mesh):
    placed = (
        P(("dp", "tensor"), None),
        P(),
        P(),
        P(None, None, "tensor"),
        P("tensor", None),
        P(None, None, "tensor"),
        P("tensor", None),
        P(None, "dp", "tensor"),
        P(),
        P(),
        P(),
    )
    return jax.shard_map(
        on_device,
        mesh=mesh,
        in_specs=placed,
        out_specs=(P(("dp", "tensor"), None), P("dp", "tensor"), P(None, "dp", "tensor")),
        check_vma=False,
    )
```

```python
import functools

import jax
import jax.numpy as jnp
import numpy as np
from jax import lax
from jax.experimental import pallas as pl
from jax.experimental.pallas import tpu as pltpu
from jax.sharding import PartitionSpec as P

MESH = pl.DeviceIdType.MESH
BF = jnp.bfloat16
F32 = jnp.float32
I32 = jnp.int32

EPS = 1e-05
ROPE_BASE = 130000.0
LOW = -1e30
HD = 64
NDP = 16
NTP = 16
NZ = 8
D = 2048
HALF = 1024
BLK = 16
REQ = 256
HOME = 128
SLOTS = HOME + NDP * BLK
ROWS = 4096
FFL = 512
PBLK = 2048
SPAN = 512
CAP = 9
BATCH = 80


FAR_FIRST = sorted(
    [(dx, dy) for dx in range(4) for dy in range(4) if (dx, dy) != (0, 0)],
    key=lambda at: -(min(at[0], 4 - at[0]) + min(at[1], 4 - at[1])),
)


class Place:
    def __init__(self):
        self.d = lax.axis_index("dp")
        self.t = lax.axis_index("tensor")
        self.z = self.t // 2
        self.c = self.t % 2
        self.sib = (self.d, self.t + 1 - 2 * self.c)

    def along_z(self, offset):
        return (self.d, ((self.z + NZ + offset) % NZ) * 2 + self.c)

    def dp_peer(self, dx, dy):
        return ((self.d // 4 + dx) % 4) * 4 + (self.d % 4 + dy) % 4


def greet(me):
    barrier = pltpu.get_barrier_semaphore()
    targets = [me.along_z(k) for k in (1, -1, 2, -2)] + [me.sib]
    targets += [(me.dp_peer(dx, dy), me.t) for dx, dy in FAR_FIRST]
    for target in targets:
        pl.semaphore_signal(barrier, inc=1, device_id=target, device_id_type=MESH)
    return lambda: pl.semaphore_wait(barrier, len(targets))


def iota(shape, axis):
    return lax.broadcasted_iota(I32, shape, axis)


def scaled_norm(wide, gain):
    factor = lax.rsqrt(jnp.mean(wide * wide, axis=-1, keepdims=True) + EPS)
    return (wide * factor * gain).astype(BF)


def gather_z(me, buf, row_of, send, recv, sib_send=None, sib_recv=None):
    signs = (1, -1)
    started = []
    sib_copies = []
    kinds = lambda way: ((2, 0, 2), (2, 1, 2), (1, 0, 1), (1, 1, 1), (3, 0, 1), (3, 1, 1), (4, way, 2))

    def block(origin, half):
        return buf.at[half, pl.ds(pl.multiple_of(row_of(origin, me.c), BLK), BLK), :]

    def message(way, index):
        distance, half, hops = kinds(way)[index]
        ref = block((me.z + NZ - signs[way] * (distance - hops)) % NZ, half)
        return pltpu.make_async_remote_copy(
            src_ref=ref, dst_ref=ref, send_sem=send.at[way, index], recv_sem=recv.at[way, index],
            device_id=me.along_z(signs[way] * hops), device_id_type=MESH,
        )

    def start(way, index):
        copy = message(way, index)
        copy.start()
        started.append(copy)

    def sibling(origin, half):
        if sib_send is None:
            return
        index = len(sib_copies)
        ref = block(origin, half)
        copy = pltpu.make_async_remote_copy(
            src_ref=ref, dst_ref=ref, send_sem=sib_send.at[index], recv_sem=sib_recv.at[index],
            device_id=me.sib, device_id_type=MESH,
        )
        copy.start()
        sib_copies.append(copy)

    def begin():
        for index in range(4):
            for way in range(2):
                start(way, index ^ way if index < 2 else index)
        for half in range(2):
            sibling(me.z, half)

    def arrive(way, index):
        message(way, index).wait_recv()
        distance, half, _ = kinds(way)[index]
        if distance == 2:
            if half == way:
                start(way, 6)
            start(way, 4 + half)
        sibling((me.z + NZ - signs[way] * distance) % NZ, half)

    def finish():
        for index in (0, 1, 2, 3, 4, 5, 6):
            for way in range(2):
                arrive(way, index if index in (2, 3, 6) else index ^ way)
    def settle():
        for copy in sib_copies:
            copy.wait_recv()

    def drain():
        for copy in started + sib_copies:
            copy.wait_send()

    return begin, finish, settle, drain


def reduce_z(me, product, own, out, landed, send, recv):
    signs = (1, -1)
    hops = (1, 1, 2, 2, 2, 1, 1)
    started = []

    def message(way, index):
        return pltpu.make_async_remote_copy(
            src_ref=out.at[way, index], dst_ref=landed.at[way, index],
            send_sem=send.at[way, index], recv_sem=recv.at[way, index],
            device_id=me.along_z(signs[way] * hops[index]), device_id_type=MESH,
        )

    def mine(offset, half):
        target = (me.z + NZ + offset) % NZ
        return own[half, pl.ds(pl.multiple_of(target * BLK, BLK), BLK), :]

    def go(way, index, value):
        out[way, index] = value.astype(BF)
        copy = message(way, index)
        copy.start()
        started.append(copy)

    def landed_sum(way, index):
        message(way, index).wait_recv()
        return landed[way, index].astype(F32)

    for half in range(2):
        own[half] = product(half)
        go(half, 2, mine(4 * signs[half], half))
        for way in range(2):
            go(way, half, mine(3 * signs[way], half))
    for half in range(2):
        for way in range(2):
            go(way, 5 + half, mine(signs[way], half))
    total = [mine(0, half) for half in range(2)]
    for half in range(2):
        for way in (1 - half, half):
            value = landed_sum(way, half) + mine(2 * signs[way], half)
            if half == way:
                value = value + landed_sum(way, 2)
            go(way, 3 + half, value)
    for base in (5, 3):
        for half in range(2):
            for way in range(2):
                total[half] = total[half] + landed_sum(way, base + half)
    return total, lambda: [copy.wait_send() for copy in started]


def exchange_dp(me, source, landing, send, recv):
    copies = []
    for i, (dx, dy) in enumerate(FAR_FIRST):
        peer = me.dp_peer(dx, dy)
        copy = pltpu.make_async_remote_copy(
            src_ref=source.at[pl.ds(pl.multiple_of(peer * BLK, BLK), BLK), :],
            dst_ref=landing.at[pl.ds(pl.multiple_of(me.d * BLK, BLK), BLK), :],
            send_sem=send.at[i], recv_sem=recv.at[i],
            device_id=(peer, me.t), device_id_type=MESH,
        )
        copy.start()
        copies.append(copy)
    here = pl.ds(pl.multiple_of(me.d * BLK, BLK), BLK)
    landing[here, :] = source[here, :]
    return copies


def column_of(row, hits):
    return jnp.sum(jnp.where(hits, row, 0.0), axis=1, keepdims=True)


def layer_kernel(
    tokens_hbm, attn_gain_hbm, mlp_gain_hbm, lengths_hbm, owners_hbm, starts_hbm, w_hbm, wo_hbm, gu_hbm, wd_hbm, cache_hbm,
    hidden_out, lse_out, cache,
    tokens, attn_gain, mlp_gain, ints, w, wo, gu, wd,
    gathered, gathered_mlp, packed, compact, outgoing, sel, route, scat, begin_ref, end_ref, end_row,
    pick, begin_away, end_away, away_ref, cos_ref, sin_ref,
    q2, score_ref, ret_away, landing, slots, attended, inner, resid_keep,
    own, ring_out, ring_in,
    dp_send, dp_recv, ag_send, ag_recv, ag_sib_send, ag_sib_recv, rs_send, rs_recv, core_send, core_recv, load_sem,
):
    me = Place()
    pairs = [
        (tokens_hbm, tokens), (attn_gain_hbm, attn_gain), (owners_hbm, ints.at[0]), (lengths_hbm, ints.at[1]),
        (starts_hbm, ints.at[2]), (w_hbm.at[0], w.at[:, pl.ds(0, 128)]), (w_hbm.at[1], w.at[:, pl.ds(128, 128)]),
        (w_hbm.at[2], w.at[:, pl.ds(256, 128)]), (cache_hbm, cache), (wo_hbm, wo.at[0]), (mlp_gain_hbm, mlp_gain), (gu_hbm, gu.at[0]), (wd_hbm, wd.at[0]),
    ]
    loads = [pltpu.make_async_copy(src, dst, load_sem.at[i]) for i, (src, dst) in enumerate(pairs)]
    for copy in loads:
        copy.start()
    wait_all = greet(me)
    loads[0].wait()
    loads[1].wait()

    def gain_row(ref):
        return jnp.concatenate([ref[i : i + 1, :].astype(F32) for i in range(16)], axis=1)

    normed = scaled_norm(tokens[...].astype(F32), gain_row(attn_gain))
    row_of = lambda zz, cc: cc * 128 + zz * BLK
    my_rows = pl.ds(pl.multiple_of(row_of(me.z, me.c), BLK), BLK)
    for half in range(2):
        gathered[half, my_rows, :] = normed[:, half * HALF : (half + 1) * HALF]
    wait_all()
    begin, finish, settle, drain_gather = gather_z(
        me, gathered, row_of, ag_send.at[0], ag_recv.at[0], ag_sib_send, ag_sib_recv
    )
    begin()

    for copy in loads[2:5]:
        copy.wait()

    def wide(m):
        return jnp.concatenate([ints[m, pl.ds(0, NDP, stride=2), :], ints[m, pl.ds(1, NDP, stride=2), :]], axis=1)

    def mine(m):
        return jnp.concatenate([ints[m, pl.ds(2 * me.d, 1), :], ints[m, pl.ds(2 * me.d + 1, 1), :]], axis=1)

    own_all, len_all, start_all = wide(0), wide(1), wide(2)
    own_row, len_row, start_row = mine(0), mine(1).astype(F32), mine(2).astype(F32)
    before = jnp.where(iota((REQ, REQ), 0) < iota((REQ, REQ), 1), 1.0, 0.0).astype(BF)
    here = own_all == me.d
    here_rank = jnp.dot(jnp.where(here, 1.0, 0.0).astype(BF), before, preferred_element_type=F32)
    away = here & (iota((NDP, REQ), 0) != me.d)
    place_in = jnp.where(away, here_rank, -1.0)
    onehot = jnp.where(iota((NDP, REQ), 0) == own_row, 1.0, 0.0)
    counts = jnp.dot(onehot.astype(BF), before, preferred_element_type=F32)
    rank = jnp.sum(onehot * counts, axis=0, keepdims=True)
    own_wide = own_row.astype(F32)
    place = jnp.where(own_row == me.d, rank, HOME + own_wide * BLK + rank)
    chosen = iota((SLOTS, REQ), 0).astype(F32) == place
    sel[...] = jnp.where(chosen, 1.0, 0.0).astype(BF)
    request = iota((REQ, REQ), 0)
    natural = ((request >> 4) & 7) * 32 + (request >> 7) * 16 + (request & 15)
    reorder = natural == iota((REQ, REQ), 1)
    place_col = column_of(place, reorder)
    place_row = jnp.sum(jnp.where(request == iota((REQ, REQ), 1), place_col, 0.0), axis=0, keepdims=True)
    route[...] = jnp.where(iota((SLOTS, REQ), 0).astype(F32) == place_row, 1.0, 0.0).astype(BF)
    scat[...] = jnp.where(iota((REQ, SLOTS), 1).astype(F32) == place_col, 1.0, 0.0).astype(BF)

    def spread(rows16):
        return jnp.concatenate(
            [jnp.broadcast_to(rows16[b : b + 1, :], (BLK, REQ)) for b in range(NDP)], axis=0
        )

    slot = (iota((NDP * BLK, REQ), 0) & (BLK - 1)).astype(F32)
    hits_in = spread(place_in) == slot
    begin_all = start_all.astype(F32)
    finish_all = begin_all + len_all.astype(F32)
    hits_home = chosen[:HOME]
    begin_col = jnp.concatenate(
        [column_of(start_row + 1.0, hits_home), column_of(spread(begin_all) + 1.0, hits_in)], axis=0
    ) - 1.0
    finish_col = jnp.concatenate(
        [column_of(start_row + len_row + 1.0, hits_home), column_of(spread(finish_all) + 1.0, hits_in)], axis=0
    ) - 1.0
    begin_ref[...] = jnp.broadcast_to(begin_col[:HOME], (HOME, 128))
    end_ref[...] = jnp.broadcast_to(finish_col[:HOME], (HOME, 128))
    eye = iota((SLOTS, SLOTS), 0) == iota((SLOTS, SLOTS), 1)
    finish_row = jnp.sum(jnp.where(eye, finish_col, 0.0), axis=0, keepdims=True)
    begin_row = jnp.sum(jnp.where(eye, begin_col, 0.0), axis=0, keepdims=True)
    end_row[...] = jnp.broadcast_to(finish_row, (8, SLOTS))
    index = iota((2 * BATCH, 1), 0).astype(F32)
    second = index >= BATCH
    within = jnp.where(second, index - BATCH, index)
    nth = jnp.floor((within + 0.5) * (1.0 / CAP))
    source = jnp.full((2 * BATCH, 1), -1000.0, F32)
    for k, (dx, dy) in enumerate(FAR_FIRST):
        at = (nth == k % 8) & (second if k >= 8 else jnp.logical_not(second))
        source = jnp.where(at, (me.dp_peer(dx, dy) * BLK).astype(F32), source)
    source = source + within - nth * CAP
    picked = iota((2 * BATCH, NDP * BLK), 1).astype(F32) == source
    pick[...] = jnp.where(picked, 1.0, 0.0).astype(BF)
    begin_away[...] = jnp.broadcast_to(column_of(begin_row[:, HOME:] + 1.0, picked) - 1.0, (2 * BATCH, 128))
    end_away[...] = jnp.broadcast_to(column_of(finish_row[:, HOME:] + 1.0, picked) - 1.0, (2 * BATCH, 128))

    len_col = column_of(len_row, reorder)
    lane = iota((1, 128), 1) & (HD // 2 - 1)
    freqs = jnp.exp(lane.astype(F32) * np.float32(-np.log(ROPE_BASE) / (HD // 2)))
    angle = len_col * freqs
    turns = jnp.floor(angle * (1.0 / (2.0 * np.pi)) + 0.5)
    left = (angle - turns * 6.28125) - turns * np.float32(2.0 * np.pi - 6.28125)
    x = 0.5 * left
    x2 = x * x
    sin_half = x * (1.0 + x2 * (-1 / 6 + x2 * (1 / 120 + x2 * (-1 / 5040 + x2 * (1 / 362880 - x2 / 39916800)))))
    cos_half = 1.0 + x2 * (
        -1 / 2 + x2 * (1 / 24 + x2 * (-1 / 720 + x2 * (1 / 40320 + x2 * (-1 / 3628800 + x2 / 479001600))))
    )
    sine = 2.0 * sin_half * cos_half
    cos_ref[...] = 1.0 - 2.0 * sin_half * sin_half
    sin_ref[...] = jnp.where((iota((REQ, 128), 1) & (HD - 1)) < HD // 2, -sine, sine)

    finish()

    def to_core(src, dst, index):
        copy = pltpu.make_async_remote_copy(
            src_ref=src, dst_ref=dst, send_sem=core_send.at[index], recv_sem=core_recv.at[index],
            device_id=me.sib, device_id_type=MESH,
        )
        copy.start()
        return copy

    for copy in loads[5:8]:
        copy.wait()
    low_half = (iota((128, 128), 1) & (HD - 1)) < HD // 2

    def project(core):
        rows = pl.ds(pl.multiple_of(core * 128, 128), 128)
        projected = jnp.dot(gathered[0, rows, :], w[:HALF], preferred_element_type=F32)
        projected = projected + jnp.dot(gathered[1, rows, :], w[HALF:], preferred_element_type=F32)
        for m in range(2):
            values = projected[:, m * 128 : (m + 1) * 128]
            partner = jnp.where(low_half, pltpu.roll(values, 96, 1), pltpu.roll(values, 32, 1))
            packed[rows, m * 128 : (m + 1) * 128] = (values * cos_ref[rows, :] + partner * sin_ref[rows, :]).astype(BF)
        packed[rows, 256:384] = projected[:, 256:384].astype(BF)

    project(me.c)
    settle()
    project(1 - me.c)
    outgoing[...] = jnp.dot(route[HOME:, :], packed[...], preferred_element_type=F32).astype(BF)
    sent = exchange_dp(me, outgoing, compact.at[pl.ds(HOME, NDP * BLK), :], dp_send.at[0], dp_recv.at[0])
    compact[:HOME, :] = jnp.dot(route[:HOME, :], packed[...], preferred_element_type=F32).astype(BF)
    loads[8].wait()

    def attend(operand, begins, ends, count):
        low_lanes = iota((count, 128), 1) < HD
        q = operand[:count, 0:128].astype(F32) * (1.0 / 8.0)
        k = operand[:count, 128:256].astype(F32)
        v = operand[:count, 256:384].astype(F32)
        spans = [pl.ds(head * count, count) for head in range(2)]
        chunks = [pl.ds(first, SPAN) for first in range(0, ROWS, SPAN)]
        own_score, top = [], []
        for head in range(2):
            qh = jnp.where(low_lanes if head == 0 else jnp.logical_not(low_lanes), q, 0.0)
            q2[spans[head], :] = qh.astype(BF)
            own_score.append(jnp.sum(qh * k, axis=1, keepdims=True))
            top.append(jnp.full((count, 128), LOW, F32))
        for chunk in chunks:
            across = (iota((1, SPAN), 1) + chunk.start).astype(F32)
            live = (across >= begins[:count, 0:1]) & (across < ends[:count, 0:1])
            for head in range(2):
                scores = lax.dot_general(
                    q2[spans[head], :], cache[0, chunk, :], (((1,), (1,)), ((), ())), preferred_element_type=F32
                )
                scores = jnp.where(live, scores, LOW)
                score_ref[spans[head], chunk] = scores
                for first in range(0, SPAN, 128):
                    top[head] = jnp.maximum(top[head], scores[:, first : first + 128])
        out, lse = [], []
        for head in range(2):
            peak = jnp.maximum(own_score[head], jnp.max(top[head], axis=1, keepdims=True))
            own_weight = jnp.exp(own_score[head] - peak)
            summed = jnp.concatenate([own_weight * v, jnp.broadcast_to(own_weight, (count, 128))], axis=1)
            for chunk in chunks:
                weights = jnp.exp(score_ref[spans[head], chunk] - peak).astype(BF)
                values = jnp.concatenate([cache[1, chunk, :], jnp.ones((SPAN, 128), BF)], axis=1)
                summed = summed + jnp.dot(weights, values, preferred_element_type=F32)
            out.append(summed[:, 0:128] / summed[:, 128:256])
            lse.append(peak + jnp.log(summed[:, 128:256]))
        high = [value.astype(BF).astype(F32) for value in lse]
        low = [x - y for x, y in zip(lse, high)]
        lane = iota((count, 128), 1)
        tail = jnp.where(lane == 0, high[0], jnp.where(lane == 1, low[0], jnp.where(lane == 2, high[1], low[1])))
        return jnp.concatenate([jnp.where(low_lanes, out[0], out[1]).astype(BF), tail.astype(BF)], axis=1)

    slots[:HOME, :] = attend(compact, begin_ref, end_ref, HOME)
    drain_gather()
    for copy in sent:
        copy.wait_recv()
    shared = [to_core(wo_hbm, wo.at[1], 0)]
    away_ref[...] = jnp.dot(pick[...], compact[HOME:, :], preferred_element_type=F32).astype(BF)
    line = iota((8 * BLK, BATCH), 0)
    unpick = ((line >> 4) * CAP + (line & 15) == iota((8 * BLK, BATCH), 1)) & ((line & 15) < CAP)
    unpick = jnp.where(unpick, 1.0, 0.0).astype(BF)
    landing[pl.ds(pl.multiple_of(me.d * BLK, BLK), BLK), :] = jnp.zeros((BLK, 256), BF)
    back = []
    found = attend(away_ref, begin_away, end_away, 2 * BATCH)
    for batch in range(2):
        ret_away[batch] = jnp.dot(
            unpick, found[batch * BATCH : (batch + 1) * BATCH], preferred_element_type=F32
        ).astype(BF)
        for k in range(batch * 8, min(batch * 8 + 8, NDP - 1)):
            copy = pltpu.make_async_remote_copy(
                src_ref=ret_away.at[batch, pl.ds(k % 8 * BLK, BLK), :],
                dst_ref=landing.at[pl.ds(pl.multiple_of(me.d * BLK, BLK), BLK), :],
                send_sem=dp_send.at[1, k], recv_sem=dp_recv.at[1, k],
                device_id=(me.dp_peer(*FAR_FIRST[k]), me.t), device_id_type=MESH,
            )
            copy.start()
            back.append(copy)

    @pl.loop(0, ROWS // PBLK)
    def _(block):
        base = pl.multiple_of(block * PBLK, PBLK)
        span = pl.ds(base, PBLK)
        position = (iota((PBLK, SLOTS), 0) + base).astype(F32)
        written = jnp.where(position == end_row[0:1, :], 1.0, 0.0)
        hit = jnp.max(written, axis=1, keepdims=True) > 0.5
        fresh = jnp.dot(written.astype(BF), compact[:, 128:384], preferred_element_type=F32)
        cache[0, span, :] = jnp.where(hit, fresh[:, 0:128], cache[0, span, :].astype(F32)).astype(BF)
        cache[1, span, :] = jnp.where(hit, fresh[:, 128:256], cache[1, span, :].astype(F32)).astype(BF)

    loads[9].wait()
    for copy in back:
        copy.wait_recv()
    slots[HOME:, :] = landing[...]

    def assemble(core):
        rows = pl.ds(pl.multiple_of(core * 128, 128), 128)
        return jnp.dot(scat[rows, :], slots[:, 0:128], preferred_element_type=F32).astype(BF)

    attended[2] = assemble(1 - me.c)
    swapped = to_core(attended.at[2], attended.at[1], 3)
    attended[0] = assemble(me.c)
    for half in range(2):
        own[0, half] = jnp.dot(attended[0], wo[0, :, half * HALF : (half + 1) * HALF], preferred_element_type=F32)
    shared[0].wait_recv()
    swapped.wait_recv()
    shared += [to_core(gu_hbm, gu.at[1], 1), to_core(wd_hbm, wd.at[1], 2)]

    def out_product(half):
        columns = pl.ds(half * HALF, HALF)
        return own[0, half] + jnp.dot(attended[1], wo[1, :, columns], preferred_element_type=F32)

    total, drain_first = reduce_z(
        me, out_product, own.at[0], ring_out.at[0], ring_in.at[0], rs_send.at[0], rs_recv.at[0]
    )
    resid = (tokens[...].astype(F32) + jnp.concatenate(total, axis=1)).astype(BF)
    resid_keep[...] = resid
    loads[10].wait()
    normed = scaled_norm(resid.astype(F32), gain_row(mlp_gain))
    row_of_chip = lambda zz, cc: zz * BLK
    my_rows = pl.ds(pl.multiple_of(me.z * BLK, BLK), BLK)
    for half in range(2):
        gathered_mlp[half, my_rows, :] = normed[:, half * HALF : (half + 1) * HALF]
    begin, finish_mlp, _, drain_mlp = gather_z(me, gathered_mlp, row_of_chip, ag_send.at[1], ag_recv.at[1])
    begin()
    spread_sel = sel[...].astype(F32)
    tail = slots[:, 128:256].astype(F32)
    for head in range(2):
        lse = tail[:, 2 * head : 2 * head + 1] + tail[:, 2 * head + 1 : 2 * head + 2]
        lse_out[head : head + 1, :] = jnp.sum(spread_sel * lse, axis=0, keepdims=True)
    drain_first()
    for copy in sent + back:
        copy.wait_send()
    loads[11].wait()
    loads[12].wait()
    shared[1].wait_recv()
    shared[2].wait_recv()
    finish_mlp()
    for core in range(2):
        for tile in range(FFL // 256):
            columns = pl.ds(tile * 256, 256)
            both = []
            for m in range(2):
                value = jnp.dot(gathered_mlp[0], gu[core, m, :HALF, columns], preferred_element_type=F32)
                both.append(value + jnp.dot(gathered_mlp[1], gu[core, m, HALF:, columns], preferred_element_type=F32))
            inner[core, :, columns] = (both[0] / (1.0 + jnp.exp(-both[0])) * both[1]).astype(BF)

    def down_product(half):
        columns = pl.ds(half * HALF, HALF)
        value = jnp.dot(inner[0], wd[0, :, columns], preferred_element_type=F32)
        return value + jnp.dot(inner[1], wd[1, :, columns], preferred_element_type=F32)

    total, drain_last = reduce_z(
        me, down_product, own.at[1], ring_out.at[1], ring_in.at[1], rs_send.at[1], rs_recv.at[1]
    )
    hidden_out[...] = (resid_keep[...].astype(F32) + jnp.concatenate(total, axis=1)).astype(BF)
    drain_mlp()
    drain_last()
    for copy in shared:
        copy.wait_send()
    swapped.wait_send()


def store_kernel(hidden, lse, cache, hidden_out, lse_out, cache_out, sems):
    pairs = [(cache.at[0], cache_out.at[0]), (cache.at[1], cache_out.at[1]), (hidden, hidden_out), (lse, lse_out)]
    copies = [pltpu.make_async_copy(src, dst, sems.at[i]) for i, (src, dst) in enumerate(pairs)]
    for copy in copies:
        copy.start()
    for copy in copies:
        copy.wait()


VMEM_SPEC = pl.BlockSpec(memory_space=pltpu.VMEM)
ANY_SPEC = pl.BlockSpec(memory_space=pl.ANY)
DMA = pltpu.SemaphoreType.DMA


def on_device(tokens, attn_gain, mlp_gain, project_in, project_out, gate_up, project_down, kv_cache, lengths, owners, cache_start):
    shape = jax.ShapeDtypeStruct
    results = (shape((BLK, D), BF), shape((2, REQ), F32), shape((2, ROWS, 128), BF))
    held = pl.pallas_call(
        layer_kernel,
        out_shape=(pltpu.VMEM((BLK, D), BF), pltpu.VMEM((2, REQ), F32), pltpu.VMEM((2, ROWS, 128), BF)),
        in_specs=[ANY_SPEC] * 11,
        out_specs=(VMEM_SPEC,) * 3,
        scratch_shapes=[
            pltpu.VMEM((BLK, D), BF), pltpu.VMEM((16, 128), BF), pltpu.VMEM((16, 128), BF), pltpu.VMEM((3, 32, 128), I32),
            pltpu.VMEM((D, 384), BF), pltpu.VMEM((2, 128, D), BF), pltpu.VMEM((2, 2, D, FFL), BF), pltpu.VMEM((2, FFL, D), BF),
            pltpu.VMEM((2, REQ, HALF), BF), pltpu.VMEM((2, 128, HALF), BF), pltpu.VMEM((REQ, 384), BF), pltpu.VMEM((SLOTS, 384), BF),
            pltpu.VMEM((NDP * BLK, 384), BF), pltpu.VMEM((SLOTS, REQ), BF), pltpu.VMEM((SLOTS, REQ), BF), pltpu.VMEM((REQ, SLOTS), BF),
            pltpu.VMEM((HOME, 128), F32), pltpu.VMEM((HOME, 128), F32), pltpu.VMEM((8, SLOTS), F32),
            pltpu.VMEM((2 * BATCH, NDP * BLK), BF), pltpu.VMEM((2 * BATCH, 128), F32), pltpu.VMEM((2 * BATCH, 128), F32),
            pltpu.VMEM((2 * BATCH, 384), BF), pltpu.VMEM((REQ, 128), F32), pltpu.VMEM((REQ, 128), F32),
            pltpu.VMEM((4 * BATCH, 128), BF), pltpu.VMEM((4 * BATCH, ROWS), F32),
            pltpu.VMEM((2, 8 * BLK, 256), BF), pltpu.VMEM((NDP * BLK, 256), BF),
            pltpu.VMEM((SLOTS, 256), BF), pltpu.VMEM((3, 128, 128), BF), pltpu.VMEM((2, 128, FFL), BF), pltpu.VMEM((BLK, D), BF),
            pltpu.VMEM((2, 2, 128, HALF), F32), pltpu.VMEM((2, 2, 7, BLK, HALF), BF), pltpu.VMEM((2, 2, 7, BLK, HALF), BF),
            DMA((2, 15)), DMA((2, 15)), DMA((2, 2, 7)), DMA((2, 2, 7)), DMA((16,)), DMA((16,)),
            DMA((2, 2, 7)), DMA((2, 2, 7)), DMA((4,)), DMA((4,)), DMA((13,)),
        ],
        compiler_params=pltpu.CompilerParams(collective_id=0, has_side_effects=True, vmem_limit_bytes=54 << 20),
        name="decode_layer",
    )(
        tokens, attn_gain.reshape(16, 128), mlp_gain.reshape(16, 128), lengths.reshape(32, 128), owners.reshape(32, 128),
        cache_start.reshape(32, 128), project_in, project_out, gate_up, project_down, kv_cache,
    )
    hidden_states, lse, kv_updated = pl.pallas_call(
        store_kernel,
        out_shape=results,
        in_specs=[VMEM_SPEC] * 3,
        out_specs=(ANY_SPEC,) * 3,
        scratch_shapes=[DMA((4,))],
        name="store_results",
    )(*(pltpu.with_memory_space_constraint(value, pltpu.VMEM) for value in held))
    return hidden_states, lse.T, kv_updated


def solution(mesh):
    placed = (
        P(("dp", "tensor"), None),
        P(),
        P(),
        P(None, None, "tensor"),
        P("tensor", None),
        P(None, None, "tensor"),
        P("tensor", None),
        P(None, "dp", "tensor"),
        P(),
        P(),
        P(),
    )
    return jax.shard_map(
        on_device,
        mesh=mesh,
        in_specs=placed,
        out_specs=(P(("dp", "tensor"), None), P("dp", "tensor"), P(None, "dp", "tensor")),
        check_vma=False,
    )
```

```python
import functools

import jax
import jax.numpy as jnp
import numpy as np
from jax import lax
from jax.experimental import pallas as pl
from jax.experimental.pallas import tpu as pltpu
from jax.sharding import PartitionSpec as P

MESH = pl.DeviceIdType.MESH
BF = jnp.bfloat16
F32 = jnp.float32
I32 = jnp.int32

EPS = 1e-05
ROPE_BASE = 130000.0
LOW = -1e30
HD = 64
NDP = 16
NTP = 16
NZ = 8
D = 2048
HALF = 1024
BLK = 16
REQ = 256
HOME = 128
SLOTS = HOME + NDP * BLK
ROWS = 4096
FFL = 512
PBLK = 2048
SPAN = 512
CAP = 9
BATCH = 80


FAR_FIRST = sorted(
    [(dx, dy) for dx in range(4) for dy in range(4) if (dx, dy) != (0, 0)],
    key=lambda at: -(min(at[0], 4 - at[0]) + min(at[1], 4 - at[1])),
)


class Place:
    def __init__(self):
        self.d = lax.axis_index("dp")
        self.t = lax.axis_index("tensor")
        self.z = self.t // 2
        self.c = self.t % 2
        self.other = self.t + 1 - 2 * self.c
        self.sib = (self.d, self.other)

    def along_z(self, offset):
        return (self.d, ((self.z + NZ + offset) % NZ) * 2 + self.c)

    def dp_peer(self, dx, dy):
        return ((self.d // 4 + dx) % 4) * 4 + (self.d % 4 + dy) % 4


def greet(me):
    barrier = pltpu.get_barrier_semaphore()
    targets = [me.along_z(k) for k in (1, -1, 2, -2)] + [me.sib]
    targets += [(me.dp_peer(dx, dy), t) for dx, dy in FAR_FIRST for t in (me.t, me.other)]
    for target in targets:
        pl.semaphore_signal(barrier, inc=1, device_id=target, device_id_type=MESH)
    return lambda: pl.semaphore_wait(barrier, len(targets))


def iota(shape, axis):
    return lax.broadcasted_iota(I32, shape, axis)


def scaled_norm(wide, gain):
    factor = lax.rsqrt(jnp.mean(wide * wide, axis=-1, keepdims=True) + EPS)
    return (wide * factor * gain).astype(BF)


def gather_z(me, buf, row_of, send, recv, sib_send=None, sib_recv=None):
    signs = (1, -1)
    started = []
    sib_copies = []
    kinds = lambda way: ((2, 0, 2), (2, 1, 2), (1, 0, 1), (1, 1, 1), (3, 0, 1), (3, 1, 1), (4, way, 2))

    def block(origin, half):
        return buf.at[half, pl.ds(pl.multiple_of(row_of(origin, me.c), BLK), BLK), :]

    def message(way, index):
        distance, half, hops = kinds(way)[index]
        ref = block((me.z + NZ - signs[way] * (distance - hops)) % NZ, half)
        return pltpu.make_async_remote_copy(
            src_ref=ref, dst_ref=ref, send_sem=send.at[way, index], recv_sem=recv.at[way, index],
            device_id=me.along_z(signs[way] * hops), device_id_type=MESH,
        )

    def start(way, index):
        copy = message(way, index)
        copy.start()
        started.append(copy)

    def sibling(origin, half):
        if sib_send is None:
            return
        index = len(sib_copies)
        ref = block(origin, half)
        copy = pltpu.make_async_remote_copy(
            src_ref=ref, dst_ref=ref, send_sem=sib_send.at[index], recv_sem=sib_recv.at[index],
            device_id=me.sib, device_id_type=MESH,
        )
        copy.start()
        sib_copies.append(copy)

    def begin():
        for index in range(4):
            for way in range(2):
                start(way, index ^ way if index < 2 else index)
        for half in range(2):
            sibling(me.z, half)

    def arrive(way, index):
        message(way, index).wait_recv()
        distance, half, _ = kinds(way)[index]
        if distance == 2:
            if half == way:
                start(way, 6)
            start(way, 4 + half)
        sibling((me.z + NZ - signs[way] * distance) % NZ, half)

    def finish():
        for index in (0, 1, 2, 3, 4, 5, 6):
            for way in range(2):
                arrive(way, index if index in (2, 3, 6) else index ^ way)
    def settle():
        for copy in sib_copies:
            copy.wait_recv()

    def drain():
        for copy in started + sib_copies:
            copy.wait_send()

    return begin, finish, settle, drain


def reduce_z(me, product, own, out, landed, send, recv):
    signs = (1, -1)
    hops = (1, 1, 2, 2, 2, 1, 1)
    started = []

    def message(way, index):
        return pltpu.make_async_remote_copy(
            src_ref=out.at[way, index], dst_ref=landed.at[way, index],
            send_sem=send.at[way, index], recv_sem=recv.at[way, index],
            device_id=me.along_z(signs[way] * hops[index]), device_id_type=MESH,
        )

    def mine(offset, half):
        target = (me.z + NZ + offset) % NZ
        return own[half, pl.ds(pl.multiple_of(target * BLK, BLK), BLK), :]

    def go(way, index, value):
        out[way, index] = value.astype(BF)
        copy = message(way, index)
        copy.start()
        started.append(copy)

    def landed_sum(way, index):
        message(way, index).wait_recv()
        return landed[way, index].astype(F32)

    for half in range(2):
        own[half] = product(half)
        go(half, 2, mine(4 * signs[half], half))
        for way in range(2):
            go(way, half, mine(3 * signs[way], half))
    for half in range(2):
        for way in range(2):
            go(way, 5 + half, mine(signs[way], half))
    total = [mine(0, half) for half in range(2)]
    for half in range(2):
        for way in (1 - half, half):
            value = landed_sum(way, half) + mine(2 * signs[way], half)
            if half == way:
                value = value + landed_sum(way, 2)
            go(way, 3 + half, value)
    for base in (5, 3):
        for half in range(2):
            for way in range(2):
                total[half] = total[half] + landed_sum(way, base + half)
    return total, lambda: [copy.wait_send() for copy in started]


def exchange_dp(me, source, landing, send, recv):
    copies = []
    for i, (dx, dy) in enumerate(FAR_FIRST):
        peer = me.dp_peer(dx, dy)
        copy = pltpu.make_async_remote_copy(
            src_ref=source.at[pl.ds(pl.multiple_of(peer * BLK, BLK), BLK), :],
            dst_ref=landing.at[pl.ds(pl.multiple_of(me.d * BLK, BLK), BLK), :],
            send_sem=send.at[i], recv_sem=recv.at[i],
            device_id=(peer, me.t), device_id_type=MESH,
        )
        copy.start()
        copies.append(copy)
    here = pl.ds(pl.multiple_of(me.d * BLK, BLK), BLK)
    landing[here, :] = source[here, :]
    return copies


def column_of(row, hits):
    return jnp.sum(jnp.where(hits, row, 0.0), axis=1, keepdims=True)


def layer_kernel(
    tokens_hbm, attn_gain_hbm, mlp_gain_hbm, lengths_hbm, owners_hbm, starts_hbm, w_hbm, wo_hbm, gu_hbm, wd_hbm, cache_hbm,
    hidden_out, lse_out, cache,
    tokens, attn_gain, mlp_gain, ints, w, wo, gu, wd,
    gathered, gathered_mlp, packed, query, fresh_kv, outgoing, sel, route, scat, begin_ref, end_ref, end_row,
    pick, begin_away, end_away, away_q, away_kv, cos_ref, sin_ref,
    q2, score_ref, ret_away, slots, tails, attended, inner, resid_keep,
    own, ring_out, ring_in,
    dp_send, dp_recv, ag_send, ag_recv, ag_sib_send, ag_sib_recv, rs_send, rs_recv, core_send, core_recv, load_sem,
):
    me = Place()
    pairs = [
        (tokens_hbm, tokens), (attn_gain_hbm, attn_gain), (owners_hbm, ints.at[0]), (lengths_hbm, ints.at[1]),
        (starts_hbm, ints.at[2]), (w_hbm.at[0], w.at[:, pl.ds(0, 128)]), (w_hbm.at[1], w.at[:, pl.ds(128, 128)]),
        (w_hbm.at[2], w.at[:, pl.ds(256, 128)]), (cache_hbm, cache), (wo_hbm, wo.at[0]), (mlp_gain_hbm, mlp_gain), (gu_hbm, gu.at[0]), (wd_hbm, wd.at[0]),
    ]
    loads = [pltpu.make_async_copy(src, dst, load_sem.at[i]) for i, (src, dst) in enumerate(pairs)]
    for copy in loads[:2]:
        copy.start()
    wait_all = greet(me)
    for copy in loads[2:]:
        copy.start()
    loads[0].wait()
    loads[1].wait()

    def gain_row(ref):
        return jnp.concatenate([ref[i : i + 1, :].astype(F32) for i in range(16)], axis=1)

    normed = scaled_norm(tokens[...].astype(F32), gain_row(attn_gain))
    row_of = lambda zz, cc: cc * 128 + zz * BLK
    my_rows = pl.ds(pl.multiple_of(row_of(me.z, me.c), BLK), BLK)
    for half in range(2):
        gathered[half, my_rows, :] = normed[:, half * HALF : (half + 1) * HALF]
    wait_all()
    begin, finish, settle, drain_gather = gather_z(
        me, gathered, row_of, ag_send.at[0], ag_recv.at[0], ag_sib_send, ag_sib_recv
    )
    begin()

    for copy in loads[2:5]:
        copy.wait()

    def wide(m):
        return jnp.concatenate([ints[m, pl.ds(0, NDP, stride=2), :], ints[m, pl.ds(1, NDP, stride=2), :]], axis=1)

    def mine(m):
        return jnp.concatenate([ints[m, pl.ds(2 * me.d, 1), :], ints[m, pl.ds(2 * me.d + 1, 1), :]], axis=1)

    own_all, len_all, start_all = wide(0), wide(1), wide(2)
    own_row, len_row, start_row = mine(0), mine(1).astype(F32), mine(2).astype(F32)
    before = jnp.where(iota((REQ, REQ), 0) < iota((REQ, REQ), 1), 1.0, 0.0).astype(BF)
    here = own_all == me.d
    here_rank = jnp.dot(jnp.where(here, 1.0, 0.0).astype(BF), before, preferred_element_type=F32)
    away = here & (iota((NDP, REQ), 0) != me.d)
    place_in = jnp.where(away, here_rank, -1.0)
    onehot = jnp.where(iota((NDP, REQ), 0) == own_row, 1.0, 0.0)
    counts = jnp.dot(onehot.astype(BF), before, preferred_element_type=F32)
    rank = jnp.sum(onehot * counts, axis=0, keepdims=True)
    own_wide = own_row.astype(F32)
    place = jnp.where(own_row == me.d, rank, HOME + own_wide * BLK + rank)
    chosen = iota((SLOTS, REQ), 0).astype(F32) == place
    sel[...] = jnp.where(chosen, 1.0, 0.0).astype(BF)
    request = iota((REQ, REQ), 0)
    natural = ((request >> 4) & 7) * 32 + (request >> 7) * 16 + (request & 15)
    reorder = natural == iota((REQ, REQ), 1)
    place_col = column_of(place, reorder)
    place_row = jnp.sum(jnp.where(request == iota((REQ, REQ), 1), place_col, 0.0), axis=0, keepdims=True)
    route[...] = jnp.where(iota((SLOTS, REQ), 0).astype(F32) == place_row, 1.0, 0.0).astype(BF)
    scat[...] = jnp.where(iota((REQ, SLOTS), 1).astype(F32) == place_col, 1.0, 0.0).astype(BF)

    def spread(rows16):
        return jnp.concatenate(
            [jnp.broadcast_to(rows16[b : b + 1, :], (BLK, REQ)) for b in range(NDP)], axis=0
        )

    slot = (iota((NDP * BLK, REQ), 0) & (BLK - 1)).astype(F32)
    hits_in = spread(place_in) == slot
    begin_all = start_all.astype(F32)
    finish_all = begin_all + len_all.astype(F32)
    hits_home = chosen[:HOME]
    begin_col = jnp.concatenate(
        [column_of(start_row + 1.0, hits_home), column_of(spread(begin_all) + 1.0, hits_in)], axis=0
    ) - 1.0
    finish_col = jnp.concatenate(
        [column_of(start_row + len_row + 1.0, hits_home), column_of(spread(finish_all) + 1.0, hits_in)], axis=0
    ) - 1.0
    begin_ref[...] = jnp.broadcast_to(begin_col[:HOME], (HOME, 128))
    end_ref[...] = jnp.broadcast_to(finish_col[:HOME], (HOME, 128))
    eye = iota((SLOTS, SLOTS), 0) == iota((SLOTS, SLOTS), 1)
    finish_row = jnp.sum(jnp.where(eye, finish_col, 0.0), axis=0, keepdims=True)
    begin_row = jnp.sum(jnp.where(eye, begin_col, 0.0), axis=0, keepdims=True)
    end_row[...] = jnp.broadcast_to(finish_row, (8, SLOTS))
    index = iota((2 * BATCH, 1), 0).astype(F32)
    second = index >= BATCH
    within = jnp.where(second, index - BATCH, index)
    nth = jnp.floor((within + 0.5) * (1.0 / CAP))
    source = jnp.full((2 * BATCH, 1), -1000.0, F32)
    for k, (dx, dy) in enumerate(FAR_FIRST):
        at = (nth == k % 8) & (second if k >= 8 else jnp.logical_not(second))
        source = jnp.where(at, (me.dp_peer(dx, dy) * BLK).astype(F32), source)
    source = source + within - nth * CAP
    picked = iota((2 * BATCH, NDP * BLK), 1).astype(F32) == source
    pick[...] = jnp.where(picked, 1.0, 0.0).astype(BF)
    begin_away[...] = jnp.broadcast_to(column_of(begin_row[:, HOME:] + 1.0, picked) - 1.0, (2 * BATCH, 128))
    end_away[...] = jnp.broadcast_to(column_of(finish_row[:, HOME:] + 1.0, picked) - 1.0, (2 * BATCH, 128))

    len_col = column_of(len_row, reorder)
    lane = iota((1, 128), 1) & (HD // 2 - 1)
    freqs = jnp.exp(lane.astype(F32) * np.float32(-np.log(ROPE_BASE) / (HD // 2)))
    angle = len_col * freqs
    turns = jnp.floor(angle * (1.0 / (2.0 * np.pi)) + 0.5)
    left = (angle - turns * 6.28125) - turns * np.float32(2.0 * np.pi - 6.28125)
    x = 0.5 * left
    x2 = x * x
    sin_half = x * (1.0 + x2 * (-1 / 6 + x2 * (1 / 120 + x2 * (-1 / 5040 + x2 * (1 / 362880 - x2 / 39916800)))))
    cos_half = 1.0 + x2 * (
        -1 / 2 + x2 * (1 / 24 + x2 * (-1 / 720 + x2 * (1 / 40320 + x2 * (-1 / 3628800 + x2 / 479001600))))
    )
    sine = 2.0 * sin_half * cos_half
    cos_ref[...] = 1.0 - 2.0 * sin_half * sin_half
    sin_ref[...] = jnp.where((iota((REQ, 128), 1) & (HD - 1)) < HD // 2, -sine, sine)

    finish()

    def to_core(src, dst, index):
        copy = pltpu.make_async_remote_copy(
            src_ref=src, dst_ref=dst, send_sem=core_send.at[index], recv_sem=core_recv.at[index],
            device_id=me.sib, device_id_type=MESH,
        )
        copy.start()
        return copy

    for copy in loads[5:8]:
        copy.wait()
    low_half = (iota((128, 128), 1) & (HD - 1)) < HD // 2

    def project(core):
        rows = pl.ds(pl.multiple_of(core * 128, 128), 128)
        projected = jnp.dot(gathered[0, rows, :], w[:HALF], preferred_element_type=F32)
        projected = projected + jnp.dot(gathered[1, rows, :], w[HALF:], preferred_element_type=F32)
        for m in range(2):
            values = projected[:, m * 128 : (m + 1) * 128]
            partner = jnp.where(low_half, pltpu.roll(values, 96, 1), pltpu.roll(values, 32, 1))
            packed[rows, m * 128 : (m + 1) * 128] = (values * cos_ref[rows, :] + partner * sin_ref[rows, :]).astype(BF)
        packed[rows, 256:384] = projected[:, 256:384].astype(BF)

    project(me.c)
    settle()
    project(1 - me.c)
    sent = []
    for lanes, landing, row in ((pl.ds(0, 128), query, 0), (pl.ds(128, 256), fresh_kv, 3)):
        outgoing[:, lanes] = jnp.dot(route[HOME:, :], packed[:, lanes], preferred_element_type=F32).astype(BF)
        there = landing.at[pl.ds(HOME, NDP * BLK), :]
        sent.append(exchange_dp(me, outgoing.at[:, lanes], there, dp_send.at[row], dp_recv.at[row]))
    home = jnp.dot(route[:HOME, :], packed[...], preferred_element_type=F32).astype(BF)
    query[:HOME, :] = home[:, 0:128]
    fresh_kv[:HOME, :] = home[:, 128:384]
    loads[8].wait()

    def attend(queries, pair, begins, ends, count, ready):
        low_lanes = iota((count, 128), 1) < HD
        q = queries[:count, :].astype(F32) * (1.0 / 8.0)
        spans = [pl.ds(head * count, count) for head in range(2)]
        chunks = [pl.ds(first, SPAN) for first in range(0, ROWS, SPAN)]
        top = []
        for head in range(2):
            qh = jnp.where(low_lanes if head == 0 else jnp.logical_not(low_lanes), q, 0.0)
            q2[spans[head], :] = qh.astype(BF)
            top.append(jnp.full((count, 128), LOW, F32))
        for chunk in chunks:
            across = (iota((1, SPAN), 1) + chunk.start).astype(F32)
            live = (across >= begins[:count, 0:1]) & (across < ends[:count, 0:1])
            for head in range(2):
                scores = lax.dot_general(
                    q2[spans[head], :], cache[0, chunk, :], (((1,), (1,)), ((), ())), preferred_element_type=F32
                )
                scores = jnp.where(live, scores, LOW)
                score_ref[spans[head], chunk] = scores
                for first in range(0, SPAN, 128):
                    top[head] = jnp.maximum(top[head], scores[:, first : first + 128])
        ready()
        k = pair[:count, 0:128].astype(F32)
        v = pair[:count, 128:256].astype(F32)
        out, lse = [], []
        for head in range(2):
            own_score = jnp.sum(q2[spans[head], :].astype(F32) * k, axis=1, keepdims=True)
            peak = jnp.maximum(own_score, jnp.max(top[head], axis=1, keepdims=True))
            own_weight = jnp.exp(own_score - peak)
            summed = jnp.concatenate([own_weight * v, jnp.broadcast_to(own_weight, (count, 128))], axis=1)
            for chunk in chunks:
                weights = jnp.exp(score_ref[spans[head], chunk] - peak).astype(BF)
                values = jnp.concatenate([cache[1, chunk, :], jnp.ones((SPAN, 128), BF)], axis=1)
                summed = summed + jnp.dot(weights, values, preferred_element_type=F32)
            out.append(summed[:, 0:128] / summed[:, 128:256])
            lse.append(peak + jnp.log(summed[:, 128:256]))
        high = [value.astype(BF).astype(F32) for value in lse]
        low = [x - y for x, y in zip(lse, high)]
        lane = iota((count, 128), 1)
        tail = jnp.where(lane == 0, high[0], jnp.where(lane == 1, low[0], jnp.where(lane == 2, high[1], low[1])))
        return jnp.where(low_lanes, out[0], out[1]).astype(BF), tail.astype(BF)

    slots[0, :HOME, :], tails[:HOME, :] = attend(query, fresh_kv, begin_ref, end_ref, HOME, lambda: None)
    drain_gather()
    for copy in sent[0]:
        copy.wait_recv()
    swapped = to_core(slots.at[0, pl.ds(0, HOME), :], slots.at[1, pl.ds(0, HOME), :], 3)
    shared = [to_core(wo_hbm, wo.at[1], 0)]
    away_q[...] = jnp.dot(pick[...], query[HOME:, :], preferred_element_type=F32).astype(BF)
    line = iota((8 * BLK, BATCH), 0)
    unpick = ((line >> 4) * CAP + (line & 15) == iota((8 * BLK, BATCH), 1)) & ((line & 15) < CAP)
    unpick = jnp.where(unpick, 1.0, 0.0).astype(BF)
    mine_there = pl.ds(pl.multiple_of(HOME + me.d * BLK, BLK), BLK)
    tails[mine_there, :] = jnp.zeros((BLK, 128), BF)
    for which in range(2):
        slots[which, mine_there, :] = jnp.zeros((BLK, 128), BF)

    def take_kv():
        for copy in sent[1]:
            copy.wait_recv()
        away_kv[...] = jnp.dot(pick[...], fresh_kv[HOME:, :], preferred_element_type=F32).astype(BF)

    found = attend(away_q, away_kv, begin_away, end_away, 2 * BATCH, take_kv)

    def give(part, row, core, landing):
        copies = []
        for k in range(NDP - 1):
            copy = pltpu.make_async_remote_copy(
                src_ref=ret_away.at[part, pl.ds(k * BLK, BLK), :], dst_ref=landing.at[mine_there, :],
                send_sem=dp_send.at[row, k], recv_sem=dp_recv.at[row, k],
                device_id=(me.dp_peer(*FAR_FIRST[k]), core), device_id_type=MESH,
            )
            copy.start()
            copies.append(copy)
        return copies

    for part in range(2):
        for batch in range(2):
            block = jnp.dot(unpick, found[part][batch * BATCH : (batch + 1) * BATCH], preferred_element_type=F32)
            ret_away[part, batch * 128 : (batch + 1) * 128, :] = block.astype(BF)
        if part == 0:
            back = give(0, 1, me.t, slots.at[0]) + give(0, 2, me.other, slots.at[1])
        else:
            back_tails = give(1, 4, me.t, tails)

    @pl.loop(0, ROWS // PBLK)
    def _(block):
        base = pl.multiple_of(block * PBLK, PBLK)
        span = pl.ds(base, PBLK)
        position = (iota((PBLK, SLOTS), 0) + base).astype(F32)
        written = jnp.where(position == end_row[0:1, :], 1.0, 0.0)
        hit = jnp.max(written, axis=1, keepdims=True) > 0.5
        fresh = jnp.dot(written.astype(BF), fresh_kv[...], preferred_element_type=F32)
        cache[0, span, :] = jnp.where(hit, fresh[:, 0:128], cache[0, span, :].astype(F32)).astype(BF)
        cache[1, span, :] = jnp.where(hit, fresh[:, 128:256], cache[1, span, :].astype(F32)).astype(BF)

    loads[9].wait()
    for copy in back:
        copy.wait_recv()
    swapped.wait_recv()
    my_half = pl.ds(pl.multiple_of(me.c * 128, 128), 128)
    for which in range(2):
        attended[which] = jnp.dot(scat[my_half, :], slots[which], preferred_element_type=F32).astype(BF)
    shared += [to_core(gu_hbm, gu.at[1], 1), to_core(wd_hbm, wd.at[1], 2)]
    shared[0].wait_recv()

    def out_product(half):
        columns = pl.ds(half * HALF, HALF)
        value = jnp.dot(attended[0], wo[0, :, columns], preferred_element_type=F32)
        return value + jnp.dot(attended[1], wo[1, :, columns], preferred_element_type=F32)

    total, drain_first = reduce_z(
        me, out_product, own.at[0], ring_out.at[0], ring_in.at[0], rs_send.at[0], rs_recv.at[0]
    )
    resid = (tokens[...].astype(F32) + jnp.concatenate(total, axis=1)).astype(BF)
    resid_keep[...] = resid
    loads[10].wait()
    normed = scaled_norm(resid.astype(F32), gain_row(mlp_gain))
    row_of_chip = lambda zz, cc: zz * BLK
    my_rows = pl.ds(pl.multiple_of(me.z * BLK, BLK), BLK)
    for half in range(2):
        gathered_mlp[half, my_rows, :] = normed[:, half * HALF : (half + 1) * HALF]
    begin, finish_mlp, _, drain_mlp = gather_z(me, gathered_mlp, row_of_chip, ag_send.at[1], ag_recv.at[1])
    begin()
    spread_sel = sel[...].astype(F32)
    for copy in back_tails:
        copy.wait_recv()
    tail = tails[...].astype(F32)
    for head in range(2):
        lse = tail[:, 2 * head : 2 * head + 1] + tail[:, 2 * head + 1 : 2 * head + 2]
        lse_out[head : head + 1, :] = jnp.sum(spread_sel * lse, axis=0, keepdims=True)
    drain_first()
    for copy in sent[0] + sent[1] + back + back_tails:
        copy.wait_send()
    loads[11].wait()
    loads[12].wait()
    shared[1].wait_recv()
    shared[2].wait_recv()
    finish_mlp()
    for core in range(2):
        for tile in range(FFL // 256):
            columns = pl.ds(tile * 256, 256)
            both = []
            for m in range(2):
                value = jnp.dot(gathered_mlp[0], gu[core, m, :HALF, columns], preferred_element_type=F32)
                both.append(value + jnp.dot(gathered_mlp[1], gu[core, m, HALF:, columns], preferred_element_type=F32))
            inner[core, :, columns] = (both[0] / (1.0 + jnp.exp(-both[0])) * both[1]).astype(BF)

    def down_product(half):
        columns = pl.ds(half * HALF, HALF)
        value = jnp.dot(inner[0], wd[0, :, columns], preferred_element_type=F32)
        return value + jnp.dot(inner[1], wd[1, :, columns], preferred_element_type=F32)

    total, drain_last = reduce_z(
        me, down_product, own.at[1], ring_out.at[1], ring_in.at[1], rs_send.at[1], rs_recv.at[1]
    )
    hidden_out[...] = (resid_keep[...].astype(F32) + jnp.concatenate(total, axis=1)).astype(BF)
    drain_mlp()
    drain_last()
    for copy in shared:
        copy.wait_send()
    swapped.wait_send()


def store_kernel(hidden, lse, cache, hidden_out, lse_out, cache_out, sems):
    pairs = [(hidden, hidden_out), (lse, lse_out)]
    for part in range(8):
        at = (part // 4, pl.ds(part % 4 * (ROWS // 4), ROWS // 4))
        pairs.append((cache.at[at], cache_out.at[at]))
    copies = [pltpu.make_async_copy(src, dst, sems.at[i]) for i, (src, dst) in enumerate(pairs)]
    for copy in copies:
        copy.start()
    for copy in copies:
        copy.wait()


VMEM_SPEC = pl.BlockSpec(memory_space=pltpu.VMEM)
ANY_SPEC = pl.BlockSpec(memory_space=pl.ANY)
DMA = pltpu.SemaphoreType.DMA


def on_device(tokens, attn_gain, mlp_gain, project_in, project_out, gate_up, project_down, kv_cache, lengths, owners, cache_start):
    shape = jax.ShapeDtypeStruct
    results = (shape((BLK, D), BF), shape((2, REQ), F32), shape((2, ROWS, 128), BF))
    held = pl.pallas_call(
        layer_kernel,
        out_shape=(pltpu.VMEM((BLK, D), BF), pltpu.VMEM((2, REQ), F32), pltpu.VMEM((2, ROWS, 128), BF)),
        in_specs=[ANY_SPEC] * 11,
        out_specs=(VMEM_SPEC,) * 3,
        scratch_shapes=[
            pltpu.VMEM((BLK, D), BF), pltpu.VMEM((16, 128), BF), pltpu.VMEM((16, 128), BF), pltpu.VMEM((3, 32, 128), I32),
            pltpu.VMEM((D, 384), BF), pltpu.VMEM((2, 128, D), BF), pltpu.VMEM((2, 2, D, FFL), BF), pltpu.VMEM((2, FFL, D), BF),
            pltpu.VMEM((2, REQ, HALF), BF), pltpu.VMEM((2, 128, HALF), BF), pltpu.VMEM((REQ, 384), BF), pltpu.VMEM((SLOTS, 128), BF), pltpu.VMEM((SLOTS, 256), BF),
            pltpu.VMEM((NDP * BLK, 384), BF), pltpu.VMEM((SLOTS, REQ), BF), pltpu.VMEM((SLOTS, REQ), BF), pltpu.VMEM((REQ, SLOTS), BF),
            pltpu.VMEM((HOME, 128), F32), pltpu.VMEM((HOME, 128), F32), pltpu.VMEM((8, SLOTS), F32),
            pltpu.VMEM((2 * BATCH, NDP * BLK), BF), pltpu.VMEM((2 * BATCH, 128), F32), pltpu.VMEM((2 * BATCH, 128), F32),
            pltpu.VMEM((2 * BATCH, 128), BF), pltpu.VMEM((2 * BATCH, 256), BF), pltpu.VMEM((REQ, 128), F32), pltpu.VMEM((REQ, 128), F32),
            pltpu.VMEM((4 * BATCH, 128), BF), pltpu.VMEM((4 * BATCH, ROWS), F32),
            pltpu.VMEM((2, NDP * BLK, 128), BF),
            pltpu.VMEM((2, SLOTS, 128), BF), pltpu.VMEM((SLOTS, 128), BF), pltpu.VMEM((2, 128, 128), BF), pltpu.VMEM((2, 128, FFL), BF), pltpu.VMEM((BLK, D), BF),
            pltpu.VMEM((2, 2, 128, HALF), F32), pltpu.VMEM((2, 2, 7, BLK, HALF), BF), pltpu.VMEM((2, 2, 7, BLK, HALF), BF),
            DMA((5, 15)), DMA((5, 15)), DMA((2, 2, 7)), DMA((2, 2, 7)), DMA((16,)), DMA((16,)),
            DMA((2, 2, 7)), DMA((2, 2, 7)), DMA((4,)), DMA((4,)), DMA((13,)),
        ],
        compiler_params=pltpu.CompilerParams(collective_id=0, has_side_effects=True, vmem_limit_bytes=54 << 20),
        name="decode_layer",
    )(
        tokens, attn_gain.reshape(16, 128), mlp_gain.reshape(16, 128), lengths.reshape(32, 128), owners.reshape(32, 128),
        cache_start.reshape(32, 128), project_in, project_out, gate_up, project_down, kv_cache,
    )
    hidden_states, lse, kv_updated = pl.pallas_call(
        store_kernel,
        out_shape=results,
        in_specs=[VMEM_SPEC] * 3,
        out_specs=(ANY_SPEC,) * 3,
        scratch_shapes=[DMA((10,))],
        name="store_results",
    )(*(pltpu.with_memory_space_constraint(value, pltpu.VMEM) for value in held))
    return hidden_states, lse.T, kv_updated


def solution(mesh):
    placed = (
        P(("dp", "tensor"), None),
        P(),
        P(),
        P(None, None, "tensor"),
        P("tensor", None),
        P(None, None, "tensor"),
        P("tensor", None),
        P(None, "dp", "tensor"),
        P(),
        P(),
        P(),
    )
    return jax.shard_map(
        on_device,
        mesh=mesh,
        in_specs=placed,
        out_specs=(P(("dp", "tensor"), None), P("dp", "tensor"), P(None, "dp", "tensor")),
        check_vma=False,
    )
```

```python
import functools

import jax
import jax.numpy as jnp
import numpy as np
from jax import lax
from jax.experimental import pallas as pl
from jax.experimental.pallas import tpu as pltpu
from jax.sharding import PartitionSpec as P

MESH = pl.DeviceIdType.MESH
BF = jnp.bfloat16
F32 = jnp.float32
I32 = jnp.int32

EPS = 1e-05
ROPE_BASE = 130000.0
LOW = -1e30
HD = 64
NDP = 16
NTP = 16
NZ = 8
D = 2048
HALF = 1024
BLK = 16
REQ = 256
HOME = 128
SLOTS = HOME + NDP * BLK
ROWS = 4096
FFL = 512
PBLK = 2048
SPAN = 512
CAP = 9
BATCH = 80


FAR_FIRST = sorted(
    [(dx, dy) for dx in range(4) for dy in range(4) if (dx, dy) != (0, 0)],
    key=lambda at: -(min(at[0], 4 - at[0]) + min(at[1], 4 - at[1])),
)


class Place:
    def __init__(self):
        self.d = lax.axis_index("dp")
        self.t = lax.axis_index("tensor")
        self.z = self.t // 2
        self.c = self.t % 2
        self.other = self.t + 1 - 2 * self.c
        self.sib = (self.d, self.other)

    def along_z(self, offset):
        return (self.d, ((self.z + NZ + offset) % NZ) * 2 + self.c)

    def dp_peer(self, dx, dy):
        return ((self.d // 4 + dx) % 4) * 4 + (self.d % 4 + dy) % 4


def greet(me):
    barrier = pltpu.get_barrier_semaphore()
    targets = [me.along_z(k) for k in (1, -1, 2, -2)] + [me.sib]
    targets += [(me.dp_peer(dx, dy), t) for dx, dy in FAR_FIRST for t in (me.t, me.other)]
    for target in targets:
        pl.semaphore_signal(barrier, inc=1, device_id=target, device_id_type=MESH)
    return lambda: pl.semaphore_wait(barrier, len(targets))


def iota(shape, axis):
    return lax.broadcasted_iota(I32, shape, axis)


def scaled_norm(wide, gain):
    factor = lax.rsqrt(jnp.mean(wide * wide, axis=-1, keepdims=True) + EPS)
    return (wide * factor * gain).astype(BF)


def gather_z(me, buf, row_of, send, recv, sib_send=None, sib_recv=None):
    signs = (1, -1)
    started = []
    sib_copies = []
    kinds = lambda way: ((2, 0, 2), (2, 1, 2), (1, 0, 1), (1, 1, 1), (3, 0, 1), (3, 1, 1), (4, way, 2))

    def block(origin, half):
        return buf.at[half, pl.ds(pl.multiple_of(row_of(origin, me.c), BLK), BLK), :]

    def message(way, index):
        distance, half, hops = kinds(way)[index]
        ref = block((me.z + NZ - signs[way] * (distance - hops)) % NZ, half)
        return pltpu.make_async_remote_copy(
            src_ref=ref, dst_ref=ref, send_sem=send.at[way, index], recv_sem=recv.at[way, index],
            device_id=me.along_z(signs[way] * hops), device_id_type=MESH,
        )

    def start(way, index):
        copy = message(way, index)
        copy.start()
        started.append(copy)

    def sibling(origin, half):
        if sib_send is None:
            return
        index = len(sib_copies)
        ref = block(origin, half)
        copy = pltpu.make_async_remote_copy(
            src_ref=ref, dst_ref=ref, send_sem=sib_send.at[index], recv_sem=sib_recv.at[index],
            device_id=me.sib, device_id_type=MESH,
        )
        copy.start()
        sib_copies.append(copy)

    def begin():
        for index in range(4):
            for way in range(2):
                start(way, index ^ way if index < 2 else index)
        for half in range(2):
            sibling(me.z, half)

    def arrive(way, index):
        message(way, index).wait_recv()
        distance, half, _ = kinds(way)[index]
        if distance == 2:
            start(way, 4 + half)
            if half == way:
                start(way, 6)
        sibling((me.z + NZ - signs[way] * distance) % NZ, half)

    def finish():
        for index in (0, 1, 2, 3, 4, 5, 6):
            for way in range(2):
                arrive(way, index if index in (2, 3, 6) else index ^ way)
    def settle():
        for copy in sib_copies:
            copy.wait_recv()

    def drain():
        for copy in started + sib_copies:
            copy.wait_send()

    return begin, finish, settle, drain


def reduce_z(me, product, own, out, landed, send, recv):
    signs = (1, -1)
    hops = (1, 1, 2, 2, 2, 1, 1)
    started = []

    def message(way, index):
        return pltpu.make_async_remote_copy(
            src_ref=out.at[way, index], dst_ref=landed.at[way, index],
            send_sem=send.at[way, index], recv_sem=recv.at[way, index],
            device_id=me.along_z(signs[way] * hops[index]), device_id_type=MESH,
        )

    def mine(offset, half):
        target = (me.z + NZ + offset) % NZ
        return own[half, pl.ds(pl.multiple_of(target * BLK, BLK), BLK), :]

    def go(way, index, value):
        out[way, index] = value.astype(BF)
        copy = message(way, index)
        copy.start()
        started.append(copy)

    def landed_sum(way, index):
        message(way, index).wait_recv()
        return landed[way, index].astype(F32)

    for half in range(2):
        own[half] = product(half)
        go(half, 2, mine(4 * signs[half], half))
        for way in (1 - half, half):
            go(way, half, mine(3 * signs[way], half))
    for half in range(2):
        for way in range(2):
            go(way, 5 + half, mine(signs[way], half))
    total = [mine(0, half) for half in range(2)]
    for half in range(2):
        for way in (1 - half, half):
            value = landed_sum(way, half) + mine(2 * signs[way], half)
            if half == way:
                value = value + landed_sum(way, 2)
            go(way, 3 + half, value)
    for base in (5, 3):
        for half in range(2):
            for way in range(2):
                total[half] = total[half] + landed_sum(way, base + half)
    return total, lambda: [copy.wait_send() for copy in started]


def exchange_dp(me, source, landing, send, recv):
    copies = []
    for i, (dx, dy) in enumerate(FAR_FIRST):
        peer = me.dp_peer(dx, dy)
        copy = pltpu.make_async_remote_copy(
            src_ref=source.at[pl.ds(pl.multiple_of(peer * BLK, BLK), BLK), :],
            dst_ref=landing.at[pl.ds(pl.multiple_of(me.d * BLK, BLK), BLK), :],
            send_sem=send.at[i], recv_sem=recv.at[i],
            device_id=(peer, me.t), device_id_type=MESH,
        )
        copy.start()
        copies.append(copy)
    here = pl.ds(pl.multiple_of(me.d * BLK, BLK), BLK)
    landing[here, :] = source[here, :]
    return copies


def column_of(row, hits):
    return jnp.sum(jnp.where(hits, row, 0.0), axis=1, keepdims=True)


def layer_kernel(
    tokens_hbm, attn_gain_hbm, mlp_gain_hbm, lengths_hbm, owners_hbm, starts_hbm, w_hbm, wo_hbm, gu_hbm, wd_hbm, cache_hbm,
    hidden_out, lse_out, cache,
    tokens, attn_gain, mlp_gain, ints, w, wo, gu, wd,
    gathered, gathered_mlp, packed, query, fresh_kv, outgoing, sel, route, scat, begin_ref, end_ref, end_row,
    pick, begin_away, end_away, away_q, away_kv, cos_ref, sin_ref,
    q2, score_ref, ret_away, slots, tails, attended, inner, resid_keep,
    own, ring_out, ring_in,
    dp_send, dp_recv, ag_send, ag_recv, ag_sib_send, ag_sib_recv, rs_send, rs_recv, core_send, core_recv, load_sem,
):
    me = Place()
    pairs = [
        (tokens_hbm, tokens), (attn_gain_hbm, attn_gain), (owners_hbm, ints.at[0]), (lengths_hbm, ints.at[1]),
        (starts_hbm, ints.at[2]), (w_hbm.at[0], w.at[:, pl.ds(0, 128)]), (w_hbm.at[1], w.at[:, pl.ds(128, 128)]),
        (w_hbm.at[2], w.at[:, pl.ds(256, 128)]), (cache_hbm, cache), (wo_hbm, wo.at[0]), (mlp_gain_hbm, mlp_gain), (gu_hbm, gu.at[0]), (wd_hbm, wd.at[0]),
    ]
    loads = [pltpu.make_async_copy(src, dst, load_sem.at[i]) for i, (src, dst) in enumerate(pairs)]
    for copy in loads[:2]:
        copy.start()
    wait_all = greet(me)
    for copy in loads[2:]:
        copy.start()
    loads[0].wait()
    loads[1].wait()

    def gain_row(ref):
        return jnp.concatenate([ref[i : i + 1, :].astype(F32) for i in range(16)], axis=1)

    normed = scaled_norm(tokens[...].astype(F32), gain_row(attn_gain))
    row_of = lambda zz, cc: cc * 128 + zz * BLK
    my_rows = pl.ds(pl.multiple_of(row_of(me.z, me.c), BLK), BLK)
    for half in range(2):
        gathered[half, my_rows, :] = normed[:, half * HALF : (half + 1) * HALF]
    wait_all()
    begin, finish, settle, drain_gather = gather_z(
        me, gathered, row_of, ag_send.at[0], ag_recv.at[0], ag_sib_send, ag_sib_recv
    )
    begin()

    for copy in loads[2:5]:
        copy.wait()

    def wide(m):
        return jnp.concatenate([ints[m, pl.ds(0, NDP, stride=2), :], ints[m, pl.ds(1, NDP, stride=2), :]], axis=1)

    def mine(m):
        return jnp.concatenate([ints[m, pl.ds(2 * me.d, 1), :], ints[m, pl.ds(2 * me.d + 1, 1), :]], axis=1)

    own_all, len_all, start_all = wide(0), wide(1), wide(2)
    own_row, len_row, start_row = mine(0), mine(1).astype(F32), mine(2).astype(F32)
    before = jnp.where(iota((REQ, REQ), 0) < iota((REQ, REQ), 1), 1.0, 0.0).astype(BF)
    here = own_all == me.d
    here_rank = jnp.dot(jnp.where(here, 1.0, 0.0).astype(BF), before, preferred_element_type=F32)
    away = here & (iota((NDP, REQ), 0) != me.d)
    place_in = jnp.where(away, here_rank, -1.0)
    onehot = jnp.where(iota((NDP, REQ), 0) == own_row, 1.0, 0.0)
    counts = jnp.dot(onehot.astype(BF), before, preferred_element_type=F32)
    rank = jnp.sum(onehot * counts, axis=0, keepdims=True)
    own_wide = own_row.astype(F32)
    place = jnp.where(own_row == me.d, rank, HOME + own_wide * BLK + rank)
    chosen = iota((SLOTS, REQ), 0).astype(F32) == place
    sel[...] = jnp.where(chosen, 1.0, 0.0).astype(BF)
    request = iota((REQ, REQ), 0)
    natural = ((request >> 4) & 7) * 32 + (request >> 7) * 16 + (request & 15)
    reorder = natural == iota((REQ, REQ), 1)
    place_col = column_of(place, reorder)
    place_row = jnp.sum(jnp.where(request == iota((REQ, REQ), 1), place_col, 0.0), axis=0, keepdims=True)
    route[...] = jnp.where(iota((SLOTS, REQ), 0).astype(F32) == place_row, 1.0, 0.0).astype(BF)
    scat[...] = jnp.where(iota((REQ, SLOTS), 1).astype(F32) == place_col, 1.0, 0.0).astype(BF)

    def spread(rows16):
        return jnp.concatenate(
            [jnp.broadcast_to(rows16[b : b + 1, :], (BLK, REQ)) for b in range(NDP)], axis=0
        )

    slot = (iota((NDP * BLK, REQ), 0) & (BLK - 1)).astype(F32)
    hits_in = spread(place_in) == slot
    begin_all = start_all.astype(F32)
    finish_all = begin_all + len_all.astype(F32)
    hits_home = chosen[:HOME]
    begin_col = jnp.concatenate(
        [column_of(start_row + 1.0, hits_home), column_of(spread(begin_all) + 1.0, hits_in)], axis=0
    ) - 1.0
    finish_col = jnp.concatenate(
        [column_of(start_row + len_row + 1.0, hits_home), column_of(spread(finish_all) + 1.0, hits_in)], axis=0
    ) - 1.0
    begin_ref[...] = jnp.broadcast_to(begin_col[:HOME], (HOME, 128))
    end_ref[...] = jnp.broadcast_to(finish_col[:HOME], (HOME, 128))
    eye = iota((SLOTS, SLOTS), 0) == iota((SLOTS, SLOTS), 1)
    finish_row = jnp.sum(jnp.where(eye, finish_col, 0.0), axis=0, keepdims=True)
    begin_row = jnp.sum(jnp.where(eye, begin_col, 0.0), axis=0, keepdims=True)
    end_row[...] = jnp.broadcast_to(finish_row, (8, SLOTS))
    index = iota((2 * BATCH, 1), 0).astype(F32)
    second = index >= BATCH
    within = jnp.where(second, index - BATCH, index)
    nth = jnp.floor((within + 0.5) * (1.0 / CAP))
    source = jnp.full((2 * BATCH, 1), -1000.0, F32)
    for k, (dx, dy) in enumerate(FAR_FIRST):
        at = (nth == k % 8) & (second if k >= 8 else jnp.logical_not(second))
        source = jnp.where(at, (me.dp_peer(dx, dy) * BLK).astype(F32), source)
    source = source + within - nth * CAP
    picked = iota((2 * BATCH, NDP * BLK), 1).astype(F32) == source
    pick[...] = jnp.where(picked, 1.0, 0.0).astype(BF)
    begin_away[...] = jnp.broadcast_to(column_of(begin_row[:, HOME:] + 1.0, picked) - 1.0, (2 * BATCH, 128))
    end_away[...] = jnp.broadcast_to(column_of(finish_row[:, HOME:] + 1.0, picked) - 1.0, (2 * BATCH, 128))

    len_col = column_of(len_row, reorder)
    lane = iota((1, 128), 1) & (HD // 2 - 1)
    freqs = jnp.exp(lane.astype(F32) * np.float32(-np.log(ROPE_BASE) / (HD // 2)))
    angle = len_col * freqs
    turns = jnp.floor(angle * (1.0 / (2.0 * np.pi)) + 0.5)
    left = (angle - turns * 6.28125) - turns * np.float32(2.0 * np.pi - 6.28125)
    x = 0.5 * left
    x2 = x * x
    sin_half = x * (1.0 + x2 * (-1 / 6 + x2 * (1 / 120 + x2 * (-1 / 5040 + x2 * (1 / 362880 - x2 / 39916800)))))
    cos_half = 1.0 + x2 * (
        -1 / 2 + x2 * (1 / 24 + x2 * (-1 / 720 + x2 * (1 / 40320 + x2 * (-1 / 3628800 + x2 / 479001600))))
    )
    sine = 2.0 * sin_half * cos_half
    cos_ref[...] = 1.0 - 2.0 * sin_half * sin_half
    sin_ref[...] = jnp.where((iota((REQ, 128), 1) & (HD - 1)) < HD // 2, -sine, sine)

    finish()

    def to_core(src, dst, index):
        copy = pltpu.make_async_remote_copy(
            src_ref=src, dst_ref=dst, send_sem=core_send.at[index], recv_sem=core_recv.at[index],
            device_id=me.sib, device_id_type=MESH,
        )
        copy.start()
        return copy

    for copy in loads[5:8]:
        copy.wait()
    low_half = (iota((128, 128), 1) & (HD - 1)) < HD // 2

    def project(core):
        rows = pl.ds(pl.multiple_of(core * 128, 128), 128)
        projected = jnp.dot(gathered[0, rows, :], w[:HALF], preferred_element_type=F32)
        projected = projected + jnp.dot(gathered[1, rows, :], w[HALF:], preferred_element_type=F32)
        for m in range(2):
            values = projected[:, m * 128 : (m + 1) * 128]
            partner = jnp.where(low_half, pltpu.roll(values, 96, 1), pltpu.roll(values, 32, 1))
            packed[rows, m * 128 : (m + 1) * 128] = (values * cos_ref[rows, :] + partner * sin_ref[rows, :]).astype(BF)
        packed[rows, 256:384] = projected[:, 256:384].astype(BF)

    project(me.c)
    settle()
    project(1 - me.c)
    sent = []
    for lanes, landing, row in ((pl.ds(0, 128), query, 0), (pl.ds(128, 256), fresh_kv, 3)):
        outgoing[:, lanes] = jnp.dot(route[HOME:, :], packed[:, lanes], preferred_element_type=F32).astype(BF)
        there = landing.at[pl.ds(HOME, NDP * BLK), :]
        sent.append(exchange_dp(me, outgoing.at[:, lanes], there, dp_send.at[row], dp_recv.at[row]))
    home = jnp.dot(route[:HOME, :], packed[...], preferred_element_type=F32).astype(BF)
    query[:HOME, :] = home[:, 0:128]
    fresh_kv[:HOME, :] = home[:, 128:384]
    loads[8].wait()

    def attend(queries, pair, begins, ends, count, ready):
        low_lanes = iota((count, 128), 1) < HD
        q = queries[:count, :].astype(F32) * (1.0 / 8.0)
        spans = [pl.ds(head * count, count) for head in range(2)]
        chunks = [pl.ds(first, SPAN) for first in range(0, ROWS, SPAN)]
        top = []
        for head in range(2):
            qh = jnp.where(low_lanes if head == 0 else jnp.logical_not(low_lanes), q, 0.0)
            q2[spans[head], :] = qh.astype(BF)
            top.append(jnp.full((count, 128), LOW, F32))
        for chunk in chunks:
            across = (iota((1, SPAN), 1) + chunk.start).astype(F32)
            live = (across >= begins[:count, 0:1]) & (across < ends[:count, 0:1])
            for head in range(2):
                scores = lax.dot_general(
                    q2[spans[head], :], cache[0, chunk, :], (((1,), (1,)), ((), ())), preferred_element_type=F32
                )
                scores = jnp.where(live, scores, LOW)
                score_ref[spans[head], chunk] = scores
                for first in range(0, SPAN, 128):
                    top[head] = jnp.maximum(top[head], scores[:, first : first + 128])
        ready()
        k = pair[:count, 0:128].astype(F32)
        v = pair[:count, 128:256].astype(F32)
        out, lse = [], []
        for head in range(2):
            own_score = jnp.sum(q2[spans[head], :].astype(F32) * k, axis=1, keepdims=True)
            peak = jnp.maximum(own_score, jnp.max(top[head], axis=1, keepdims=True))
            own_weight = jnp.exp(own_score - peak)
            summed = jnp.concatenate([own_weight * v, jnp.broadcast_to(own_weight, (count, 128))], axis=1)
            for chunk in chunks:
                weights = jnp.exp(score_ref[spans[head], chunk] - peak).astype(BF)
                values = jnp.concatenate([cache[1, chunk, :], jnp.ones((SPAN, 128), BF)], axis=1)
                summed = summed + jnp.dot(weights, values, preferred_element_type=F32)
            out.append(summed[:, 0:128] / summed[:, 128:256])
            lse.append(peak + jnp.log(summed[:, 128:256]))
        high = [value.astype(BF).astype(F32) for value in lse]
        low = [x - y for x, y in zip(lse, high)]
        lane = iota((count, 128), 1)
        tail = jnp.where(lane == 0, high[0], jnp.where(lane == 1, low[0], jnp.where(lane == 2, high[1], low[1])))
        return jnp.where(low_lanes, out[0], out[1]).astype(BF), tail.astype(BF)

    slots[0, :HOME, :], tails[:HOME, :] = attend(query, fresh_kv, begin_ref, end_ref, HOME, lambda: None)
    drain_gather()
    for copy in sent[0]:
        copy.wait_recv()
    swapped = to_core(slots.at[0, pl.ds(0, HOME), :], slots.at[1, pl.ds(0, HOME), :], 3)
    shared = [to_core(wo_hbm, wo.at[1], 0)]
    away_q[...] = jnp.dot(pick[...], query[HOME:, :], preferred_element_type=F32).astype(BF)
    line = iota((8 * BLK, BATCH), 0)
    unpick = ((line >> 4) * CAP + (line & 15) == iota((8 * BLK, BATCH), 1)) & ((line & 15) < CAP)
    unpick = jnp.where(unpick, 1.0, 0.0).astype(BF)
    mine_there = pl.ds(pl.multiple_of(HOME + me.d * BLK, BLK), BLK)
    tails[mine_there, :] = jnp.zeros((BLK, 128), BF)
    for which in range(2):
        slots[which, mine_there, :] = jnp.zeros((BLK, 128), BF)

    def take_kv():
        for copy in sent[1]:
            copy.wait_recv()
        away_kv[...] = jnp.dot(pick[...], fresh_kv[HOME:, :], preferred_element_type=F32).astype(BF)

    found = attend(away_q, away_kv, begin_away, end_away, 2 * BATCH, take_kv)

    def give(part, row, core, landing):
        copies = []
        for k in range(NDP - 1):
            copy = pltpu.make_async_remote_copy(
                src_ref=ret_away.at[part, pl.ds(k * BLK, BLK), :], dst_ref=landing.at[mine_there, :],
                send_sem=dp_send.at[row, k], recv_sem=dp_recv.at[row, k],
                device_id=(me.dp_peer(*FAR_FIRST[k]), core), device_id_type=MESH,
            )
            copy.start()
            copies.append(copy)
        return copies

    for part in range(2):
        for batch in range(2):
            block = jnp.dot(unpick, found[part][batch * BATCH : (batch + 1) * BATCH], preferred_element_type=F32)
            ret_away[part, batch * 128 : (batch + 1) * 128, :] = block.astype(BF)
        if part == 0:
            back = give(0, 1, me.t, slots.at[0]) + give(0, 2, me.other, slots.at[1])
        else:
            back_tails = give(1, 4, me.t, tails)

    @pl.loop(0, ROWS // PBLK)
    def _(block):
        base = pl.multiple_of(block * PBLK, PBLK)
        span = pl.ds(base, PBLK)
        position = (iota((PBLK, SLOTS), 0) + base).astype(F32)
        written = jnp.where(position == end_row[0:1, :], 1.0, 0.0)
        hit = jnp.max(written, axis=1, keepdims=True) > 0.5
        fresh = jnp.dot(written.astype(BF), fresh_kv[...], preferred_element_type=F32)
        cache[0, span, :] = jnp.where(hit, fresh[:, 0:128], cache[0, span, :].astype(F32)).astype(BF)
        cache[1, span, :] = jnp.where(hit, fresh[:, 128:256], cache[1, span, :].astype(F32)).astype(BF)

    loads[9].wait()
    for copy in back:
        copy.wait_recv()
    swapped.wait_recv()
    my_half = pl.ds(pl.multiple_of(me.c * 128, 128), 128)
    for which in range(2):
        attended[which] = jnp.dot(scat[my_half, :], slots[which], preferred_element_type=F32).astype(BF)
    shared += [to_core(gu_hbm, gu.at[1], 1), to_core(wd_hbm, wd.at[1], 2)]
    shared[0].wait_recv()

    def out_product(half):
        columns = pl.ds(half * HALF, HALF)
        value = jnp.dot(attended[0], wo[0, :, columns], preferred_element_type=F32)
        return value + jnp.dot(attended[1], wo[1, :, columns], preferred_element_type=F32)

    total, drain_first = reduce_z(
        me, out_product, own.at[0], ring_out.at[0], ring_in.at[0], rs_send.at[0], rs_recv.at[0]
    )
    resid = (tokens[...].astype(F32) + jnp.concatenate(total, axis=1)).astype(BF)
    resid_keep[...] = resid
    loads[10].wait()
    normed = scaled_norm(resid.astype(F32), gain_row(mlp_gain))
    row_of_chip = lambda zz, cc: zz * BLK
    my_rows = pl.ds(pl.multiple_of(me.z * BLK, BLK), BLK)
    for half in range(2):
        gathered_mlp[half, my_rows, :] = normed[:, half * HALF : (half + 1) * HALF]
    begin, finish_mlp, _, drain_mlp = gather_z(me, gathered_mlp, row_of_chip, ag_send.at[1], ag_recv.at[1])
    begin()
    spread_sel = sel[...].astype(F32)
    for copy in back_tails:
        copy.wait_recv()
    tail = tails[...].astype(F32)
    for head in range(2):
        lse = tail[:, 2 * head : 2 * head + 1] + tail[:, 2 * head + 1 : 2 * head + 2]
        lse_out[head : head + 1, :] = jnp.sum(spread_sel * lse, axis=0, keepdims=True)
    drain_first()
    for copy in sent[0] + sent[1] + back + back_tails:
        copy.wait_send()
    finish_mlp()
    loads[11].wait()
    loads[12].wait()
    shared[1].wait_recv()
    shared[2].wait_recv()
    for core in range(2):
        for tile in range(FFL // 256):
            columns = pl.ds(tile * 256, 256)
            both = []
            for m in range(2):
                value = jnp.dot(gathered_mlp[0], gu[core, m, :HALF, columns], preferred_element_type=F32)
                both.append(value + jnp.dot(gathered_mlp[1], gu[core, m, HALF:, columns], preferred_element_type=F32))
            inner[core, :, columns] = (both[0] / (1.0 + jnp.exp(-both[0])) * both[1]).astype(BF)

    def down_product(half):
        columns = pl.ds(half * HALF, HALF)
        value = jnp.dot(inner[0], wd[0, :, columns], preferred_element_type=F32)
        return value + jnp.dot(inner[1], wd[1, :, columns], preferred_element_type=F32)

    total, drain_last = reduce_z(
        me, down_product, own.at[1], ring_out.at[1], ring_in.at[1], rs_send.at[1], rs_recv.at[1]
    )
    hidden_out[...] = (resid_keep[...].astype(F32) + jnp.concatenate(total, axis=1)).astype(BF)
    drain_mlp()
    drain_last()
    for copy in shared:
        copy.wait_send()
    swapped.wait_send()


def store_kernel(hidden, lse, cache, hidden_out, lse_out, cache_out, sems):
    pairs = [(hidden, hidden_out), (lse, lse_out)]
    for part in range(8):
        at = (part // 4, pl.ds(part % 4 * (ROWS // 4), ROWS // 4))
        pairs.append((cache.at[at], cache_out.at[at]))
    copies = [pltpu.make_async_copy(src, dst, sems.at[i]) for i, (src, dst) in enumerate(pairs)]
    for copy in copies:
        copy.start()
    for copy in copies:
        copy.wait()


VMEM_SPEC = pl.BlockSpec(memory_space=pltpu.VMEM)
ANY_SPEC = pl.BlockSpec(memory_space=pl.ANY)
DMA = pltpu.SemaphoreType.DMA


def on_device(tokens, attn_gain, mlp_gain, project_in, project_out, gate_up, project_down, kv_cache, lengths, owners, cache_start):
    shape = jax.ShapeDtypeStruct
    results = (shape((BLK, D), BF), shape((2, REQ), F32), shape((2, ROWS, 128), BF))
    held = pl.pallas_call(
        layer_kernel,
        out_shape=(pltpu.VMEM((BLK, D), BF), pltpu.VMEM((2, REQ), F32), pltpu.VMEM((2, ROWS, 128), BF)),
        in_specs=[ANY_SPEC] * 11,
        out_specs=(VMEM_SPEC,) * 3,
        scratch_shapes=[
            pltpu.VMEM((BLK, D), BF), pltpu.VMEM((16, 128), BF), pltpu.VMEM((16, 128), BF), pltpu.VMEM((3, 32, 128), I32),
            pltpu.VMEM((D, 384), BF), pltpu.VMEM((2, 128, D), BF), pltpu.VMEM((2, 2, D, FFL), BF), pltpu.VMEM((2, FFL, D), BF),
            pltpu.VMEM((2, REQ, HALF), BF), pltpu.VMEM((2, 128, HALF), BF), pltpu.VMEM((REQ, 384), BF), pltpu.VMEM((SLOTS, 128), BF), pltpu.VMEM((SLOTS, 256), BF),
            pltpu.VMEM((NDP * BLK, 384), BF), pltpu.VMEM((SLOTS, REQ), BF), pltpu.VMEM((SLOTS, REQ), BF), pltpu.VMEM((REQ, SLOTS), BF),
            pltpu.VMEM((HOME, 128), F32), pltpu.VMEM((HOME, 128), F32), pltpu.VMEM((8, SLOTS), F32),
            pltpu.VMEM((2 * BATCH, NDP * BLK), BF), pltpu.VMEM((2 * BATCH, 128), F32), pltpu.VMEM((2 * BATCH, 128), F32),
            pltpu.VMEM((2 * BATCH, 128), BF), pltpu.VMEM((2 * BATCH, 256), BF), pltpu.VMEM((REQ, 128), F32), pltpu.VMEM((REQ, 128), F32),
            pltpu.VMEM((4 * BATCH, 128), BF), pltpu.VMEM((4 * BATCH, ROWS), F32),
            pltpu.VMEM((2, NDP * BLK, 128), BF),
            pltpu.VMEM((2, SLOTS, 128), BF), pltpu.VMEM((SLOTS, 128), BF), pltpu.VMEM((2, 128, 128), BF), pltpu.VMEM((2, 128, FFL), BF), pltpu.VMEM((BLK, D), BF),
            pltpu.VMEM((2, 2, 128, HALF), F32), pltpu.VMEM((2, 2, 7, BLK, HALF), BF), pltpu.VMEM((2, 2, 7, BLK, HALF), BF),
            DMA((5, 15)), DMA((5, 15)), DMA((2, 2, 7)), DMA((2, 2, 7)), DMA((16,)), DMA((16,)),
            DMA((2, 2, 7)), DMA((2, 2, 7)), DMA((4,)), DMA((4,)), DMA((13,)),
        ],
        compiler_params=pltpu.CompilerParams(collective_id=0, has_side_effects=True, vmem_limit_bytes=54 << 20),
        name="decode_layer",
    )(
        tokens, attn_gain.reshape(16, 128), mlp_gain.reshape(16, 128), lengths.reshape(32, 128), owners.reshape(32, 128),
        cache_start.reshape(32, 128), project_in, project_out, gate_up, project_down, kv_cache,
    )
    hidden_states, lse, kv_updated = pl.pallas_call(
        store_kernel,
        out_shape=results,
        in_specs=[VMEM_SPEC] * 3,
        out_specs=(ANY_SPEC,) * 3,
        scratch_shapes=[DMA((10,))],
        name="store_results",
    )(*(pltpu.with_memory_space_constraint(value, pltpu.VMEM) for value in held))
    return hidden_states, lse.T, kv_updated


def solution(mesh):
    placed = (
        P(("dp", "tensor"), None),
        P(),
        P(),
        P(None, None, "tensor"),
        P("tensor", None),
        P(None, None, "tensor"),
        P("tensor", None),
        P(None, "dp", "tensor"),
        P(),
        P(),
        P(),
    )
    return jax.shard_map(
        on_device,
        mesh=mesh,
        in_specs=placed,
        out_specs=(P(("dp", "tensor"), None), P("dp", "tensor"), P(None, "dp", "tensor")),
        check_vma=False,
    )
```
